32 devices in a mesh: groups: 2 (over y), latent: 8 (over z, x), hidden: 2 (over core).
Axes of the slice: x: 2, y: 2, z: 4, core: 2. Of those that a mesh axis runs over, the one named last changes fastest.
Arguments:
- input_codes: int32 [288, 2304], P('groups', ('latent', 'hidden')), parts along dimension 0, may hold values from -128 to 127
- cotangent_codes: int32 [288, 2304], P('groups', ('latent', 'hidden')), parts along dimension 0, may hold values from -128 to 127
- dictionary: bfloat16 [8192, 2304], P(('latent', 'hidden')), as said below
- encoder_bias: float32 [8192], P(('latent', 'hidden')), may hold values from -12 to 0, as said below
- decoder_bias: float32 [2304], replicated, may hold values from -1.2 to 1.2
- norm_gain: float32 [2304], replicated, may hold values from 0.1 to 1.9
- gate_weight: bfloat16 [8192, 2304], P(('latent', 'hidden')), may hold values from -0.1875 to 0.1875
- up_weight: bfloat16 [8192, 2304], P(('latent', 'hidden')), may hold values from -0.1875 to 0.1875
- down_weight: bfloat16 [8192, 2304], P(('latent', 'hidden')), may hold values from -0.09375 to 0.09375
Outputs:
- block_output: bfloat16 [288, 2304], P('groups', ('latent', 'hidden')), parts along dimension 0
- dictionary_grad: bfloat16 [8192, 4608], P(('latent', 'hidden'), 'groups'), parts along dimension 1
The draws below stay inside these ranges and needn't reach their ends.
There are 2 independent parts, one for each index of `groups`. The reference program is written for one: setup_inputs(seed, part) draws one part's arguments, and reference() takes and returns one part's arrays. A program takes and returns all parts, laid end to end along the dimension named above; an argument that names none is the same for every part. Nothing has to cross between parts.
Inputs may be any that keep to these rules, and one draw needn't show every extreme that they name: `dictionary`: every entry is a whole multiple of 2^-10, at most 119 such units in magnitude. `encoder_bias`: every entry is a whole multiple of 2^-16.
All inputs are finite; a program needn't handle non-finite values.
Results may differ from the reference program's by a relative error of at most 0.0072.
Values may be sent and summed in bfloat16 or wider, within the bound.
A program may use at most 64 MiB of HBM per device.

```python
import math
import jax
import jax.numpy as jnp
from jax import lax

D = 2304
FF = 8192
LAT = 8192
B = 144


INPUT_SPREAD = 1.1547


def upper_tail(point):
    factor = 1.0 / (1.0 + 0.3275911 * point / math.sqrt(2.0))
    series = factor * (0.254829592 + factor * (-0.284496736 + factor * (1.421413741 + factor * (-1.453152027 + factor * 1.061405429))))
    return 0.5 * series * math.exp(-0.5 * point * point)


def normal_quantile(upper_share):
    lower_end = 0.0
    upper_end = 10.0
    for counter in range(80):
        middle = 0.5 * (lower_end + upper_end)
        if upper_tail(middle) > upper_share:
            lower_end = middle
        else:
            upper_end = middle
    return 0.5 * (lower_end + upper_end)


def row_limits():
    position = jnp.arange(LAT, dtype=jnp.int32)
    return 16 + position * 48 // LAT


def draw_dictionary(key, part):
    limits = row_limits()[:, None]
    integer_codes = jax.random.randint(key, (LAT, D), -limits, limits + 1)
    return (integer_codes.astype(jnp.float32) * 2.0 ** (-10)).astype(jnp.bfloat16)


def draw_encoder_bias(key, part):
    active_share = min(0.25, 400.0 / LAT)
    limits = row_limits().astype(jnp.float32)
    spread = INPUT_SPREAD * jnp.sqrt(limits * (limits + 1.0) / 3.0) * 2.0 ** (-10)
    depth = normal_quantile(active_share) * math.sqrt(D) * spread
    center_units = jnp.floor(depth * 65536.0)
    jitter_codes = jax.random.randint(key, (LAT,), -512, 513)
    jitter_units = jnp.floor(jitter_codes.astype(jnp.float32) * (center_units * 0.15 / 512.0))
    return (jitter_units - center_units) * 2.0 ** (-16)


def plant(drawn, rng, low, largest):
    longest = drawn.shape.index(max(drawn.shape))
    spots = []
    for shift in (0, 1):
        where = [jax.random.randint(jax.random.fold_in(rng, axis), (), 0, length) for axis, length in enumerate(drawn.shape)]
        where[longest] = (where[longest] + shift) % drawn.shape[longest]
        spots.append(tuple(where))
    return drawn.at[spots[0]].set(low).at[spots[1]].set(largest)


def spiked(values, key, source, target, shards_of, factor):
    owner, partner = [(jnp.arange(values.shape[dim]) // (values.shape[dim] // shards_of)).reshape([-1 if axis == dim else 1 for axis in range(values.ndim)]) for dim in (source, target)]
    chosen = jax.random.permutation(key, shards_of)[partner]
    strong = (owner == chosen) | (owner == (partner + shards_of // 2) % shards_of)
    return jnp.where(strong, factor * values, values)


def shard_levels(stream_key, extent, cuts, least, top_value):
    def one(axis_at, shards_of):
        steps = jax.random.uniform(jax.random.fold_in(jax.random.fold_in(stream_key, 6), axis_at), (shards_of,), jnp.float32, least / len(cuts), top_value / len(cuts))
        return jnp.repeat(jnp.exp(steps), extent[axis_at] // shards_of).reshape((-1,) + (1,) * (len(extent) - axis_at - 1))

    factor_of = one(*cuts[0])
    for cut in cuts[1:]:
        factor_of = factor_of * one(*cut)
    return factor_of


def bell_draw(stream_key, dims, width, most, shards=(), held_as=jnp.bfloat16):
    entries = jax.random.normal(stream_key, dims, jnp.float32) * width
    if len(shards) > 0:
        entries = shard_levels(stream_key, dims, shards, -0.22, 0.18) * entries
    return jnp.clip(entries, min=-most, max=most).astype(held_as)


def noise_with(stream_key, extent, width, reach, shards, heavy, held_as=jnp.bfloat16):
    entries = width * jax.random.normal(stream_key, extent, jnp.float32)
    if shards:
        entries = entries * shard_levels(stream_key, extent, shards, -0.22, 0.18)
    return jnp.clip(spiked(entries, jax.random.fold_in(stream_key, 3), *heavy), -reach, reach).astype(held_as)


def setup_inputs(seed: int = 0, part: int = 0) -> dict:
    splits = jax.random.split(jax.random.key(seed), 10)
    part_keys = jax.random.split(jax.random.fold_in(splits[9], part), 10)
    return {
        "input_codes": plant(jax.random.randint(part_keys[0], (B, D), -128, 128), jax.random.fold_in(part_keys[0], 1), -128, 127).astype(jnp.int32),
        "cotangent_codes": plant(jax.random.randint(part_keys[1], (B, D), -128, 128), jax.random.fold_in(part_keys[1], 1), -128, 127).astype(jnp.int32),
        "dictionary": draw_dictionary(jax.random.fold_in(splits[9], 71), part),
        "encoder_bias": draw_encoder_bias(jax.random.fold_in(splits[9], 71), part),
        "decoder_bias": bell_draw(splits[4], (D,), 0.2, 1.2, (), jnp.float32),
        "norm_gain": jnp.clip(1.0 + 0.18 * jax.random.normal(splits[5], (D,), jnp.float32), 0.1, 1.9),
        "gate_weight": noise_with(splits[6], (FF, D), D ** -0.5, 0.1875, ((0, 16),), (0, 1, 16, 2.0)),
        "up_weight": noise_with(splits[7], (FF, D), D ** -0.5, 0.1875, ((0, 16),), (0, 1, 16, 2.0)),
        "down_weight": noise_with(splits[8], (FF, D), FF ** -0.5, 0.09375, ((0, 16),), (0, 1, 16, 2.0)),
    }


CODE_STEP = 2.0 ** (-6)
NORM_EPSILON = 1e-06
GELU_ROOT = 0.7978845608028654
GELU_CUBIC = 0.044715
ACROSS = (((1,), (1,)), ((), ()))
DOWNWARD = (((0,), (0,)), ((), ()))

def gelu_parts(values):
    argument = GELU_ROOT * (values + GELU_CUBIC * values * values * values)
    tanh_value = jnp.tanh(argument)
    result = 0.5 * values * (1.0 + tanh_value)
    derivative = 0.5 * (1.0 + tanh_value) + 0.5 * values * (1.0 - tanh_value * tanh_value) * GELU_ROOT * (1.0 + 3.0 * GELU_CUBIC * values * values)
    return (result, derivative)

def reference(input_codes, cotangent_codes, dictionary, encoder_bias, decoder_bias, norm_gain, gate_weight, up_weight, down_weight):
    inputs = (input_codes.astype(jnp.float32) * CODE_STEP).astype(jnp.bfloat16)
    preact = lax.dot_general(inputs, dictionary, ACROSS, preferred_element_type=jnp.float32) + encoder_bias
    latents = jnp.maximum(preact, 0.0).astype(jnp.bfloat16)
    rebuilt = jnp.dot(latents, dictionary, preferred_element_type=jnp.float32) + decoder_bias
    inverse = lax.rsqrt(lax.optimization_barrier(jnp.sum(rebuilt * rebuilt, axis=1, keepdims=True)) / D + NORM_EPSILON)
    normed = (rebuilt * inverse * norm_gain).astype(jnp.bfloat16)
    gate_proj = lax.dot_general(normed, gate_weight, ACROSS, preferred_element_type=jnp.float32)
    up_proj = lax.dot_general(normed, up_weight, ACROSS, preferred_element_type=jnp.float32)
    gelu_value, gelu_slope = gelu_parts(gate_proj)
    hidden = (gelu_value * up_proj).astype(jnp.bfloat16)
    block_output = jnp.dot(hidden, down_weight, preferred_element_type=jnp.float32).astype(jnp.bfloat16)
    upstream = (cotangent_codes.astype(jnp.float32) * CODE_STEP).astype(jnp.bfloat16)
    hidden_grad = lax.dot_general(upstream, down_weight, ACROSS, preferred_element_type=jnp.float32)
    gate_grad = (hidden_grad * up_proj * gelu_slope).astype(jnp.bfloat16)
    up_grad = (hidden_grad * gelu_value).astype(jnp.bfloat16)
    normed_grad = jnp.dot(gate_grad, gate_weight, preferred_element_type=jnp.float32) + jnp.dot(up_grad, up_weight, preferred_element_type=jnp.float32)
    scaled = normed_grad * norm_gain
    inner_row = lax.optimization_barrier(jnp.sum(scaled * rebuilt, axis=1, keepdims=True))
    inverse_cube = inverse * inverse * inverse
    rebuilt_grad = (inverse * scaled - inverse_cube * rebuilt * (inner_row / D) + (rebuilt - inputs.astype(jnp.float32))).astype(jnp.bfloat16)
    latent_grad = lax.dot_general(rebuilt_grad, dictionary, ACROSS, preferred_element_type=jnp.float32)
    preact_grad = jnp.where(preact > 0.0, latent_grad, 0.0).astype(jnp.bfloat16)
    dictionary_grad = lax.dot_general(latents, rebuilt_grad, DOWNWARD, preferred_element_type=jnp.float32) + lax.dot_general(preact_grad, inputs, DOWNWARD, preferred_element_type=jnp.float32)
    return (block_output, dictionary_grad.astype(jnp.bfloat16))
```

```python
import types

import jax
import jax.numpy as jnp
from jax import lax
from jax.experimental import pallas as pl
from jax.experimental.pallas import tpu as pltpu
from jax.sharding import PartitionSpec as P

ROWS = 8
PACK = 16
LANES = 128
TILE = 256
MESH = pl.DeviceIdType.MESH
F32 = jnp.float32
BF16 = jnp.bfloat16


def group_kernel(L, H, refs_in, refs_out, s):
    (codes_x, codes_u, dic_hbm, ebias_in, dbias_in, gain_in, gate_hbm, up_hbm, down_hbm) = refs_in
    (out_cols, left, right) = refs_out
    me = lax.axis_index("latent")
    h = lax.axis_index("hidden")
    other = 1 - h
    rows, own_width = codes_x.shape
    width = dic_hbm.shape[1]
    units = dic_hbm.shape[0]
    C = rows // ROWS
    K = C // H
    extra = K - L
    n_dev = L * H
    mine = me * H + h
    pad = out_cols.shape[2]
    rest = own_width - LANES
    per = LANES // rest

    def ext(hid):
        return (2 + 3 * hid) % L

    def at(lat, hid):
        return {"latent": lat, "hidden": hid}

    def rcopy(src, dst, ss, rs, lat, hid):
        return pltpu.make_async_remote_copy(
            src_ref=src, dst_ref=dst, send_sem=ss, recv_sem=rs,
            device_id=at(lat, hid), device_id_type=MESH,
        )

    def each(n, body):
        def step(i, carry):
            body(i)
            return carry

        lax.fori_loop(0, n, step, 0)

    def slots(body):
        body(0, me)
        if extra:
            @pl.when(me == ext(h))
            def _():
                body(1, L)

    barrier = pltpu.get_barrier_semaphore()
    for j in range(L):
        for i in range(H):
            if i or j:
                pl.semaphore_signal(
                    barrier, inc=1, device_id=at(lax.rem(me + j, L), lax.rem(h + i, H)), device_id_type=MESH
                )

    loads = []
    for i, (src, dst) in enumerate((
        (codes_x, s.codes_x), (codes_u, s.codes_u), (dic_hbm, s.dic), (ebias_in, s.ebias),
        (dbias_in, s.dbias), (gain_in, s.gain), (down_hbm, s.down), (gate_hbm, s.gate), (up_hbm, s.up),
    )):
        cp = pltpu.make_async_copy(src, dst, s.load_sem.at[i])
        cp.start()
        loads.append(cp)

    def stage(codes, arr):
        value = codes[...].astype(F32) * (2.0 ** (-6))
        shift = lax.rem(mine * own_width, LANES)
        arr[mine, pl.ds(0, rows)] = pltpu.roll(value[:, :LANES], shift, 1).astype(BF16)
        over = jnp.concatenate([value[:, LANES:], jnp.zeros((rows, LANES - rest), F32)], axis=1)
        for b in range(s.gx.shape[1] // PACK - rows // PACK):
            packed = None
            for g in range(b * per, min((b + 1) * per, rows // PACK)):
                part = over[g * PACK : (g + 1) * PACK]
                part = pltpu.roll(part, (g % per) * rest, 1) if g % per else part
                packed = part if packed is None else packed + part
            arr[mine, pl.ds(rows + b * PACK, PACK)] = packed.astype(BF16)

    X = 2
    Z = L // X
    z, x = me // X, lax.rem(me, X)
    across_me = z * X + 1 - x

    def peer(j):
        if Z == 4:
            return (z + 1 - 2 * lax.rem(z, 2), z + 2 - 4 * (z // 2), 3 - z)[j]
        return lax.rem(z + 1 + j, Z)

    def in_column(j):
        return peer(j) * X + x

    def beside(j):
        return peer(j) * X + 1 - x

    near = range(Z - 1)
    far = (1, 2, 0) if Z == 4 else near
    ext_here = lax.rem(ext(h), X) == x
    ext_mine = me == ext(h)
    ext_passes = jnp.logical_and(ext_here, jnp.logical_not(ext_mine))

    def when_extra(cond, body):
        if extra:
            @pl.when(cond)
            def _():
                body(L, Z)

    def wait_here(buf, sem):
        rcopy(buf, buf, sem, sem, me, other).wait_recv()

    def wait_sent(buf, sem):
        rcopy(buf, buf, sem, sem, me, other).wait_send()

    def cols_start(arr, a):
        for j in far:
            for lat in (beside(j), in_column(j)):
                rcopy(arr.at[mine], arr.at[mine], s.col_ss.at[a], s.col_rs.at[a, me], lat, h).start()
        rcopy(arr.at[mine], arr.at[mine], s.col_ss.at[a], s.col_rs.at[a, me], across_me, h).start()
        rcopy(arr.at[mine], arr.at[mine], s.col_fs.at[a], s.col_fr.at[a], me, other).start()

    def cols_relay(arr, a):
        order = [across_me]
        for j in near:
            order += [in_column(j), beside(j)]
        for lat in order:
            piece = arr.at[lat * H + h]
            wait_here(piece, s.col_rs.at[a, lat])
            rcopy(piece, piece, s.col_fs.at[a], s.col_fr.at[a], me, other).start()

    def cols_take(arr, a):
        wait_here(arr.at[pl.ds(0, L)], s.col_fr.at[a])

    def cols_drain(arr, a):
        wait_sent(arr.at[pl.ds(0, L - 1)], s.col_ss.at[a])
        wait_sent(arr.at[pl.ds(0, L)], s.col_fs.at[a])

    def cols_rows(arr, put):
        lane = lax.broadcasted_iota(jnp.int32, (rows, LANES), 1)

        def main(i):
            return arr[i, pl.ds(0, rows)].astype(F32)

        def over(i):
            block = arr[i, pl.ds(rows, s.gx.shape[1] - rows)].astype(F32)
            parts = []
            for g in range(rows // PACK):
                b = g // per
                move = (i * own_width - (g % per) * rest) % LANES
                part = block[b * PACK : (b + 1) * PACK]
                parts.append(pltpu.roll(part, move, 1) if move else part)
            return jnp.concatenate(parts, axis=0)

        for t in range(width // LANES):
            value = None
            for i in range(n_dev):
                first, offset = divmod(i * own_width, LANES)
                if first == t:
                    new = main(i)
                    value = new if value is None else jnp.where(lane >= offset, new, value)
                elif first == t - 1:
                    value = over(i)
                    if offset:
                        value = jnp.where(lane >= offset, value, main(i))
            put(t, value)

    def hand_over(full, a, k):
        c = h * K + k
        rcopy(full.at[c], full.at[c], s.ag_fs.at[a], s.ag_fr.at[a], me, other).start()

    def step_across(full, a, k, i):
        c = h * K + k
        rcopy(full.at[c], full.at[c], s.ag_xs.at[a], s.ag_xr.at[a, i], across_me, h).start()

    def spread_start(full, a):
        def one(slot, k):
            c = h * K + k
            i = Z if slot else z
            for j in far:
                rcopy(full.at[c], full.at[c], s.ag_ss.at[a, slot], s.ag_rr.at[a, i], in_column(j), h).start()
            step_across(full, a, k, i)
            hand_over(full, a, k)

        slots(one)

    def relay_column(full, a, k, i):
        wait_here(full.at[h * K + k], s.ag_rr.at[a, i])
        step_across(full, a, k, i)
        hand_over(full, a, k)

    def relay_across(full, a, k, i):
        wait_here(full.at[h * K + k], s.ag_xr.at[a, i])
        hand_over(full, a, k)

    def spread_column(full, a):
        for j in near:
            relay_column(full, a, in_column(j), peer(j))
        when_extra(ext_passes, lambda k, i: relay_column(full, a, k, i))

    def spread_across(full, a):
        relay_across(full, a, across_me, z)
        for j in near:
            relay_across(full, a, beside(j), peer(j))
        when_extra(jnp.logical_not(ext_here), lambda k, i: relay_across(full, a, k, i))

    def spread_take(full, a):
        wait_here(full.at[pl.ds(other * K, K)], s.ag_fr.at[a])

    def either(cond, body, less, more):
        if extra:
            @pl.when(cond)
            def _():
                body(more)

            @pl.when(jnp.logical_not(cond))
            def _():
                body(less)
        else:
            body(less)

    def spread_drain(full, a):
        slots(lambda slot, k: wait_sent(full.at[pl.ds(0, Z - 1)], s.ag_ss.at[a, slot]))
        either(ext_here, lambda n: wait_sent(full.at[pl.ds(0, n)], s.ag_xs.at[a]), Z, Z + 1)
        wait_sent(full.at[pl.ds(0, K)], s.ag_fs.at[a])

    def rows_of(full, dst):
        dst[...] = full[...].astype(F32).reshape(rows, width).astype(BF16)

    def sum_tile(a, t, value):
        cols = pl.ds(t * wide, wide)
        s.own[a, :, :, cols] = value.reshape(C, ROWS, wide)
        rcopy(
            s.own.at[a, pl.ds(other * K, K), :, cols], s.sib.at[a, :, :, cols],
            s.rs_cs.at[a], s.rs_cr.at[a], me, other,
        ).start()

    wide = 3 * TILE if width % (3 * TILE) == 0 else LANES
    n_wide = width // wide

    def sum_start(a):
        wait_here(s.sib.at[a], s.rs_cr.at[a])

    def sum_chip(a, k):
        return s.own[a, h * K + k] + s.sib[a, k]

    def sum_middle(a):
        def leave(k, i):
            s.comb[a, k] = sum_chip(a, k).astype(BF16)
            rcopy(s.comb.at[a, k], s.xbuf.at[a, k], s.rs_xs.at[a], s.rs_xr.at[a, i], across_me, h).start()

        for j in far:
            leave(beside(j), peer(j))
        when_extra(jnp.logical_not(ext_here), leave)
        leave(across_me, z)

    def sum_cross(a):
        def total(k, i):
            value = sum_chip(a, k)
            wait_here(s.xbuf.at[a, k], s.rs_xr.at[a, i])
            return value + s.xbuf[a, k].astype(F32)

        def leave(slot, k, i, owner):
            s.comb[a, k] = total(k, i).astype(BF16)
            rcopy(s.comb.at[a, k], s.rbuf.at[a, slot, z], s.rs_ss.at[a], s.rs_rr.at[a, slot], owner, h).start()

        for j in far:
            leave(0, in_column(j), peer(j), in_column(j))
        when_extra(ext_passes, lambda k, i: leave(1, k, i, ext(h)))
        s.acc[a, 0] = total(me, z)

        def keep(k, i):
            s.acc[a, 1] = total(k, i)

        when_extra(ext_mine, keep)

    def sum_value(a, slot):
        value = s.acc[a, slot]
        wait_here(s.rbuf.at[a, slot, pl.ds(0, Z - 1)], s.rs_rr.at[a, slot])
        for j in near:
            value = value + s.rbuf[a, slot, peer(j)].astype(F32)
        return value

    def sum_drain(a):
        wait_sent(s.sib.at[a], s.rs_cs.at[a])
        either(jnp.logical_not(ext_here), lambda n: wait_sent(s.xbuf.at[a, pl.ds(0, n)], s.rs_xs.at[a]), Z, Z + 1)
        either(ext_passes, lambda n: wait_sent(s.xbuf.at[a, pl.ds(0, n)], s.rs_ss.at[a]), Z - 1, Z)

    across = (((1,), (1,)), ((), ()))

    def mm_t(x, w):
        return lax.dot_general(x, w, across, preferred_element_type=F32)

    def mm(x, w):
        return lax.dot_general(x, w, (((1,), (0,)), ((), ())), preferred_element_type=F32)

    deep = TILE if units % TILE == 0 else units
    n_deep = units // deep

    loads[0].wait()
    stage(s.codes_x, s.gx)
    pl.semaphore_wait(barrier, n_dev - 1)
    cols_start(s.gx, 0)
    loads[1].wait()
    stage(s.codes_u, s.gu)
    cols_relay(s.gx, 0)
    cols_start(s.gu, 1)
    cols_take(s.gx, 0)
    x_rows = right.at[pl.ds(rows, rows)]
    r_rows = right.at[pl.ds(0, rows)]

    def put_x(t, value):
        right[pl.ds(rows, rows), t * LANES : (t + 1) * LANES] = value.astype(BF16)
        s.full_x[:, :, t * LANES : (t + 1) * LANES] = value.reshape(C, ROWS, LANES).astype(BF16)

    cols_rows(s.gx, put_x)
    loads[2].wait()
    loads[3].wait()
    for t in range(n_deep):
        cols = pl.ds(t * deep, deep)
        pre = mm_t(x_rows[...], s.dic[cols, :]) + s.ebias[:, cols]
        s.pre[:, cols] = pre
        left[pl.ds(0, rows), cols] = jnp.maximum(pre, 0.0).astype(BF16)
    for t in range(n_wide):
        sum_tile(0, t, mm(left[pl.ds(0, rows), :], s.dic[:, t * wide : (t + 1) * wide]))
    cols_relay(s.gu, 1)
    sum_start(0)
    sum_middle(0)
    sum_cross(0)
    cols_take(s.gu, 1)

    def put_u(t, value):
        s.u_rows[:, t * LANES : (t + 1) * LANES] = value.astype(BF16)

    cols_rows(s.gu, put_u)
    loads[6].wait()
    for t in range(n_deep):
        cols = pl.ds(t * deep, deep)
        s.hgrad[:, cols] = mm_t(s.u_rows[...], s.down[cols, :])
    loads[4].wait()
    loads[5].wait()

    def norm(slot, k):
        rebuilt = sum_value(0, slot) + s.dbias[...]
        inverse = lax.rsqrt(jnp.sum(rebuilt * rebuilt, axis=1, keepdims=True) / width + 1e-06)
        s.rebuilt[slot] = rebuilt
        s.inverse[slot] = jnp.broadcast_to(inverse, (ROWS, LANES))
        s.full_n[h * K + k] = (rebuilt * inverse * s.gain[...]).astype(BF16)

    slots(norm)
    spread_start(s.full_n, 0)
    loads[7].wait()
    loads[8].wait()
    spread_column(s.full_n, 0)
    spread_across(s.full_n, 0)
    spread_take(s.full_n, 0)
    rows_of(s.full_n, s.n_rows)
    for t in range(n_deep):
        cols = pl.ds(t * deep, deep)
        g = mm_t(s.n_rows[...], s.gate[cols, :])
        u = mm_t(s.n_rows[...], s.up[cols, :])
        th = jnp.tanh(0.7978845608028654 * (g + 0.044715 * g * g * g))
        value = 0.5 * g * (1.0 + th)
        slope = 0.5 * (1.0 + th) + 0.5 * g * (1.0 - th * th) * 0.7978845608028654 * (
            1.0 + 3.0 * 0.044715 * g * g
        )
        hg = s.hgrad[:, cols]
        s.hid[:, cols] = (value * u).astype(BF16)
        s.ggrad[:, cols] = (hg * u * slope).astype(BF16)
        s.ugrad[:, cols] = (hg * value).astype(BF16)
    for t in range(n_wide):
        cols = slice(t * wide, (t + 1) * wide)
        sum_tile(1, t, mm(s.ggrad[...], s.gate[:, cols]) + mm(s.ugrad[...], s.up[:, cols]))
    sum_start(1)
    sum_middle(1)
    for t in range(n_wide):
        sum_tile(2, t, mm(s.hid[...], s.down[:, t * wide : (t + 1) * wide]))
    sum_start(2)
    sum_cross(1)
    sum_middle(2)
    sum_cross(2)

    def back(slot, k):
        scaled = sum_value(1, slot) * s.gain[...]
        rebuilt = s.rebuilt[slot]
        inverse = s.inverse[slot][:, :1]
        inner = jnp.sum(scaled * rebuilt, axis=1, keepdims=True)
        target = s.full_x[h * K + k].astype(F32)
        s.full_r[h * K + k] = (
            inverse * scaled - inverse * inverse * inverse * rebuilt * (inner / width) + (rebuilt - target)
        ).astype(BF16)

    def turn_back(slot, k):
        value = sum_value(2, slot)
        c = h * K + k
        for i in range(n_dev):
            piece = value[:, i * own_width : (i + 1) * own_width]
            piece = jnp.concatenate([piece, jnp.zeros((ROWS, pad - own_width), F32)], axis=1)
            s.stage_o[slot, i] = piece.astype(BF16)

        def send(i):
            @pl.when(i != mine)
            def _():
                rcopy(s.stage_o.at[slot, i], s.arr_o.at[c], s.to_ss.at[slot], s.to_rs.at[0], i // H, lax.rem(i, H)).start()

            @pl.when(i == mine)
            def _():
                s.arr_o[c] = s.stage_o[slot, i]

        each(n_dev, send)

    slots(back)
    spread_start(s.full_r, 1)
    spread_column(s.full_r, 1)
    spread_across(s.full_r, 1)
    slots(turn_back)
    spread_take(s.full_r, 1)
    rows_of(s.full_r, r_rows)
    for t in range(n_deep):
        cols = pl.ds(t * deep, deep)
        grad = mm_t(r_rows[...], s.dic[cols, :])
        left[pl.ds(rows, rows), cols] = jnp.where(s.pre[:, cols] > 0.0, grad, 0.0).astype(BF16)

    either(ext_mine, lambda n: wait_here(s.arr_o.at[pl.ds(0, n)], s.to_rs.at[0]), C - 1, C - 2)
    out_cols[...] = s.arr_o[...]

    for a, arr in enumerate((s.gx, s.gu)):
        cols_drain(arr, a)
    for a, full in enumerate((s.full_n, s.full_r)):
        spread_drain(full, a)
    for a in range(3):
        sum_drain(a)
    slots(lambda slot, k: wait_sent(s.stage_o.at[slot, pl.ds(0, n_dev - 1)], s.to_ss.at[slot]))


def run_group(L, H, *args):
    codes, dic = args[0], args[2]
    rows, own_width = codes.shape
    units, width = dic.shape
    C = rows // ROWS
    K = C // H
    Z = L // 2
    n_dev = L * H
    pad = -(-own_width // LANES) * LANES
    per = LANES // (own_width - LANES)
    high = rows + PACK * -(-(rows // PACK) // per)
    V, D, R = pltpu.VMEM, pltpu.SemaphoreType.DMA, ROWS
    scratch = dict(
        codes_x=V((rows, own_width), jnp.int32), codes_u=V((rows, own_width), jnp.int32),
        ebias=V((1, units), F32), dbias=V((width,), F32), gain=V((width,), F32),
        dic=V((units, width), BF16), gate=V((units, width), BF16),
        up=V((units, width), BF16), down=V((units, width), BF16),
        gx=V((n_dev, high, LANES), BF16), gu=V((n_dev, high, LANES), BF16),
        full_x=V((C, R, width), BF16), full_n=V((C, R, width), BF16), full_r=V((C, R, width), BF16),
        u_rows=V((rows, width), BF16), n_rows=V((rows, width), BF16),
        pre=V((rows, units), F32), hgrad=V((rows, units), F32), hid=V((rows, units), BF16),
        ggrad=V((rows, units), BF16), ugrad=V((rows, units), BF16),
        own=V((3, C, R, width), F32), xbuf=V((3, K, R, width), BF16),
        sib=V((3, K, R, width), F32), comb=V((3, K, R, width), BF16),
        rbuf=V((3, 2, Z, R, width), BF16), acc=V((3, 2, R, width), F32),
        rebuilt=V((2, R, width), F32), inverse=V((2, R, LANES), F32),
        stage_o=V((2, n_dev, R, pad), BF16), arr_o=V((C, R, pad), BF16),
        load_sem=D((9,)),
        col_ss=D((2,)), col_rs=D((2, L)), col_fs=D((2,)), col_fr=D((2,)),
        ag_ss=D((2, 2)), ag_xs=D((2,)), ag_xr=D((2, Z + 1)), ag_rr=D((2, Z + 1)), ag_fs=D((2,)), ag_fr=D((2,)),
        rs_cs=D((3,)), rs_cr=D((3,)), rs_ss=D((3,)), rs_rr=D((3, 2)), rs_xs=D((3,)), rs_xr=D((3, Z + 1)),
        to_ss=D((2,)), to_rs=D((1,)),
    )
    names = list(scratch)

    def body(*refs):
        group_kernel(L, H, refs[:9], refs[9:12], types.SimpleNamespace(**dict(zip(names, refs[12:]))))

    hbm = pl.BlockSpec(memory_space=pltpu.HBM)
    vm = pl.BlockSpec(memory_space=pltpu.VMEM)
    cols, left, right = pl.pallas_call(
        body,
        name="group_step",
        out_shape=(
            V((C, R, pad), BF16),
            V((2 * rows, units), BF16),
            V((2 * rows, width), BF16),
        ),
        in_specs=[hbm] * 9,
        out_specs=(vm, vm, vm),
        scratch_shapes=[scratch[n] for n in names],
        compiler_params=pltpu.CompilerParams(collective_id=0, has_side_effects=True, vmem_limit_bytes=60 * 2**20),
    )(*args)

    step = width // 6 if width % (6 * LANES) == 0 else LANES
    n_step = width // step

    def product(cols, left, right, block, grad, tiles, sem):
        copies = []
        for t in range(n_step):
            at = slice(t * step, (t + 1) * step)
            tiles[t] = lax.dot_general(
                left[...], right[:, at], (((0,), (0,)), ((), ())), preferred_element_type=F32
            ).astype(BF16)
            copies.append(pltpu.make_async_copy(tiles.at[t], grad.at[:, at], sem.at[t]))
            copies[-1].start()
        block[...] = cols[...].astype(F32).reshape(rows, pad)[:, :own_width].astype(BF16)
        for cp in copies:
            cp.wait()

    return pl.pallas_call(
        product,
        name="dictionary_product",
        out_shape=(
            jax.ShapeDtypeStruct((rows, own_width), BF16),
            jax.ShapeDtypeStruct((units, width), BF16),
        ),
        in_specs=[vm, vm, vm],
        out_specs=(vm, pl.BlockSpec(memory_space=pl.ANY)),
        scratch_shapes=[V((n_step, units, step), BF16), D((n_step,))],
        compiler_params=pltpu.CompilerParams(vmem_limit_bytes=16 * 2**20),
    )(cols, left, right)


def fits(L, H, rows, own_width, width, units, units_mlp):
    rest = own_width - LANES
    if H != 2 or rows % (ROWS * H) or rows % PACK or width % LANES or units % LANES or units != units_mlp:
        return False
    if rest <= 0 or rest >= LANES or LANES % rest or own_width * L * H != width:
        return False
    return L >= 6 and L % 2 == 0 and 0 <= rows // ROWS // H - L <= 1


CODE_STEP = 2.0 ** (-6)
NORM_EPSILON = 1e-06
GELU_ROOT = 0.7978845608028654
GELU_CUBIC = 0.044715
ACROSS = (((1,), (1,)), ((), ()))
DOWNWARD = (((0,), (0,)), ((), ()))


def gelu_parts(values):
    argument = GELU_ROOT * (values + GELU_CUBIC * values * values * values)
    tanh_value = jnp.tanh(argument)
    result = 0.5 * values * (1.0 + tanh_value)
    derivative = 0.5 * (1.0 + tanh_value) + 0.5 * values * (
        1.0 - tanh_value * tanh_value
    ) * GELU_ROOT * (1.0 + 3.0 * GELU_CUBIC * values * values)
    return (result, derivative)


def per_device(
    input_codes,
    cotangent_codes,
    dictionary,
    encoder_bias,
    decoder_bias,
    norm_gain,
    gate_weight,
    up_weight,
    down_weight,
):
    L, H = lax.axis_size("latent"), lax.axis_size("hidden")
    rows, width = input_codes.shape[0], dictionary.shape[1]
    if fits(L, H, rows, input_codes.shape[1], width, dictionary.shape[0], gate_weight.shape[0]):
        return run_group(
            L, H, input_codes, cotangent_codes, dictionary, encoder_bias[None, :], decoder_bias,
            norm_gain, gate_weight, up_weight, down_weight,
        )
    own_width = input_codes.shape[1]
    model_width = own_width * lax.axis_size(("latent", "hidden"))
    cotangent_local = (cotangent_codes.astype(jnp.float32) * CODE_STEP).astype(jnp.bfloat16)
    hidden_grad = None
    inputs_local = (input_codes.astype(jnp.float32) * CODE_STEP).astype(jnp.bfloat16)
    inputs = lax.all_gather(inputs_local, ("latent", "hidden"), axis=1, tiled=True)
    preact = (
        lax.dot_general(inputs, dictionary, ACROSS, preferred_element_type=jnp.float32)
        + encoder_bias
    )
    latents = jnp.maximum(preact, 0.0).astype(jnp.bfloat16)
    partial_value = jnp.dot(latents, dictionary, preferred_element_type=jnp.float32)
    rebuilt = lax.psum(partial_value, ("latent", "hidden")) + decoder_bias
    inverse = lax.rsqrt(
        jnp.sum(rebuilt * rebuilt, axis=1, keepdims=True) / model_width + NORM_EPSILON
    )
    normed = (rebuilt * inverse * norm_gain).astype(jnp.bfloat16)
    target = inputs.astype(jnp.float32)
    gate_proj = lax.dot_general(normed, gate_weight, ACROSS, preferred_element_type=jnp.float32)
    up_proj = lax.dot_general(normed, up_weight, ACROSS, preferred_element_type=jnp.float32)
    gelu_value, gelu_slope = gelu_parts(gate_proj)
    hidden = (gelu_value * up_proj).astype(jnp.bfloat16)
    output_terms = jnp.dot(hidden, down_weight, preferred_element_type=jnp.float32)
    block_output = lax.psum_scatter(
        output_terms, ("latent", "hidden"), scatter_dimension=1, tiled=True
    ).astype(jnp.bfloat16)
    hidden_grad = lax.dot_general(
        lax.all_gather(cotangent_local, ("latent", "hidden"), axis=1, tiled=True),
        down_weight,
        ACROSS,
        preferred_element_type=jnp.float32,
    )
    gate_grad = (hidden_grad * up_proj * gelu_slope).astype(jnp.bfloat16)
    up_grad = (hidden_grad * gelu_value).astype(jnp.bfloat16)
    partial_grad = jnp.dot(gate_grad, gate_weight, preferred_element_type=jnp.float32) + jnp.dot(
        up_grad, up_weight, preferred_element_type=jnp.float32
    )
    scaled = lax.psum(partial_grad, ("latent", "hidden")) * norm_gain
    inner_row = jnp.sum(scaled * rebuilt, axis=1, keepdims=True)
    inverse_cube = inverse * inverse * inverse
    rebuilt_grad = (
        inverse * scaled - inverse_cube * rebuilt * (inner_row / model_width) + (rebuilt - target)
    ).astype(jnp.bfloat16)
    latent_grad = lax.dot_general(
        rebuilt_grad, dictionary, ACROSS, preferred_element_type=jnp.float32
    )
    preact_grad = jnp.where(preact > 0.0, latent_grad, 0.0).astype(jnp.bfloat16)
    dictionary_grad = lax.dot_general(
        latents, rebuilt_grad, DOWNWARD, preferred_element_type=jnp.float32
    ) + lax.dot_general(preact_grad, inputs, DOWNWARD, preferred_element_type=jnp.float32)
    return (block_output, dictionary_grad.astype(jnp.bfloat16))


def solution(mesh):
    in_specs = (
        P("groups", ("latent", "hidden")),
        P("groups", ("latent", "hidden")),
        P(("latent", "hidden"), None),
        P(("latent", "hidden")),
        P(),
        P(),
        P(("latent", "hidden"), None),
        P(("latent", "hidden"), None),
        P(("latent", "hidden"), None),
    )
    out_specs = (P("groups", ("latent", "hidden")), P(("latent", "hidden"), "groups"))
    return jax.shard_map(
        per_device, mesh=mesh, in_specs=in_specs, out_specs=out_specs, check_vma=False
    )
```

```python
import types

import jax
import jax.numpy as jnp
from jax import lax
from jax.experimental import pallas as pl
from jax.experimental.pallas import tpu as pltpu
from jax.sharding import PartitionSpec as P

ROWS = 8
PACK = 16
LANES = 128
TILE = 256
MESH = pl.DeviceIdType.MESH
F32 = jnp.float32
BF16 = jnp.bfloat16


def group_kernel(L, H, refs_in, refs_out, s):
    (codes_x, codes_u, dic_hbm, ebias_in, dbias_in, gain_in, gate_hbm, up_hbm, down_hbm) = refs_in
    (out_cols, left, right) = refs_out
    me = lax.axis_index("latent")
    h = lax.axis_index("hidden")
    other = 1 - h
    rows, own_width = codes_x.shape
    width = dic_hbm.shape[1]
    units = dic_hbm.shape[0]
    C = rows // ROWS
    K = C // H
    extra = K - L
    n_dev = L * H
    mine = me * H + h
    high = s.gx.shape[1]
    rest = own_width - LANES
    per = LANES // rest

    def ext(hid):
        return (2 + 3 * hid) % L

    def at(lat, hid):
        return {"latent": lat, "hidden": hid}

    def rcopy(src, dst, ss, rs, lat, hid):
        return pltpu.make_async_remote_copy(
            src_ref=src, dst_ref=dst, send_sem=ss, recv_sem=rs,
            device_id=at(lat, hid), device_id_type=MESH,
        )

    def each(n, body):
        def step(i, carry):
            body(i)
            return carry

        lax.fori_loop(0, n, step, 0)

    def slots(body):
        body(0, me)
        if extra:
            @pl.when(me == ext(h))
            def _():
                body(1, L)

    barrier = pltpu.get_barrier_semaphore()
    for j in range(L):
        for i in range(H):
            if i or j:
                pl.semaphore_signal(
                    barrier, inc=1, device_id=at(lax.rem(me + j, L), lax.rem(h + i, H)), device_id_type=MESH
                )

    loads = []
    for i, (src, dst) in enumerate((
        (codes_x, s.codes_x), (codes_u, s.codes_u), (dic_hbm, s.dic), (ebias_in, s.ebias),
        (dbias_in, s.dbias), (gain_in, s.gain), (down_hbm, s.down), (gate_hbm, s.gate), (up_hbm, s.up),
    )):
        cp = pltpu.make_async_copy(src, dst, s.load_sem.at[i])
        cp.start()
        loads.append(cp)

    def stage(codes, arr):
        value = codes[...].astype(F32) * (2.0 ** (-6))
        shift = lax.rem(mine * own_width, LANES)
        arr[mine, pl.ds(0, rows)] = pltpu.roll(value[:, :LANES], shift, 1).astype(BF16)
        over = jnp.concatenate([value[:, LANES:], jnp.zeros((rows, LANES - rest), F32)], axis=1)
        for b in range(s.gx.shape[1] // PACK - rows // PACK):
            packed = None
            for g in range(b * per, min((b + 1) * per, rows // PACK)):
                part = over[g * PACK : (g + 1) * PACK]
                part = pltpu.roll(part, (g % per) * rest, 1) if g % per else part
                packed = part if packed is None else packed + part
            arr[mine, pl.ds(rows + b * PACK, PACK)] = packed.astype(BF16)

    X = 2
    Z = L // X
    z, x = me // X, lax.rem(me, X)
    across_me = z * X + 1 - x
    near_z, same_z, flip_z = z + 1 - 2 * lax.rem(z, 2), z + 2 - 4 * (z // 2), 3 - z
    peers = (near_z, same_z, flip_z)
    far = (same_z, flip_z, near_z)

    def col(zz):
        return zz * X + x

    def beside(zz):
        return zz * X + 1 - x

    ext_z = ext(h) // X
    ext_here = lax.rem(ext(h), X) == x
    ext_mine = me == ext(h)
    ext_passes = jnp.logical_and(ext_here, jnp.logical_not(ext_mine))

    def when_extra(cond, body):
        if extra:
            @pl.when(cond)
            def _():
                body(L, Z)

    def wait_here(buf, sem):
        rcopy(buf, buf, sem, sem, me, other).wait_recv()

    def wait_sent(buf, sem):
        rcopy(buf, buf, sem, sem, me, other).wait_send()

    def cols_send(arr, a, i, lat):
        rcopy(arr.at[i], arr.at[i], s.col_ss.at[a], s.col_rs.at[a, i // H], lat, h).start()

    def cols_give(arr, a, i):
        rcopy(arr.at[i], arr.at[i], s.col_fs.at[a], s.col_fr.at[a], me, other).start()

    def cols_got(arr, a, lat, relay=False):
        i = lat * H + h
        wait_here(arr.at[i], s.col_rs.at[a, lat])
        if relay:
            cols_send(arr, a, i, across_me)
        cols_give(arr, a, i)

    def cols_start(arr, a):
        for zz in far:
            for lat in (beside(zz), col(zz)):
                cols_send(arr, a, mine, lat)
        cols_send(arr, a, mine, across_me)
        cols_give(arr, a, mine)

    def cols_relay(arr, a):
        cols_got(arr, a, across_me)
        for zz in peers:
            cols_got(arr, a, col(zz))
            cols_got(arr, a, beside(zz))

    def cols_lean_start(arr, a):
        for zz in far:
            cols_send(arr, a, mine, col(zz))
        cols_send(arr, a, mine, across_me)
        cols_give(arr, a, mine)

    def cols_lean_column(arr, a):
        for zz in peers:
            cols_got(arr, a, col(zz), True)

    def cols_lean_across(arr, a):
        cols_got(arr, a, across_me)
        for zz in peers:
            cols_got(arr, a, beside(zz))

    def cols_take(arr, a):
        wait_here(arr.at[pl.ds(0, L)], s.col_fr.at[a])

    def cols_drain(arr, a):
        wait_sent(arr.at[pl.ds(0, L - 1)], s.col_ss.at[a])
        wait_sent(arr.at[pl.ds(0, L)], s.col_fs.at[a])

    def cols_rows(arr, put):
        lane = lax.broadcasted_iota(jnp.int32, (rows, LANES), 1)

        def main(i):
            return arr[i, pl.ds(0, rows)].astype(F32)

        def over(i):
            block = arr[i, pl.ds(rows, s.gx.shape[1] - rows)].astype(F32)
            parts = []
            for g in range(rows // PACK):
                b = g // per
                move = (i * own_width - (g % per) * rest) % LANES
                part = block[b * PACK : (b + 1) * PACK]
                parts.append(pltpu.roll(part, move, 1) if move else part)
            return jnp.concatenate(parts, axis=0)

        for t in range(width // LANES):
            value = None
            for i in range(n_dev):
                first, offset = divmod(i * own_width, LANES)
                if first == t:
                    new = main(i)
                    value = new if value is None else jnp.where(lane >= offset, new, value)
                elif first == t - 1:
                    value = over(i)
                    if offset:
                        value = jnp.where(lane >= offset, value, main(i))
            put(t, value)

    def hand_over(full, a, k):
        c = h * K + k
        rcopy(full.at[c], full.at[c], s.ag_fs.at[a], s.ag_fr.at[a], me, other).start()

    def step_across(full, a, k, i):
        c = h * K + k
        rcopy(full.at[c], full.at[c], s.ag_xs.at[a], s.ag_xr.at[a, i], across_me, h).start()

    def spread_start(full, a):
        def one(slot, k):
            c = h * K + k
            i = Z if slot else z
            for zz in far:
                rcopy(full.at[c], full.at[c], s.ag_ss.at[a, slot], s.ag_rr.at[a, i], col(zz), h).start()
            step_across(full, a, k, i)
            hand_over(full, a, k)

        slots(one)

    def relay_column(full, a, k, i):
        wait_here(full.at[h * K + k], s.ag_rr.at[a, i])
        step_across(full, a, k, i)
        hand_over(full, a, k)

    def relay_across(full, a, k, i):
        wait_here(full.at[h * K + k], s.ag_xr.at[a, i])
        hand_over(full, a, k)

    def spread_column(full, a):
        for zz in peers:
            relay_column(full, a, col(zz), zz)
        when_extra(ext_passes, lambda k, i: relay_column(full, a, k, i))

    def spread_across(full, a):
        relay_across(full, a, across_me, z)
        for zz in peers:
            relay_across(full, a, beside(zz), zz)
        when_extra(jnp.logical_not(ext_here), lambda k, i: relay_across(full, a, k, i))

    def spread_take(full, a):
        wait_here(full.at[pl.ds(other * K, K)], s.ag_fr.at[a])

    def either(cond, body, no, yes):
        @pl.when(cond)
        def _():
            body(yes)

        @pl.when(jnp.logical_not(cond))
        def _():
            body(no)

    def spread_drain(full, a):
        slots(lambda slot, k: wait_sent(full.at[pl.ds(0, Z - 1)], s.ag_ss.at[a, slot]))
        either(ext_here, lambda n: wait_sent(full.at[pl.ds(0, n)], s.ag_xs.at[a]), Z, Z + 1)
        wait_sent(full.at[pl.ds(0, K)], s.ag_fs.at[a])

    def rows_of(full, dst):
        dst[...] = full[...].astype(F32).reshape(rows, width).astype(BF16)

    def sum_tile(a, t, value):
        cols = pl.ds(t * wide, wide)
        s.own[a, :, :, cols] = value.reshape(C, ROWS, wide)
        rcopy(
            s.own.at[a, pl.ds(other * K, K), :, cols], s.sib.at[a, :, :, cols],
            s.rs_cs.at[a], s.rs_cr.at[a], me, other,
        ).start()

    wide = 3 * TILE if width % (3 * TILE) == 0 else LANES
    n_wide = width // wide

    def sum_start(a):
        wait_here(s.sib.at[a], s.rs_cr.at[a])

    def sum_chip(a, k):
        return s.own[a, h * K + k] + s.sib[a, k]

    def sum_middle(a):
        def leave(k, i):
            s.comb[a, k] = sum_chip(a, k).astype(BF16)
            rcopy(s.comb.at[a, k], s.xbuf.at[a, k], s.rs_xs.at[a], s.rs_xr.at[a, i], across_me, h).start()

        for zz in far:
            leave(beside(zz), zz)
        when_extra(jnp.logical_not(ext_here), leave)
        leave(across_me, z)

    def sum_cross(a):
        def total(k, i):
            value = sum_chip(a, k)
            wait_here(s.xbuf.at[a, k], s.rs_xr.at[a, i])
            return value + s.xbuf[a, k].astype(F32)

        def leave(slot, k, i, owner):
            s.comb[a, k] = total(k, i).astype(BF16)
            rcopy(s.comb.at[a, k], s.rbuf.at[a, slot, z], s.rs_ss.at[a], s.rs_rr.at[a, slot], owner, h).start()

        for zz in far:
            leave(0, col(zz), zz, col(zz))
        when_extra(ext_passes, lambda k, i: leave(1, k, i, ext(h)))
        s.acc[a, 0] = total(me, z)

        def keep(k, i):
            s.acc[a, 1] = total(k, i)

        when_extra(ext_mine, keep)

    def sum_value(a, slot):
        value = s.acc[a, slot]
        wait_here(s.rbuf.at[a, slot, pl.ds(0, Z - 1)], s.rs_rr.at[a, slot])
        for zz in peers:
            value = value + s.rbuf[a, slot, zz].astype(F32)
        return value

    def sum_drain(a):
        wait_sent(s.sib.at[a], s.rs_cs.at[a])
        either(jnp.logical_not(ext_here), lambda n: wait_sent(s.xbuf.at[a, pl.ds(0, n)], s.rs_xs.at[a]), Z, Z + 1)
        either(ext_passes, lambda n: wait_sent(s.xbuf.at[a, pl.ds(0, n)], s.rs_ss.at[a]), Z - 1, Z)

    def out_tile(t, value):
        s.wide_out[:, t * wide : (t + 1) * wide] = value

    def out_pieces():
        lane = lax.broadcasted_iota(jnp.int32, (rows, LANES), 1)
        group = lax.broadcasted_iota(jnp.int32, (PACK, LANES), 1) // rest
        for i in range(n_dev):
            first, offset = divmod(i * own_width, LANES)
            here = s.wide_out[:, first * LANES : (first + 1) * LANES]
            there = s.wide_out[:, (first + 1) * LANES : (first + 2) * LANES]
            piece = s.own_out.at[i % H, i // H]
            piece[pl.ds(0, rows)] = jnp.where(lane >= offset, here, there) if offset else here
            for b in range(high // PACK - rows // PACK):
                packed = jnp.zeros((PACK, LANES), F32)
                for g in range(b * per, min((b + 1) * per, rows // PACK)):
                    part = there[g * PACK : (g + 1) * PACK]
                    move = ((g % per) * rest - offset) % LANES
                    part = pltpu.roll(part, move, 1) if move else part
                    packed = jnp.where(group == g % per, part, packed)
                piece[pl.ds(rows + b * PACK, PACK)] = packed
        rcopy(s.own_out.at[other], s.sib_out, s.out_cs.at[0], s.out_cr.at[0], me, other).start()

    def out_chip(lat):
        return s.own_out[h, lat] + s.sib_out[lat]

    def out_middle():
        wait_here(s.sib_out, s.out_cr.at[0])
        for lat, i in [(beside(zz), zz) for zz in far] + [(across_me, z)]:
            s.comb_out[lat] = out_chip(lat).astype(BF16)
            rcopy(s.comb_out.at[lat], s.xbuf_out.at[lat], s.out_xs.at[0], s.out_xr.at[i], across_me, h).start()

    def out_total(lat, i):
        wait_here(s.xbuf_out.at[lat], s.out_xr.at[i])
        return out_chip(lat) + s.xbuf_out[lat].astype(F32)

    def out_cross():
        for zz in far:
            lat = col(zz)
            s.comb_out[lat] = out_total(lat, zz).astype(BF16)
            rcopy(s.comb_out.at[lat], s.rbuf_out.at[z], s.out_ss.at[0], s.out_rr.at[0], lat, h).start()
        s.acc_out[...] = out_total(me, z)

    def out_final():
        wait_here(s.rbuf_out.at[pl.ds(0, Z - 1)], s.out_rr.at[0])
        value = s.acc_out[...]
        for zz in peers:
            value = value + s.rbuf_out[zz].astype(F32)
        back_by = lax.rem(LANES - lax.rem(mine * own_width, LANES), LANES)
        out_cols[:, :LANES] = pltpu.roll(value[:rows], back_by, 1).astype(BF16)
        parts = []
        for g in range(rows // PACK):
            part = value[rows + (g // per) * PACK : rows + (g // per + 1) * PACK]
            move = (-(g % per) * rest) % LANES
            parts.append(pltpu.roll(part, move, 1) if move else part)
        out_cols[:, LANES:] = jnp.concatenate(parts, axis=0)[:, :rest].astype(BF16)

    def out_drain():
        wait_sent(s.sib_out, s.out_cs.at[0])
        wait_sent(s.xbuf_out.at[pl.ds(0, Z)], s.out_xs.at[0])
        wait_sent(s.xbuf_out.at[pl.ds(0, Z - 1)], s.out_ss.at[0])

    across = (((1,), (1,)), ((), ()))

    def mm_t(x, w):
        return lax.dot_general(x, w, across, preferred_element_type=F32)

    def mm(x, w):
        return lax.dot_general(x, w, (((1,), (0,)), ((), ())), preferred_element_type=F32)

    deep = TILE if units % TILE == 0 else units
    n_deep = units // deep

    loads[0].wait()
    stage(s.codes_x, s.gx)
    pl.semaphore_wait(barrier, n_dev - 1)
    cols_start(s.gx, 0)
    loads[1].wait()
    stage(s.codes_u, s.gu)
    cols_relay(s.gx, 0)
    cols_lean_start(s.gu, 1)
    cols_take(s.gx, 0)
    x_rows = right.at[pl.ds(rows, rows)]
    r_rows = right.at[pl.ds(0, rows)]

    def put_x(t, value):
        right[pl.ds(rows, rows), t * LANES : (t + 1) * LANES] = value.astype(BF16)
        s.full_x[:, :, t * LANES : (t + 1) * LANES] = value.reshape(C, ROWS, LANES).astype(BF16)

    cols_rows(s.gx, put_x)
    loads[2].wait()
    loads[3].wait()
    for t in range(n_deep):
        cols = pl.ds(t * deep, deep)
        pre = mm_t(x_rows[...], s.dic[cols, :]) + s.ebias[:, cols]
        s.pre[:, cols] = pre
        left[pl.ds(0, rows), cols] = jnp.maximum(pre, 0.0).astype(BF16)
    for t in range(n_wide):
        sum_tile(0, t, mm(left[pl.ds(0, rows), :], s.dic[:, t * wide : (t + 1) * wide]))
    sum_start(0)
    sum_middle(0)
    sum_cross(0)
    cols_lean_column(s.gu, 1)

    def put_u(t, value):
        s.u_rows[:, t * LANES : (t + 1) * LANES] = value.astype(BF16)

    loads[4].wait()
    loads[5].wait()

    def norm(slot, k):
        rebuilt = sum_value(0, slot) + s.dbias[...]
        inverse = lax.rsqrt(jnp.sum(rebuilt * rebuilt, axis=1, keepdims=True) / width + 1e-06)
        s.rebuilt[slot] = rebuilt
        s.inverse[slot] = jnp.broadcast_to(inverse, (ROWS, LANES))
        s.full_n[h * K + k] = (rebuilt * inverse * s.gain[...]).astype(BF16)

    slots(norm)
    spread_start(s.full_n, 0)
    cols_lean_across(s.gu, 1)
    cols_take(s.gu, 1)
    cols_rows(s.gu, put_u)
    loads[6].wait()
    for t in range(n_deep):
        cols = pl.ds(t * deep, deep)
        s.hgrad[:, cols] = mm_t(s.u_rows[...], s.down[cols, :])
    loads[7].wait()
    loads[8].wait()
    spread_column(s.full_n, 0)
    spread_across(s.full_n, 0)
    spread_take(s.full_n, 0)
    rows_of(s.full_n, s.n_rows)
    for t in range(n_deep):
        cols = pl.ds(t * deep, deep)
        g = mm_t(s.n_rows[...], s.gate[cols, :])
        u = mm_t(s.n_rows[...], s.up[cols, :])
        th = jnp.tanh(0.7978845608028654 * (g + 0.044715 * g * g * g))
        value = 0.5 * g * (1.0 + th)
        slope = 0.5 * (1.0 + th) + 0.5 * g * (1.0 - th * th) * 0.7978845608028654 * (
            1.0 + 3.0 * 0.044715 * g * g
        )
        hg = s.hgrad[:, cols]
        s.hid[:, cols] = (value * u).astype(BF16)
        s.ggrad[:, cols] = (hg * u * slope).astype(BF16)
        s.ugrad[:, cols] = (hg * value).astype(BF16)
    for t in range(n_wide):
        cols = slice(t * wide, (t + 1) * wide)
        sum_tile(1, t, mm(s.ggrad[...], s.gate[:, cols]) + mm(s.ugrad[...], s.up[:, cols]))
    sum_start(1)
    sum_middle(1)
    for t in range(n_wide):
        out_tile(t, mm(s.hid[...], s.down[:, t * wide : (t + 1) * wide]))
    out_pieces()
    sum_cross(1)
    out_middle()

    def back(slot, k):
        scaled = sum_value(1, slot) * s.gain[...]
        rebuilt = s.rebuilt[slot]
        inverse = s.inverse[slot][:, :1]
        inner = jnp.sum(scaled * rebuilt, axis=1, keepdims=True)
        target = s.full_x[h * K + k].astype(F32)
        s.full_r[h * K + k] = (
            inverse * scaled - inverse * inverse * inverse * rebuilt * (inner / width) + (rebuilt - target)
        ).astype(BF16)

    slots(back)
    spread_start(s.full_r, 1)
    spread_column(s.full_r, 1)
    out_cross()
    spread_across(s.full_r, 1)
    spread_take(s.full_r, 1)
    rows_of(s.full_r, r_rows)
    for t in range(n_deep):
        cols = pl.ds(t * deep, deep)
        grad = mm_t(r_rows[...], s.dic[cols, :])
        left[pl.ds(rows, rows), cols] = jnp.where(s.pre[:, cols] > 0.0, grad, 0.0).astype(BF16)

    out_final()
    for a, arr in enumerate((s.gx, s.gu)):
        cols_drain(arr, a)
    for a, full in enumerate((s.full_n, s.full_r)):
        spread_drain(full, a)
    for a in range(2):
        sum_drain(a)
    out_drain()


def run_group(L, H, *args):
    codes, dic = args[0], args[2]
    rows, own_width = codes.shape
    units, width = dic.shape
    C = rows // ROWS
    K = C // H
    Z = L // 2
    n_dev = L * H
    per = LANES // (own_width - LANES)
    high = rows + PACK * -(-(rows // PACK) // per)
    V, D, R = pltpu.VMEM, pltpu.SemaphoreType.DMA, ROWS
    scratch = dict(
        codes_x=V((rows, own_width), jnp.int32), codes_u=V((rows, own_width), jnp.int32),
        ebias=V((1, units), F32), dbias=V((width,), F32), gain=V((width,), F32),
        dic=V((units, width), BF16), gate=V((units, width), BF16),
        up=V((units, width), BF16), down=V((units, width), BF16),
        gx=V((n_dev, high, LANES), BF16), gu=V((n_dev, high, LANES), BF16),
        full_x=V((C, R, width), BF16), full_n=V((C, R, width), BF16), full_r=V((C, R, width), BF16),
        u_rows=V((rows, width), BF16), n_rows=V((rows, width), BF16),
        pre=V((rows, units), F32), hgrad=V((rows, units), F32), hid=V((rows, units), BF16),
        ggrad=V((rows, units), BF16), ugrad=V((rows, units), BF16),
        own=V((2, C, R, width), F32), xbuf=V((2, K, R, width), BF16),
        sib=V((2, K, R, width), F32), comb=V((2, K, R, width), BF16),
        rbuf=V((2, 2, Z, R, width), BF16), acc=V((2, 2, R, width), F32),
        rebuilt=V((2, R, width), F32), inverse=V((2, R, LANES), F32),
        wide_out=V((rows, width), F32), own_out=V((H, L, high, LANES), F32), sib_out=V((L, high, LANES), F32),
        comb_out=V((L, high, LANES), BF16), xbuf_out=V((L, high, LANES), BF16),
        rbuf_out=V((Z, high, LANES), BF16), acc_out=V((high, LANES), F32),
        load_sem=D((9,)),
        col_ss=D((2,)), col_rs=D((2, L)), col_fs=D((2,)), col_fr=D((2,)),
        ag_ss=D((2, 2)), ag_xs=D((2,)), ag_xr=D((2, Z + 1)), ag_rr=D((2, Z + 1)), ag_fs=D((2,)), ag_fr=D((2,)),
        rs_cs=D((2,)), rs_cr=D((2,)), rs_ss=D((2,)), rs_rr=D((2, 2)), rs_xs=D((2,)), rs_xr=D((2, Z + 1)),
        out_cs=D((1,)), out_cr=D((1,)), out_xs=D((1,)), out_xr=D((Z,)), out_ss=D((1,)), out_rr=D((1,)),
    )
    names = list(scratch)

    def body(*refs):
        group_kernel(L, H, refs[:9], refs[9:12], types.SimpleNamespace(**dict(zip(names, refs[12:]))))

    hbm = pl.BlockSpec(memory_space=pltpu.HBM)
    vm = pl.BlockSpec(memory_space=pltpu.VMEM)
    cols, left, right = pl.pallas_call(
        body,
        name="group_step",
        out_shape=(
            V((rows, own_width), BF16),
            V((2 * rows, units), BF16),
            V((2 * rows, width), BF16),
        ),
        in_specs=[hbm] * 9,
        out_specs=(vm, vm, vm),
        scratch_shapes=[scratch[n] for n in names],
        compiler_params=pltpu.CompilerParams(collective_id=0, has_side_effects=True, vmem_limit_bytes=60 * 2**20),
    )(*args)

    step = width // 6 if width % (6 * LANES) == 0 else LANES
    n_step = width // step

    def product(cols, left, right, block, grad, tiles, sem):
        copies = []
        for t in range(n_step):
            at = slice(t * step, (t + 1) * step)
            tiles[t] = lax.dot_general(
                left[...], right[:, at], (((0,), (0,)), ((), ())), preferred_element_type=F32
            ).astype(BF16)
            copies.append(pltpu.make_async_copy(tiles.at[t], grad.at[:, at], sem.at[t]))
            copies[-1].start()
        block[...] = cols[...]
        for cp in copies:
            cp.wait()

    return pl.pallas_call(
        product,
        name="dictionary_product",
        out_shape=(
            jax.ShapeDtypeStruct((rows, own_width), BF16),
            jax.ShapeDtypeStruct((units, width), BF16),
        ),
        in_specs=[vm, vm, vm],
        out_specs=(vm, pl.BlockSpec(memory_space=pl.ANY)),
        scratch_shapes=[V((n_step, units, step), BF16), D((n_step,))],
        compiler_params=pltpu.CompilerParams(vmem_limit_bytes=16 * 2**20),
    )(cols, left, right)


def fits(L, H, rows, own_width, width, units, units_mlp):
    rest = own_width - LANES
    if H != 2 or rows % (ROWS * H) or rows % PACK or width % LANES or units % LANES or units != units_mlp:
        return False
    if rest <= 0 or rest >= LANES or LANES % rest or own_width * L * H != width:
        return False
    return L == 8 and rows // ROWS // H == L + 1


CODE_STEP = 2.0 ** (-6)
NORM_EPSILON = 1e-06
GELU_ROOT = 0.7978845608028654
GELU_CUBIC = 0.044715
ACROSS = (((1,), (1,)), ((), ()))
DOWNWARD = (((0,), (0,)), ((), ()))


def gelu_parts(values):
    argument = GELU_ROOT * (values + GELU_CUBIC * values * values * values)
    tanh_value = jnp.tanh(argument)
    result = 0.5 * values * (1.0 + tanh_value)
    derivative = 0.5 * (1.0 + tanh_value) + 0.5 * values * (
        1.0 - tanh_value * tanh_value
    ) * GELU_ROOT * (1.0 + 3.0 * GELU_CUBIC * values * values)
    return (result, derivative)


def per_device(
    input_codes,
    cotangent_codes,
    dictionary,
    encoder_bias,
    decoder_bias,
    norm_gain,
    gate_weight,
    up_weight,
    down_weight,
):
    L, H = lax.axis_size("latent"), lax.axis_size("hidden")
    rows, width = input_codes.shape[0], dictionary.shape[1]
    if fits(L, H, rows, input_codes.shape[1], width, dictionary.shape[0], gate_weight.shape[0]):
        return run_group(
            L, H, input_codes, cotangent_codes, dictionary, encoder_bias[None, :], decoder_bias,
            norm_gain, gate_weight, up_weight, down_weight,
        )
    own_width = input_codes.shape[1]
    model_width = own_width * lax.axis_size(("latent", "hidden"))
    cotangent_local = (cotangent_codes.astype(jnp.float32) * CODE_STEP).astype(jnp.bfloat16)
    hidden_grad = None
    inputs_local = (input_codes.astype(jnp.float32) * CODE_STEP).astype(jnp.bfloat16)
    inputs = lax.all_gather(inputs_local, ("latent", "hidden"), axis=1, tiled=True)
    preact = (
        lax.dot_general(inputs, dictionary, ACROSS, preferred_element_type=jnp.float32)
        + encoder_bias
    )
    latents = jnp.maximum(preact, 0.0).astype(jnp.bfloat16)
    partial_value = jnp.dot(latents, dictionary, preferred_element_type=jnp.float32)
    rebuilt = lax.psum(partial_value, ("latent", "hidden")) + decoder_bias
    inverse = lax.rsqrt(
        jnp.sum(rebuilt * rebuilt, axis=1, keepdims=True) / model_width + NORM_EPSILON
    )
    normed = (rebuilt * inverse * norm_gain).astype(jnp.bfloat16)
    target = inputs.astype(jnp.float32)
    gate_proj = lax.dot_general(normed, gate_weight, ACROSS, preferred_element_type=jnp.float32)
    up_proj = lax.dot_general(normed, up_weight, ACROSS, preferred_element_type=jnp.float32)
    gelu_value, gelu_slope = gelu_parts(gate_proj)
    hidden = (gelu_value * up_proj).astype(jnp.bfloat16)
    output_terms = jnp.dot(hidden, down_weight, preferred_element_type=jnp.float32)
    block_output = lax.psum_scatter(
        output_terms, ("latent", "hidden"), scatter_dimension=1, tiled=True
    ).astype(jnp.bfloat16)
    hidden_grad = lax.dot_general(
        lax.all_gather(cotangent_local, ("latent", "hidden"), axis=1, tiled=True),
        down_weight,
        ACROSS,
        preferred_element_type=jnp.float32,
    )
    gate_grad = (hidden_grad * up_proj * gelu_slope).astype(jnp.bfloat16)
    up_grad = (hidden_grad * gelu_value).astype(jnp.bfloat16)
    partial_grad = jnp.dot(gate_grad, gate_weight, preferred_element_type=jnp.float32) + jnp.dot(
        up_grad, up_weight, preferred_element_type=jnp.float32
    )
    scaled = lax.psum(partial_grad, ("latent", "hidden")) * norm_gain
    inner_row = jnp.sum(scaled * rebuilt, axis=1, keepdims=True)
    inverse_cube = inverse * inverse * inverse
    rebuilt_grad = (
        inverse * scaled - inverse_cube * rebuilt * (inner_row / model_width) + (rebuilt - target)
    ).astype(jnp.bfloat16)
    latent_grad = lax.dot_general(
        rebuilt_grad, dictionary, ACROSS, preferred_element_type=jnp.float32
    )
    preact_grad = jnp.where(preact > 0.0, latent_grad, 0.0).astype(jnp.bfloat16)
    dictionary_grad = lax.dot_general(
        latents, rebuilt_grad, DOWNWARD, preferred_element_type=jnp.float32
    ) + lax.dot_general(preact_grad, inputs, DOWNWARD, preferred_element_type=jnp.float32)
    return (block_output, dictionary_grad.astype(jnp.bfloat16))


def solution(mesh):
    in_specs = (
        P("groups", ("latent", "hidden")),
        P("groups", ("latent", "hidden")),
        P(("latent", "hidden"), None),
        P(("latent", "hidden")),
        P(),
        P(),
        P(("latent", "hidden"), None),
        P(("latent", "hidden"), None),
        P(("latent", "hidden"), None),
    )
    out_specs = (P("groups", ("latent", "hidden")), P(("latent", "hidden"), "groups"))
    return jax.shard_map(
        per_device, mesh=mesh, in_specs=in_specs, out_specs=out_specs, check_vma=False
    )
```

```python
import types

import jax
import jax.numpy as jnp
from jax import lax
from jax.experimental import pallas as pl
from jax.experimental.pallas import tpu as pltpu
from jax.sharding import PartitionSpec as P

ROWS = 8
PACK = 16
LANES = 128
TILE = 256
MESH = pl.DeviceIdType.MESH
F32 = jnp.float32
BF16 = jnp.bfloat16


def group_kernel(L, H, refs_in, refs_out, s):
    (codes_x, codes_u, dic_hbm, ebias_in, dbias_in, gain_in, gate_hbm, up_hbm, down_hbm) = refs_in
    (out_cols, left, right) = refs_out
    me = lax.axis_index("latent")
    h = lax.axis_index("hidden")
    other = 1 - h
    rows, own_width = codes_x.shape
    width = dic_hbm.shape[1]
    units = dic_hbm.shape[0]
    C = rows // ROWS
    K = C // H
    extra = K - L
    n_dev = L * H
    mine = me * H + h
    high = s.gx.shape[1]
    rest = own_width - LANES
    per = LANES // rest

    def ext(hid):
        return (2 + 3 * hid) % L

    def at(lat, hid):
        return {"latent": lat, "hidden": hid}

    def rcopy(src, dst, ss, rs, lat, hid):
        return pltpu.make_async_remote_copy(
            src_ref=src, dst_ref=dst, send_sem=ss, recv_sem=rs,
            device_id=at(lat, hid), device_id_type=MESH,
        )

    def each(n, body):
        def step(i, carry):
            body(i)
            return carry

        lax.fori_loop(0, n, step, 0)

    def slots(body):
        body(0, me)
        if extra:
            @pl.when(me == ext(h))
            def _():
                body(1, L)

    barrier = pltpu.get_barrier_semaphore()
    for j in range(L):
        for i in range(H):
            if i or j:
                pl.semaphore_signal(
                    barrier, inc=1, device_id=at(lax.rem(me + j, L), lax.rem(h + i, H)), device_id_type=MESH
                )

    loads = []
    for i, (src, dst) in enumerate((
        (codes_x, s.codes_x), (codes_u, s.codes_u), (dic_hbm, s.dic), (ebias_in, s.ebias),
        (dbias_in, s.dbias), (gain_in, s.gain), (down_hbm, s.down), (gate_hbm, s.gate), (up_hbm, s.up),
    )):
        cp = pltpu.make_async_copy(src, dst, s.load_sem.at[i])
        cp.start()
        loads.append(cp)

    def stage(codes, arr):
        value = codes[...].astype(F32) * (2.0 ** (-6))
        shift = lax.rem(mine * own_width, LANES)
        arr[mine, pl.ds(0, rows)] = pltpu.roll(value[:, :LANES], shift, 1).astype(BF16)
        over = jnp.concatenate([value[:, LANES:], jnp.zeros((rows, LANES - rest), F32)], axis=1)
        for b in range(s.gx.shape[1] // PACK - rows // PACK):
            packed = None
            for g in range(b * per, min((b + 1) * per, rows // PACK)):
                part = over[g * PACK : (g + 1) * PACK]
                part = pltpu.roll(part, (g % per) * rest, 1) if g % per else part
                packed = part if packed is None else packed + part
            arr[mine, pl.ds(rows + b * PACK, PACK)] = packed.astype(BF16)

    X = 2
    Z = L // X
    z, x = me // X, lax.rem(me, X)
    across_me = z * X + 1 - x
    near_z, same_z, flip_z = z + 1 - 2 * lax.rem(z, 2), z + 2 - 4 * (z // 2), 3 - z
    peers = (near_z, same_z, flip_z)
    far = (same_z, flip_z, near_z)

    def col(zz):
        return zz * X + x

    def beside(zz):
        return zz * X + 1 - x

    ext_z = ext(h) // X
    ext_here = lax.rem(ext(h), X) == x
    ext_mine = me == ext(h)
    ext_passes = jnp.logical_and(ext_here, jnp.logical_not(ext_mine))

    def when_extra(cond, body):
        if extra:
            @pl.when(cond)
            def _():
                body(L, Z)

    def wait_here(buf, sem):
        rcopy(buf, buf, sem, sem, me, other).wait_recv()

    def wait_sent(buf, sem):
        rcopy(buf, buf, sem, sem, me, other).wait_send()

    def cols_send(arr, a, i, lat):
        rcopy(arr.at[i], arr.at[i], s.col_ss.at[a], s.col_rs.at[a, i // H], lat, h).start()

    def cols_give(arr, a, i):
        rcopy(arr.at[i], arr.at[i], s.col_fs.at[a], s.col_fr.at[a], me, other).start()

    def cols_got(arr, a, lat, relay=False):
        i = lat * H + h
        wait_here(arr.at[i], s.col_rs.at[a, lat])
        if relay:
            cols_send(arr, a, i, across_me)
        cols_give(arr, a, i)

    def cols_start(arr, a):
        for zz in far:
            for lat in (beside(zz), col(zz)):
                cols_send(arr, a, mine, lat)
        cols_send(arr, a, mine, across_me)
        cols_give(arr, a, mine)

    def cols_relay(arr, a):
        cols_got(arr, a, across_me)
        for zz in peers:
            cols_got(arr, a, col(zz))
            cols_got(arr, a, beside(zz))

    def cols_lean_start(arr, a):
        for zz in far:
            cols_send(arr, a, mine, col(zz))
        cols_send(arr, a, mine, across_me)
        cols_give(arr, a, mine)

    def cols_lean_column(arr, a):
        for zz in peers:
            cols_got(arr, a, col(zz), True)

    def cols_lean_across(arr, a):
        cols_got(arr, a, across_me)
        for zz in peers:
            cols_got(arr, a, beside(zz))

    def cols_take(arr, a):
        wait_here(arr.at[pl.ds(0, L)], s.col_fr.at[a])

    def cols_drain(arr, a):
        wait_sent(arr.at[pl.ds(0, L - 1)], s.col_ss.at[a])
        wait_sent(arr.at[pl.ds(0, L)], s.col_fs.at[a])

    def cols_rows(arr, put):
        lane = lax.broadcasted_iota(jnp.int32, (rows, LANES), 1)

        def main(i):
            return arr[i, pl.ds(0, rows)].astype(F32)

        def over(i):
            block = arr[i, pl.ds(rows, s.gx.shape[1] - rows)].astype(F32)
            parts = []
            for g in range(rows // PACK):
                b = g // per
                move = (i * own_width - (g % per) * rest) % LANES
                part = block[b * PACK : (b + 1) * PACK]
                parts.append(pltpu.roll(part, move, 1) if move else part)
            return jnp.concatenate(parts, axis=0)

        for t in range(width // LANES):
            value = None
            for i in range(n_dev):
                first, offset = divmod(i * own_width, LANES)
                if first == t:
                    new = main(i)
                    value = new if value is None else jnp.where(lane >= offset, new, value)
                elif first == t - 1:
                    value = over(i)
                    if offset:
                        value = jnp.where(lane >= offset, value, main(i))
            put(t, value)

    def hand_over(full, a, k):
        c = h * K + k
        rcopy(full.at[c], full.at[c], s.ag_fs.at[a], s.ag_fr.at[a], me, other).start()

    def step_across(full, a, k, i):
        c = h * K + k
        rcopy(full.at[c], full.at[c], s.ag_xs.at[a], s.ag_xr.at[a, i], across_me, h).start()

    def spread_start(full, a):
        def one(slot, k):
            c = h * K + k
            i = Z if slot else z
            for zz in far:
                rcopy(full.at[c], full.at[c], s.ag_ss.at[a, slot], s.ag_rr.at[a, i], col(zz), h).start()
            step_across(full, a, k, i)
            hand_over(full, a, k)

        slots(one)

    def relay_column(full, a, k, i):
        wait_here(full.at[h * K + k], s.ag_rr.at[a, i])
        step_across(full, a, k, i)
        hand_over(full, a, k)

    def relay_across(full, a, k, i):
        wait_here(full.at[h * K + k], s.ag_xr.at[a, i])
        hand_over(full, a, k)

    def spread_column(full, a):
        for zz in peers:
            relay_column(full, a, col(zz), zz)
        when_extra(ext_passes, lambda k, i: relay_column(full, a, k, i))

    def spread_across(full, a):
        relay_across(full, a, across_me, z)
        for zz in peers:
            relay_across(full, a, beside(zz), zz)
        when_extra(jnp.logical_not(ext_here), lambda k, i: relay_across(full, a, k, i))

    def spread_take(full, a):
        wait_here(full.at[pl.ds(other * K, K)], s.ag_fr.at[a])

    def either(cond, body, no, yes):
        @pl.when(cond)
        def _():
            body(yes)

        @pl.when(jnp.logical_not(cond))
        def _():
            body(no)

    def spread_drain(full, a):
        slots(lambda slot, k: wait_sent(full.at[pl.ds(0, Z - 1)], s.ag_ss.at[a, slot]))
        either(ext_here, lambda n: wait_sent(full.at[pl.ds(0, n)], s.ag_xs.at[a]), Z, Z + 1)
        wait_sent(full.at[pl.ds(0, K)], s.ag_fs.at[a])

    def rows_of(full, dst):
        dst[...] = full[...].astype(F32).reshape(rows, width).astype(BF16)

    def sum_tile(a, t, value):
        cols = pl.ds(t * wide, wide)
        s.own[a, :, :, cols] = value.reshape(C, ROWS, wide)
        rcopy(
            s.own.at[a, pl.ds(other * K, K), :, cols], s.sib.at[a, :, :, cols],
            s.rs_cs.at[a], s.rs_cr.at[a], me, other,
        ).start()

    wide = 3 * TILE if width % (3 * TILE) == 0 else LANES
    n_wide = width // wide

    def sum_start(a):
        wait_here(s.sib.at[a], s.rs_cr.at[a])

    def sum_chip(a, k):
        return s.own[a, h * K + k] + s.sib[a, k]

    def sum_middle(a):
        def leave(k, i):
            s.comb[a, k] = sum_chip(a, k).astype(BF16)
            rcopy(s.comb.at[a, k], s.xbuf.at[a, k], s.rs_xs.at[a], s.rs_xr.at[a, i], across_me, h).start()

        for zz in far:
            leave(beside(zz), zz)
        when_extra(jnp.logical_not(ext_here), leave)
        leave(across_me, z)

    def sum_cross(a):
        def total(k, i):
            value = sum_chip(a, k)
            wait_here(s.xbuf.at[a, k], s.rs_xr.at[a, i])
            return value + s.xbuf[a, k].astype(F32)

        def leave(slot, k, i, owner):
            s.comb[a, k] = total(k, i).astype(BF16)
            rcopy(s.comb.at[a, k], s.rbuf.at[a, slot, z], s.rs_ss.at[a], s.rs_rr.at[a, slot], owner, h).start()

        for zz in far:
            leave(0, col(zz), zz, col(zz))
        when_extra(ext_passes, lambda k, i: leave(1, k, i, ext(h)))
        s.acc[a, 0] = total(me, z)

        def keep(k, i):
            s.acc[a, 1] = total(k, i)

        when_extra(ext_mine, keep)

    def sum_value(a, slot):
        value = s.acc[a, slot]
        wait_here(s.rbuf.at[a, slot, pl.ds(0, Z - 1)], s.rs_rr.at[a, slot])
        for zz in peers:
            value = value + s.rbuf[a, slot, zz].astype(F32)
        return value

    def sum_drain(a):
        wait_sent(s.sib.at[a], s.rs_cs.at[a])
        either(jnp.logical_not(ext_here), lambda n: wait_sent(s.xbuf.at[a, pl.ds(0, n)], s.rs_xs.at[a]), Z, Z + 1)
        either(ext_passes, lambda n: wait_sent(s.xbuf.at[a, pl.ds(0, n)], s.rs_ss.at[a]), Z - 1, Z)

    def out_tile(t, value):
        s.wide_out[:, t * wide : (t + 1) * wide] = value

    def out_pieces():
        lane = lax.broadcasted_iota(jnp.int32, (rows, LANES), 1)
        group = lax.broadcasted_iota(jnp.int32, (PACK, LANES), 1) // rest
        for i in range(n_dev):
            first, offset = divmod(i * own_width, LANES)
            here = s.wide_out[:, first * LANES : (first + 1) * LANES]
            there = s.wide_out[:, (first + 1) * LANES : (first + 2) * LANES]
            piece = s.own_out.at[i % H, i // H]
            piece[pl.ds(0, rows)] = jnp.where(lane >= offset, here, there) if offset else here
            for b in range(high // PACK - rows // PACK):
                packed = jnp.zeros((PACK, LANES), F32)
                for g in range(b * per, min((b + 1) * per, rows // PACK)):
                    part = there[g * PACK : (g + 1) * PACK]
                    move = ((g % per) * rest - offset) % LANES
                    part = pltpu.roll(part, move, 1) if move else part
                    packed = jnp.where(group == g % per, part, packed)
                piece[pl.ds(rows + b * PACK, PACK)] = packed
        rcopy(s.own_out.at[other], s.sib_out, s.out_cs.at[0], s.out_cr.at[0], me, other).start()

    def out_chip(lat):
        return s.own_out[h, lat] + s.sib_out[lat]

    def out_middle():
        wait_here(s.sib_out, s.out_cr.at[0])
        for lat, i in [(beside(zz), zz) for zz in far] + [(across_me, z)]:
            s.comb_out[lat] = out_chip(lat).astype(BF16)
            rcopy(s.comb_out.at[lat], s.xbuf_out.at[lat], s.out_xs.at[0], s.out_xr.at[i], across_me, h).start()

    def out_total(lat, i):
        wait_here(s.xbuf_out.at[lat], s.out_xr.at[i])
        return out_chip(lat) + s.xbuf_out[lat].astype(F32)

    def out_cross():
        for zz in far:
            lat = col(zz)
            s.comb_out[lat] = out_total(lat, zz).astype(BF16)
            rcopy(s.comb_out.at[lat], s.rbuf_out.at[z], s.out_ss.at[0], s.out_rr.at[0], lat, h).start()
        s.acc_out[...] = out_total(me, z)

    def out_final():
        wait_here(s.rbuf_out.at[pl.ds(0, Z - 1)], s.out_rr.at[0])
        value = s.acc_out[...]
        for zz in peers:
            value = value + s.rbuf_out[zz].astype(F32)
        back_by = lax.rem(LANES - lax.rem(mine * own_width, LANES), LANES)
        out_cols[:, :LANES] = pltpu.roll(value[:rows], back_by, 1).astype(BF16)
        parts = []
        for g in range(rows // PACK):
            part = value[rows + (g // per) * PACK : rows + (g // per + 1) * PACK]
            move = (-(g % per) * rest) % LANES
            parts.append(pltpu.roll(part, move, 1) if move else part)
        out_cols[:, LANES:] = jnp.concatenate(parts, axis=0)[:, :rest].astype(BF16)

    def out_drain():
        wait_sent(s.sib_out, s.out_cs.at[0])
        wait_sent(s.xbuf_out.at[pl.ds(0, Z)], s.out_xs.at[0])
        wait_sent(s.xbuf_out.at[pl.ds(0, Z - 1)], s.out_ss.at[0])

    across = (((1,), (1,)), ((), ()))

    def mm_t(x, w):
        return lax.dot_general(x, w, across, preferred_element_type=F32)

    def mm(x, w):
        return lax.dot_general(x, w, (((1,), (0,)), ((), ())), preferred_element_type=F32)

    deep = TILE if units % TILE == 0 else units
    n_deep = units // deep

    loads[0].wait()
    stage(s.codes_x, s.gx)
    pl.semaphore_wait(barrier, n_dev - 1)
    cols_start(s.gx, 0)
    loads[1].wait()
    stage(s.codes_u, s.gu)
    cols_relay(s.gx, 0)
    cols_lean_start(s.gu, 1)
    cols_take(s.gx, 0)
    x_rows = right.at[pl.ds(rows, rows)]
    r_rows = right.at[pl.ds(0, rows)]

    def put_x(t, value):
        right[pl.ds(rows, rows), t * LANES : (t + 1) * LANES] = value.astype(BF16)
        s.full_x[:, :, t * LANES : (t + 1) * LANES] = value.reshape(C, ROWS, LANES).astype(BF16)

    cols_rows(s.gx, put_x)
    loads[2].wait()
    loads[3].wait()
    for t in range(n_deep):
        cols = pl.ds(t * deep, deep)
        pre = mm_t(x_rows[...], s.dic[cols, :]) + s.ebias[:, cols]
        s.pre[:, cols] = pre
        left[pl.ds(0, rows), cols] = jnp.maximum(pre, 0.0).astype(BF16)
    for t in range(n_wide):
        sum_tile(0, t, mm(left[pl.ds(0, rows), :], s.dic[:, t * wide : (t + 1) * wide]))
    sum_start(0)
    sum_middle(0)
    sum_cross(0)
    cols_lean_column(s.gu, 1)

    def put_u(t, value):
        s.u_rows[:, t * LANES : (t + 1) * LANES] = value.astype(BF16)

    loads[4].wait()
    loads[5].wait()

    def norm(slot, k):
        rebuilt = sum_value(0, slot) + s.dbias[...]
        inverse = lax.rsqrt(jnp.sum(rebuilt * rebuilt, axis=1, keepdims=True) / width + 1e-06)
        s.rebuilt[slot] = rebuilt
        s.inverse[slot] = jnp.broadcast_to(inverse, (ROWS, LANES))
        s.full_n[h * K + k] = (rebuilt * inverse * s.gain[...]).astype(BF16)

    slots(norm)
    spread_start(s.full_n, 0)
    cols_lean_across(s.gu, 1)
    cols_take(s.gu, 1)
    cols_rows(s.gu, put_u)
    loads[6].wait()
    for t in range(n_deep):
        cols = pl.ds(t * deep, deep)
        s.hgrad[:, cols] = mm_t(s.u_rows[...], s.down[cols, :])
    loads[7].wait()
    loads[8].wait()
    spread_column(s.full_n, 0)
    spread_across(s.full_n, 0)
    spread_take(s.full_n, 0)
    rows_of(s.full_n, s.n_rows)
    for t in range(n_deep):
        cols = pl.ds(t * deep, deep)
        g = mm_t(s.n_rows[...], s.gate[cols, :])
        u = mm_t(s.n_rows[...], s.up[cols, :])
        th = jnp.tanh(0.7978845608028654 * (g + 0.044715 * g * g * g))
        value = 0.5 * g * (1.0 + th)
        slope = 0.5 * (1.0 + th) + 0.5 * g * (1.0 - th * th) * 0.7978845608028654 * (
            1.0 + 3.0 * 0.044715 * g * g
        )
        hg = s.hgrad[:, cols]
        s.hid[:, cols] = (value * u).astype(BF16)
        s.ggrad[:, cols] = (hg * u * slope).astype(BF16)
        s.ugrad[:, cols] = (hg * value).astype(BF16)
    for t in range(n_wide):
        cols = slice(t * wide, (t + 1) * wide)
        sum_tile(1, t, mm(s.ggrad[...], s.gate[:, cols]) + mm(s.ugrad[...], s.up[:, cols]))
    sum_start(1)
    sum_middle(1)
    for t in range(n_wide):
        out_tile(t, mm(s.hid[...], s.down[:, t * wide : (t + 1) * wide]))
    sum_cross(1)
    out_pieces()
    out_middle()

    def back(slot, k):
        scaled = sum_value(1, slot) * s.gain[...]
        rebuilt = s.rebuilt[slot]
        inverse = s.inverse[slot][:, :1]
        inner = jnp.sum(scaled * rebuilt, axis=1, keepdims=True)
        target = s.full_x[h * K + k].astype(F32)
        s.full_r[h * K + k] = (
            inverse * scaled - inverse * inverse * inverse * rebuilt * (inner / width) + (rebuilt - target)
        ).astype(BF16)

    slots(back)
    spread_start(s.full_r, 1)
    spread_column(s.full_r, 1)
    out_cross()
    spread_across(s.full_r, 1)
    spread_take(s.full_r, 1)
    rows_of(s.full_r, r_rows)
    for t in range(n_deep):
        cols = pl.ds(t * deep, deep)
        grad = mm_t(r_rows[...], s.dic[cols, :])
        left[pl.ds(rows, rows), cols] = jnp.where(s.pre[:, cols] > 0.0, grad, 0.0).astype(BF16)

    out_final()
    for a, arr in enumerate((s.gx, s.gu)):
        cols_drain(arr, a)
    for a, full in enumerate((s.full_n, s.full_r)):
        spread_drain(full, a)
    for a in range(2):
        sum_drain(a)
    out_drain()


def run_group(L, H, *args):
    codes, dic = args[0], args[2]
    rows, own_width = codes.shape
    units, width = dic.shape
    C = rows // ROWS
    K = C // H
    Z = L // 2
    n_dev = L * H
    per = LANES // (own_width - LANES)
    high = rows + PACK * -(-(rows // PACK) // per)
    V, D, R = pltpu.VMEM, pltpu.SemaphoreType.DMA, ROWS
    scratch = dict(
        codes_x=V((rows, own_width), jnp.int32), codes_u=V((rows, own_width), jnp.int32),
        ebias=V((1, units), F32), dbias=V((width,), F32), gain=V((width,), F32),
        dic=V((units, width), BF16), gate=V((units, width), BF16),
        up=V((units, width), BF16), down=V((units, width), BF16),
        gx=V((n_dev, high, LANES), BF16), gu=V((n_dev, high, LANES), BF16),
        full_x=V((C, R, width), BF16), full_n=V((C, R, width), BF16), full_r=V((C, R, width), BF16),
        u_rows=V((rows, width), BF16), n_rows=V((rows, width), BF16),
        pre=V((rows, units), F32), hgrad=V((rows, units), F32), hid=V((rows, units), BF16),
        ggrad=V((rows, units), BF16), ugrad=V((rows, units), BF16),
        own=V((2, C, R, width), F32), xbuf=V((2, K, R, width), BF16),
        sib=V((2, K, R, width), F32), comb=V((2, K, R, width), BF16),
        rbuf=V((2, 2, Z, R, width), BF16), acc=V((2, 2, R, width), F32),
        rebuilt=V((2, R, width), F32), inverse=V((2, R, LANES), F32),
        wide_out=V((rows, width), F32), own_out=V((H, L, high, LANES), F32), sib_out=V((L, high, LANES), F32),
        comb_out=V((L, high, LANES), BF16), xbuf_out=V((L, high, LANES), BF16),
        rbuf_out=V((Z, high, LANES), BF16), acc_out=V((high, LANES), F32),
        load_sem=D((9,)),
        col_ss=D((2,)), col_rs=D((2, L)), col_fs=D((2,)), col_fr=D((2,)),
        ag_ss=D((2, 2)), ag_xs=D((2,)), ag_xr=D((2, Z + 1)), ag_rr=D((2, Z + 1)), ag_fs=D((2,)), ag_fr=D((2,)),
        rs_cs=D((2,)), rs_cr=D((2,)), rs_ss=D((2,)), rs_rr=D((2, 2)), rs_xs=D((2,)), rs_xr=D((2, Z + 1)),
        out_cs=D((1,)), out_cr=D((1,)), out_xs=D((1,)), out_xr=D((Z,)), out_ss=D((1,)), out_rr=D((1,)),
    )
    names = list(scratch)

    def body(*refs):
        group_kernel(L, H, refs[:9], refs[9:12], types.SimpleNamespace(**dict(zip(names, refs[12:]))))

    hbm = pl.BlockSpec(memory_space=pltpu.HBM)
    vm = pl.BlockSpec(memory_space=pltpu.VMEM)
    cols, left, right = pl.pallas_call(
        body,
        name="group_step",
        out_shape=(
            V((rows, own_width), BF16),
            V((2 * rows, units), BF16),
            V((2 * rows, width), BF16),
        ),
        in_specs=[hbm] * 9,
        out_specs=(vm, vm, vm),
        scratch_shapes=[scratch[n] for n in names],
        compiler_params=pltpu.CompilerParams(collective_id=0, has_side_effects=True, vmem_limit_bytes=60 * 2**20),
    )(*args)

    step = width // 6 if width % (6 * LANES) == 0 else LANES
    n_step = width // step

    def product(cols, left, right, block, grad, tiles, sem):
        copies = []
        for t in range(n_step):
            at = slice(t * step, (t + 1) * step)
            tiles[t] = lax.dot_general(
                left[...], right[:, at], (((0,), (0,)), ((), ())), preferred_element_type=F32
            ).astype(BF16)
            copies.append(pltpu.make_async_copy(tiles.at[t], grad.at[:, at], sem.at[t]))
            copies[-1].start()
        block[...] = cols[...]
        for cp in copies:
            cp.wait()

    return pl.pallas_call(
        product,
        name="dictionary_product",
        out_shape=(
            jax.ShapeDtypeStruct((rows, own_width), BF16),
            jax.ShapeDtypeStruct((units, width), BF16),
        ),
        in_specs=[vm, vm, vm],
        out_specs=(vm, pl.BlockSpec(memory_space=pl.ANY)),
        scratch_shapes=[V((n_step, units, step), BF16), D((n_step,))],
        compiler_params=pltpu.CompilerParams(vmem_limit_bytes=16 * 2**20),
    )(cols, left, right)


def fits(L, H, rows, own_width, width, units, units_mlp):
    rest = own_width - LANES
    if H != 2 or rows % (ROWS * H) or rows % PACK or width % LANES or units % LANES or units != units_mlp:
        return False
    if rest <= 0 or rest >= LANES or LANES % rest or own_width * L * H != width:
        return False
    return L == 8 and rows // ROWS // H == L + 1


CODE_STEP = 2.0 ** (-6)
NORM_EPSILON = 1e-06
GELU_ROOT = 0.7978845608028654
GELU_CUBIC = 0.044715
ACROSS = (((1,), (1,)), ((), ()))
DOWNWARD = (((0,), (0,)), ((), ()))


def gelu_parts(values):
    argument = GELU_ROOT * (values + GELU_CUBIC * values * values * values)
    tanh_value = jnp.tanh(argument)
    result = 0.5 * values * (1.0 + tanh_value)
    derivative = 0.5 * (1.0 + tanh_value) + 0.5 * values * (
        1.0 - tanh_value * tanh_value
    ) * GELU_ROOT * (1.0 + 3.0 * GELU_CUBIC * values * values)
    return (result, derivative)


def per_device(
    input_codes,
    cotangent_codes,
    dictionary,
    encoder_bias,
    decoder_bias,
    norm_gain,
    gate_weight,
    up_weight,
    down_weight,
):
    L, H = lax.axis_size("latent"), lax.axis_size("hidden")
    rows, width = input_codes.shape[0], dictionary.shape[1]
    if fits(L, H, rows, input_codes.shape[1], width, dictionary.shape[0], gate_weight.shape[0]):
        return run_group(
            L, H, input_codes, cotangent_codes, dictionary, encoder_bias[None, :], decoder_bias,
            norm_gain, gate_weight, up_weight, down_weight,
        )
    own_width = input_codes.shape[1]
    model_width = own_width * lax.axis_size(("latent", "hidden"))
    cotangent_local = (cotangent_codes.astype(jnp.float32) * CODE_STEP).astype(jnp.bfloat16)
    hidden_grad = None
    inputs_local = (input_codes.astype(jnp.float32) * CODE_STEP).astype(jnp.bfloat16)
    inputs = lax.all_gather(inputs_local, ("latent", "hidden"), axis=1, tiled=True)
    preact = (
        lax.dot_general(inputs, dictionary, ACROSS, preferred_element_type=jnp.float32)
        + encoder_bias
    )
    latents = jnp.maximum(preact, 0.0).astype(jnp.bfloat16)
    partial_value = jnp.dot(latents, dictionary, preferred_element_type=jnp.float32)
    rebuilt = lax.psum(partial_value, ("latent", "hidden")) + decoder_bias
    inverse = lax.rsqrt(
        jnp.sum(rebuilt * rebuilt, axis=1, keepdims=True) / model_width + NORM_EPSILON
    )
    normed = (rebuilt * inverse * norm_gain).astype(jnp.bfloat16)
    target = inputs.astype(jnp.float32)
    gate_proj = lax.dot_general(normed, gate_weight, ACROSS, preferred_element_type=jnp.float32)
    up_proj = lax.dot_general(normed, up_weight, ACROSS, preferred_element_type=jnp.float32)
    gelu_value, gelu_slope = gelu_parts(gate_proj)
    hidden = (gelu_value * up_proj).astype(jnp.bfloat16)
    output_terms = jnp.dot(hidden, down_weight, preferred_element_type=jnp.float32)
    block_output = lax.psum_scatter(
        output_terms, ("latent", "hidden"), scatter_dimension=1, tiled=True
    ).astype(jnp.bfloat16)
    hidden_grad = lax.dot_general(
        lax.all_gather(cotangent_local, ("latent", "hidden"), axis=1, tiled=True),
        down_weight,
        ACROSS,
        preferred_element_type=jnp.float32,
    )
    gate_grad = (hidden_grad * up_proj * gelu_slope).astype(jnp.bfloat16)
    up_grad = (hidden_grad * gelu_value).astype(jnp.bfloat16)
    partial_grad = jnp.dot(gate_grad, gate_weight, preferred_element_type=jnp.float32) + jnp.dot(
        up_grad, up_weight, preferred_element_type=jnp.float32
    )
    scaled = lax.psum(partial_grad, ("latent", "hidden")) * norm_gain
    inner_row = jnp.sum(scaled * rebuilt, axis=1, keepdims=True)
    inverse_cube = inverse * inverse * inverse
    rebuilt_grad = (
        inverse * scaled - inverse_cube * rebuilt * (inner_row / model_width) + (rebuilt - target)
    ).astype(jnp.bfloat16)
    latent_grad = lax.dot_general(
        rebuilt_grad, dictionary, ACROSS, preferred_element_type=jnp.float32
    )
    preact_grad = jnp.where(preact > 0.0, latent_grad, 0.0).astype(jnp.bfloat16)
    dictionary_grad = lax.dot_general(
        latents, rebuilt_grad, DOWNWARD, preferred_element_type=jnp.float32
    ) + lax.dot_general(preact_grad, inputs, DOWNWARD, preferred_element_type=jnp.float32)
    return (block_output, dictionary_grad.astype(jnp.bfloat16))


def solution(mesh):
    in_specs = (
        P("groups", ("latent", "hidden")),
        P("groups", ("latent", "hidden")),
        P(("latent", "hidden"), None),
        P(("latent", "hidden")),
        P(),
        P(),
        P(("latent", "hidden"), None),
        P(("latent", "hidden"), None),
        P(("latent", "hidden"), None),
    )
    out_specs = (P("groups", ("latent", "hidden")), P(("latent", "hidden"), "groups"))
    return jax.shard_map(
        per_device, mesh=mesh, in_specs=in_specs, out_specs=out_specs, check_vma=False
    )
```

```python
import types

import jax
import jax.numpy as jnp
from jax import lax
from jax.experimental import pallas as pl
from jax.experimental.pallas import tpu as pltpu
from jax.sharding import PartitionSpec as P

ROWS = 8
PACK = 16
PARTS = 1
LANES = 128
TILE = 256
MESH = pl.DeviceIdType.MESH
F32 = jnp.float32
BF16 = jnp.bfloat16


def group_kernel(L, H, refs_in, refs_out, s):
    (codes_x, codes_u, dic_hbm, ebias_in, dbias_in, gain_in, gate_hbm, up_hbm, down_hbm) = refs_in
    (out_cols, left, right) = refs_out
    me = lax.axis_index("latent")
    h = lax.axis_index("hidden")
    other = 1 - h
    rows, own_width = codes_x.shape
    width = dic_hbm.shape[1]
    units = dic_hbm.shape[0]
    C = rows // ROWS
    K = C // H
    extra = K - L
    n_dev = L * H
    mine = me * H + h
    high = s.gx.shape[1]
    rest = own_width - LANES
    per = LANES // rest

    def ext(hid):
        return (2 + 3 * hid) % L

    def at(lat, hid):
        return {"latent": lat, "hidden": hid}

    def rcopy(src, dst, ss, rs, lat, hid):
        return pltpu.make_async_remote_copy(
            src_ref=src, dst_ref=dst, send_sem=ss, recv_sem=rs,
            device_id=at(lat, hid), device_id_type=MESH,
        )

    def each(n, body):
        def step(i, carry):
            body(i)
            return carry

        lax.fori_loop(0, n, step, 0)

    def slots(body):
        body(0, me)
        if extra:
            @pl.when(me == ext(h))
            def _():
                body(1, L)

    barrier = pltpu.get_barrier_semaphore()
    for j in range(L):
        for i in range(H):
            if i or j:
                pl.semaphore_signal(
                    barrier, inc=1, device_id=at(lax.rem(me + j, L), lax.rem(h + i, H)), device_id_type=MESH
                )

    loads = []
    for i, (src, dst) in enumerate((
        (codes_x, s.codes_x), (codes_u, s.codes_u), (dic_hbm, s.dic), (ebias_in, s.ebias),
        (dbias_in, s.dbias), (gain_in, s.gain), (down_hbm, s.down), (gate_hbm, s.gate), (up_hbm, s.up),
    )):
        cp = pltpu.make_async_copy(src, dst, s.load_sem.at[i])
        cp.start()
        loads.append(cp)

    def stage(codes, arr):
        value = codes[...].astype(F32) * (2.0 ** (-6))
        shift = lax.rem(mine * own_width, LANES)
        arr[mine, pl.ds(0, rows)] = pltpu.roll(value[:, :LANES], shift, 1).astype(BF16)
        over = jnp.concatenate([value[:, LANES:], jnp.zeros((rows, LANES - rest), F32)], axis=1)
        for b in range(s.gx.shape[1] // PACK - rows // PACK):
            packed = None
            for g in range(b * per, min((b + 1) * per, rows // PACK)):
                part = over[g * PACK : (g + 1) * PACK]
                part = pltpu.roll(part, (g % per) * rest, 1) if g % per else part
                packed = part if packed is None else packed + part
            arr[mine, pl.ds(rows + b * PACK, PACK)] = packed.astype(BF16)

    X = 2
    Z = L // X
    z, x = me // X, lax.rem(me, X)
    across_me = z * X + 1 - x
    near_z, same_z, flip_z = z + 1 - 2 * lax.rem(z, 2), z + 2 - 4 * (z // 2), 3 - z
    peers = (near_z, same_z, flip_z)
    far = (same_z, flip_z, near_z)

    def col(zz):
        return zz * X + x

    def beside(zz):
        return zz * X + 1 - x

    ext_z = ext(h) // X
    ext_here = lax.rem(ext(h), X) == x
    ext_mine = me == ext(h)
    ext_passes = jnp.logical_and(ext_here, jnp.logical_not(ext_mine))

    def when_extra(cond, body):
        if extra:
            @pl.when(cond)
            def _():
                body(L, Z)

    def wait_here(buf, sem):
        rcopy(buf, buf, sem, sem, me, other).wait_recv()

    def wait_sent(buf, sem):
        rcopy(buf, buf, sem, sem, me, other).wait_send()

    def cols_send(arr, a, i, lat):
        rcopy(arr.at[i], arr.at[i], s.col_ss.at[a], s.col_rs.at[a, i // H], lat, h).start()

    def cols_give(arr, a, i):
        rcopy(arr.at[i], arr.at[i], s.col_fs.at[a], s.col_fr.at[a], me, other).start()

    def cols_got(arr, a, lat, relay=False):
        i = lat * H + h
        wait_here(arr.at[i], s.col_rs.at[a, lat])
        if relay:
            cols_send(arr, a, i, across_me)
        cols_give(arr, a, i)

    def cols_start(arr, a):
        for zz in far:
            cols_send(arr, a, mine, col(zz))
        cols_send(arr, a, mine, across_me)
        cols_give(arr, a, mine)

    def cols_column(arr, a):
        for zz in peers:
            cols_got(arr, a, col(zz), True)

    def cols_across(arr, a):
        cols_got(arr, a, across_me)
        for zz in peers:
            cols_got(arr, a, beside(zz))

    def cols_take(arr, a):
        wait_here(arr.at[pl.ds(0, L)], s.col_fr.at[a])

    def cols_drain(arr, a):
        wait_sent(arr.at[pl.ds(0, L - 1)], s.col_ss.at[a])
        wait_sent(arr.at[pl.ds(0, L)], s.col_fs.at[a])

    def cols_rows(arr, put):
        lane = lax.broadcasted_iota(jnp.int32, (rows, LANES), 1)

        def main(i):
            return arr[i, pl.ds(0, rows)].astype(F32)

        def over(i):
            block = arr[i, pl.ds(rows, s.gx.shape[1] - rows)].astype(F32)
            parts = []
            for g in range(rows // PACK):
                b = g // per
                move = (i * own_width - (g % per) * rest) % LANES
                part = block[b * PACK : (b + 1) * PACK]
                parts.append(pltpu.roll(part, move, 1) if move else part)
            return jnp.concatenate(parts, axis=0)

        for t in range(width // LANES):
            value = None
            for i in range(n_dev):
                first, offset = divmod(i * own_width, LANES)
                if first == t:
                    new = main(i)
                    value = new if value is None else jnp.where(lane >= offset, new, value)
                elif first == t - 1:
                    value = over(i)
                    if offset:
                        value = jnp.where(lane >= offset, value, main(i))
            put(t, value)

    part_width = width // PARTS

    def part(full, c, p):
        return full.at[c, :, pl.ds(p * part_width, part_width)]

    def hand_over(full, a, k, p):
        piece = part(full, h * K + k, p)
        rcopy(piece, piece, s.ag_fs.at[a], s.ag_fr.at[a, p], me, other).start()

    def step_across(full, a, k, i, p):
        piece = part(full, h * K + k, p)
        rcopy(piece, piece, s.ag_xs.at[a], s.ag_xr.at[a, i, p], across_me, h).start()

    def spread_start(full, a, ready=None):
        def one(slot, k):
            if ready is not None:
                ready(slot, k)
            c = h * K + k
            i = Z if slot else z
            for p in range(PARTS):
                piece = part(full, c, p)
                for zz in far:
                    rcopy(piece, piece, s.ag_ss.at[a, slot], s.ag_rr.at[a, i, p], col(zz), h).start()
                step_across(full, a, k, i, p)
                hand_over(full, a, k, p)

        slots(one)

    def relay_column(full, a, k, i, p):
        wait_here(part(full, h * K + k, p), s.ag_rr.at[a, i, p])
        step_across(full, a, k, i, p)
        hand_over(full, a, k, p)

    def relay_across(full, a, k, i, p):
        wait_here(part(full, h * K + k, p), s.ag_xr.at[a, i, p])
        hand_over(full, a, k, p)

    def spread_column(full, a):
        for p in range(PARTS):
            for zz in peers:
                relay_column(full, a, col(zz), zz, p)
            when_extra(ext_passes, lambda k, i: relay_column(full, a, k, i, p))

    def spread_across(full, a, p):
        relay_across(full, a, across_me, z, p)
        for zz in peers:
            relay_across(full, a, beside(zz), zz, p)
        when_extra(jnp.logical_not(ext_here), lambda k, i: relay_across(full, a, k, i, p))

    def spread_take(full, a, p):
        wait_here(full.at[pl.ds(other * K, K), :, pl.ds(p * part_width, part_width)], s.ag_fr.at[a, p])

    def either(cond, body, no, yes):
        @pl.when(cond)
        def _():
            body(yes)

        @pl.when(jnp.logical_not(cond))
        def _():
            body(no)

    def spread_drain(full, a):
        slots(lambda slot, k: wait_sent(full.at[pl.ds(0, Z - 1)], s.ag_ss.at[a, slot]))
        either(ext_here, lambda n: wait_sent(full.at[pl.ds(0, n)], s.ag_xs.at[a]), Z, Z + 1)
        wait_sent(full.at[pl.ds(0, K)], s.ag_fs.at[a])

    def rows_of(full, dst, p):
        at_cols = slice(p * part_width, (p + 1) * part_width)
        dst[:, at_cols] = full[:, :, at_cols].astype(F32).reshape(rows, part_width).astype(BF16)

    def sum_tile(a, t, value):
        cols = pl.ds(t * wide, wide)
        s.own[a, :, :, cols] = value.reshape(C, ROWS, wide)
        rcopy(
            s.own.at[a, pl.ds(other * K, K), :, cols], s.sib.at[a, :, :, cols],
            s.rs_cs.at[a], s.rs_cr.at[a], me, other,
        ).start()

    wide = 3 * TILE if width % (3 * TILE) == 0 else LANES
    n_wide = width // wide

    def sum_start(a):
        wait_here(s.sib.at[a], s.rs_cr.at[a])

    def sum_chip(a, k):
        return s.own[a, h * K + k] + s.sib[a, k]

    def sum_middle(a):
        def leave(k, i):
            s.comb[a, k] = sum_chip(a, k).astype(BF16)
            rcopy(s.comb.at[a, k], s.xbuf.at[a, k], s.rs_xs.at[a], s.rs_xr.at[a, i], across_me, h).start()

        for zz in far:
            leave(beside(zz), zz)
        when_extra(jnp.logical_not(ext_here), leave)
        leave(across_me, z)

    def sum_cross(a):
        def total(k, i):
            value = sum_chip(a, k)
            wait_here(s.xbuf.at[a, k], s.rs_xr.at[a, i])
            return value + s.xbuf[a, k].astype(F32)

        def leave(slot, k, i, owner):
            s.comb[a, k] = total(k, i).astype(BF16)
            rcopy(s.comb.at[a, k], s.rbuf.at[a, slot, z], s.rs_ss.at[a], s.rs_rr.at[a, slot], owner, h).start()

        for zz in far:
            leave(0, col(zz), zz, col(zz))
        when_extra(ext_passes, lambda k, i: leave(1, k, i, ext(h)))
        s.acc[a, 0] = total(me, z)

        def keep(k, i):
            s.acc[a, 1] = total(k, i)

        when_extra(ext_mine, keep)

    def sum_value(a, slot):
        value = s.acc[a, slot]
        wait_here(s.rbuf.at[a, slot, pl.ds(0, Z - 1)], s.rs_rr.at[a, slot])
        for zz in peers:
            value = value + s.rbuf[a, slot, zz].astype(F32)
        return value

    def sum_drain(a):
        wait_sent(s.sib.at[a], s.rs_cs.at[a])
        either(jnp.logical_not(ext_here), lambda n: wait_sent(s.xbuf.at[a, pl.ds(0, n)], s.rs_xs.at[a]), Z, Z + 1)
        either(ext_passes, lambda n: wait_sent(s.xbuf.at[a, pl.ds(0, n)], s.rs_ss.at[a]), Z - 1, Z)

    def out_tile(t, value):
        s.wide_out[:, t * wide : (t + 1) * wide] = value

    def out_pieces():
        lane = lax.broadcasted_iota(jnp.int32, (rows, LANES), 1)
        group = lax.broadcasted_iota(jnp.int32, (PACK, LANES), 1) // rest
        for i in range(n_dev):
            first, offset = divmod(i * own_width, LANES)
            here = s.wide_out[:, first * LANES : (first + 1) * LANES]
            there = s.wide_out[:, (first + 1) * LANES : (first + 2) * LANES]
            piece = s.own_out.at[i % H, i // H]
            piece[pl.ds(0, rows)] = jnp.where(lane >= offset, here, there) if offset else here
            for b in range(high // PACK - rows // PACK):
                packed = jnp.zeros((PACK, LANES), F32)
                for g in range(b * per, min((b + 1) * per, rows // PACK)):
                    part = there[g * PACK : (g + 1) * PACK]
                    move = ((g % per) * rest - offset) % LANES
                    part = pltpu.roll(part, move, 1) if move else part
                    packed = jnp.where(group == g % per, part, packed)
                piece[pl.ds(rows + b * PACK, PACK)] = packed
        rcopy(s.own_out.at[other], s.sib_out, s.out_cs.at[0], s.out_cr.at[0], me, other).start()

    def out_chip(lat):
        return s.own_out[h, lat] + s.sib_out[lat]

    def out_middle():
        wait_here(s.sib_out, s.out_cr.at[0])
        for lat, i in [(beside(zz), zz) for zz in far] + [(across_me, z)]:
            s.comb_out[lat] = out_chip(lat).astype(BF16)
            rcopy(s.comb_out.at[lat], s.xbuf_out.at[lat], s.out_xs.at[0], s.out_xr.at[i], across_me, h).start()

    def out_total(lat, i):
        wait_here(s.xbuf_out.at[lat], s.out_xr.at[i])
        return out_chip(lat) + s.xbuf_out[lat].astype(F32)

    def out_cross():
        for zz in far:
            lat = col(zz)
            s.comb_out[lat] = out_total(lat, zz).astype(BF16)
            rcopy(s.comb_out.at[lat], s.rbuf_out.at[z], s.out_ss.at[0], s.out_rr.at[0], lat, h).start()
        s.acc_out[...] = out_total(me, z)

    def out_final():
        wait_here(s.rbuf_out.at[pl.ds(0, Z - 1)], s.out_rr.at[0])
        value = s.acc_out[...]
        for zz in peers:
            value = value + s.rbuf_out[zz].astype(F32)
        back_by = lax.rem(LANES - lax.rem(mine * own_width, LANES), LANES)
        out_cols[:, :LANES] = pltpu.roll(value[:rows], back_by, 1).astype(BF16)
        parts = []
        for g in range(rows // PACK):
            part = value[rows + (g // per) * PACK : rows + (g // per + 1) * PACK]
            move = (-(g % per) * rest) % LANES
            parts.append(pltpu.roll(part, move, 1) if move else part)
        out_cols[:, LANES:] = jnp.concatenate(parts, axis=0)[:, :rest].astype(BF16)

    def out_drain():
        wait_sent(s.sib_out, s.out_cs.at[0])
        wait_sent(s.xbuf_out.at[pl.ds(0, Z)], s.out_xs.at[0])
        wait_sent(s.xbuf_out.at[pl.ds(0, Z - 1)], s.out_ss.at[0])

    across = (((1,), (1,)), ((), ()))

    def mm_t(x, w):
        return lax.dot_general(x, w, across, preferred_element_type=F32)

    def mm(x, w):
        return lax.dot_general(x, w, (((1,), (0,)), ((), ())), preferred_element_type=F32)

    deep = TILE if units % TILE == 0 else units
    n_deep = units // deep

    def flip(src, dst):
        for t in range(units // LANES):
            at_rows = slice(t * LANES, (t + 1) * LANES)
            dst[:, at_rows] = src[at_rows, :].T

    loads[0].wait()
    stage(s.codes_x, s.gx)
    pl.semaphore_wait(barrier, n_dev - 1)
    cols_start(s.gx, 0)
    loads[1].wait()
    stage(s.codes_u, s.gu)
    loads[2].wait()
    flip(s.dic, s.dic_t)
    cols_column(s.gx, 0)
    cols_across(s.gx, 0)
    cols_start(s.gu, 1)
    cols_take(s.gx, 0)
    x_rows = right.at[pl.ds(rows, rows)]
    r_rows = right.at[pl.ds(0, rows)]

    def put_x(t, value):
        right[pl.ds(rows, rows), t * LANES : (t + 1) * LANES] = value.astype(BF16)
        s.full_x[:, :, t * LANES : (t + 1) * LANES] = value.reshape(C, ROWS, LANES).astype(BF16)

    cols_rows(s.gx, put_x)
    loads[3].wait()
    for t in range(n_deep):
        cols = pl.ds(t * deep, deep)
        pre = mm(x_rows[...], s.dic_t[:, cols]) + s.ebias[:, cols]
        s.pre[:, cols] = pre
        left[pl.ds(0, rows), cols] = jnp.maximum(pre, 0.0).astype(BF16)
    for t in range(n_wide):
        sum_tile(0, t, mm(left[pl.ds(0, rows), :], s.dic[:, t * wide : (t + 1) * wide]))
    sum_start(0)
    sum_middle(0)
    loads[7].wait()
    flip(s.gate, s.gate_t)
    loads[8].wait()
    flip(s.up, s.up_t)
    sum_cross(0)
    cols_column(s.gu, 1)

    def put_u(t, value):
        s.u_rows[:, t * LANES : (t + 1) * LANES] = value.astype(BF16)

    loads[4].wait()
    loads[5].wait()

    def norm(slot, k):
        rebuilt = sum_value(0, slot) + s.dbias[...]
        inverse = lax.rsqrt(jnp.sum(rebuilt * rebuilt, axis=1, keepdims=True) / width + 1e-06)
        s.rebuilt[slot] = rebuilt
        s.inverse[slot] = jnp.broadcast_to(inverse, (ROWS, LANES))
        s.full_n[h * K + k] = (rebuilt * inverse * s.gain[...]).astype(BF16)

    spread_start(s.full_n, 0, norm)
    cols_across(s.gu, 1)
    cols_take(s.gu, 1)
    cols_rows(s.gu, put_u)
    loads[6].wait()
    for t in range(n_deep):
        cols = pl.ds(t * deep, deep)
        s.hgrad[:, cols] = mm_t(s.u_rows[...], s.down[cols, :])
    spread_column(s.full_n, 0)
    for p in range(PARTS):
        spread_across(s.full_n, 0, p)
        spread_take(s.full_n, 0, p)
        rows_of(s.full_n, s.n_rows, p)
        if p < PARTS - 1:
            at_cols = slice(p * part_width, (p + 1) * part_width)
            for t in range(n_deep):
                cols = pl.ds(t * deep, deep)
                g = mm(s.n_rows[:, at_cols], s.gate_t[at_cols, cols])
                u = mm(s.n_rows[:, at_cols], s.up_t[at_cols, cols])
                s.g_sum[:, cols] = g + s.g_sum[:, cols] if p else g
                s.u_sum[:, cols] = u + s.u_sum[:, cols] if p else u
    last = slice((PARTS - 1) * part_width, width)
    for t in range(n_deep):
        cols = pl.ds(t * deep, deep)
        g = mm(s.n_rows[:, last], s.gate_t[last, cols])
        u = mm(s.n_rows[:, last], s.up_t[last, cols])
        if PARTS > 1:
            g = g + s.g_sum[:, cols]
            u = u + s.u_sum[:, cols]
        th = jnp.tanh(0.7978845608028654 * (g + 0.044715 * g * g * g))
        value = 0.5 * g * (1.0 + th)
        slope = 0.5 * (1.0 + th) + 0.5 * g * (1.0 - th * th) * 0.7978845608028654 * (
            1.0 + 3.0 * 0.044715 * g * g
        )
        hg = s.hgrad[:, cols]
        s.hid[:, cols] = (value * u).astype(BF16)
        s.ggrad[:, cols] = (hg * u * slope).astype(BF16)
        s.ugrad[:, cols] = (hg * value).astype(BF16)
    for t in range(n_wide):
        cols = slice(t * wide, (t + 1) * wide)
        sum_tile(1, t, mm(s.ggrad[...], s.gate[:, cols]) + mm(s.ugrad[...], s.up[:, cols]))
    sum_start(1)
    sum_middle(1)
    for t in range(n_wide):
        out_tile(t, mm(s.hid[...], s.down[:, t * wide : (t + 1) * wide]))
    sum_cross(1)
    out_pieces()
    out_middle()

    def back(slot, k):
        scaled = sum_value(1, slot) * s.gain[...]
        rebuilt = s.rebuilt[slot]
        inverse = s.inverse[slot][:, :1]
        inner = jnp.sum(scaled * rebuilt, axis=1, keepdims=True)
        target = s.full_x[h * K + k].astype(F32)
        s.full_r[h * K + k] = (
            inverse * scaled - inverse * inverse * inverse * rebuilt * (inner / width) + (rebuilt - target)
        ).astype(BF16)

    spread_start(s.full_r, 1, back)
    for a, arr in enumerate((s.gx, s.gu)):
        cols_drain(arr, a)
    spread_drain(s.full_n, 0)
    sum_drain(0)
    spread_column(s.full_r, 1)
    out_cross()
    for p in range(PARTS):
        spread_across(s.full_r, 1, p)
        spread_take(s.full_r, 1, p)
        rows_of(s.full_r, r_rows, p)
        if p < PARTS - 1:
            at_cols = slice(p * part_width, (p + 1) * part_width)
            for t in range(n_deep):
                cols = pl.ds(t * deep, deep)
                g = mm(r_rows[:, at_cols], s.dic_t[at_cols, cols])
                s.g_sum[:, cols] = g + s.g_sum[:, cols] if p else g
    for t in range(n_deep):
        cols = pl.ds(t * deep, deep)
        grad = mm(r_rows[:, last], s.dic_t[last, cols])
        if PARTS > 1:
            grad = grad + s.g_sum[:, cols]
        left[pl.ds(rows, rows), cols] = jnp.where(s.pre[:, cols] > 0.0, grad, 0.0).astype(BF16)

    out_final()
    spread_drain(s.full_r, 1)
    sum_drain(1)
    out_drain()


def run_group(L, H, *args):
    codes, dic = args[0], args[2]
    rows, own_width = codes.shape
    units, width = dic.shape
    C = rows // ROWS
    K = C // H
    Z = L // 2
    n_dev = L * H
    per = LANES // (own_width - LANES)
    high = rows + PACK * -(-(rows // PACK) // per)
    V, D, R = pltpu.VMEM, pltpu.SemaphoreType.DMA, ROWS
    scratch = dict(
        codes_x=V((rows, own_width), jnp.int32), codes_u=V((rows, own_width), jnp.int32),
        ebias=V((1, units), F32), dbias=V((width,), F32), gain=V((width,), F32),
        dic=V((units, width), BF16), gate=V((units, width), BF16),
        up=V((units, width), BF16), down=V((units, width), BF16),
        dic_t=V((width, units), BF16), gate_t=V((width, units), BF16), up_t=V((width, units), BF16),
        g_sum=V((rows, units), F32), u_sum=V((rows, units), F32),
        gx=V((n_dev, high, LANES), BF16), gu=V((n_dev, high, LANES), BF16),
        full_x=V((C, R, width), BF16), full_n=V((C, R, width), BF16), full_r=V((C, R, width), BF16),
        u_rows=V((rows, width), BF16), n_rows=V((rows, width), BF16),
        pre=V((rows, units), F32), hgrad=V((rows, units), F32), hid=V((rows, units), BF16),
        ggrad=V((rows, units), BF16), ugrad=V((rows, units), BF16),
        own=V((2, C, R, width), F32), xbuf=V((2, K, R, width), BF16),
        sib=V((2, K, R, width), F32), comb=V((2, K, R, width), BF16),
        rbuf=V((2, 2, Z, R, width), BF16), acc=V((2, 2, R, width), F32),
        rebuilt=V((2, R, width), F32), inverse=V((2, R, LANES), F32),
        wide_out=V((rows, width), F32), own_out=V((H, L, high, LANES), F32), sib_out=V((L, high, LANES), F32),
        comb_out=V((L, high, LANES), BF16), xbuf_out=V((L, high, LANES), BF16),
        rbuf_out=V((Z, high, LANES), BF16), acc_out=V((high, LANES), F32),
        load_sem=D((9,)),
        col_ss=D((2,)), col_rs=D((2, L)), col_fs=D((2,)), col_fr=D((2,)),
        ag_ss=D((2, 2)), ag_xs=D((2,)), ag_xr=D((2, Z + 1, PARTS)), ag_rr=D((2, Z + 1, PARTS)), ag_fs=D((2,)), ag_fr=D((2, PARTS)),
        rs_cs=D((2,)), rs_cr=D((2,)), rs_ss=D((2,)), rs_rr=D((2, 2)), rs_xs=D((2,)), rs_xr=D((2, Z + 1)),
        out_cs=D((1,)), out_cr=D((1,)), out_xs=D((1,)), out_xr=D((Z,)), out_ss=D((1,)), out_rr=D((1,)),
    )
    names = list(scratch)

    def body(*refs):
        group_kernel(L, H, refs[:9], refs[9:12], types.SimpleNamespace(**dict(zip(names, refs[12:]))))

    hbm = pl.BlockSpec(memory_space=pltpu.HBM)
    vm = pl.BlockSpec(memory_space=pltpu.VMEM)
    cols, left, right = pl.pallas_call(
        body,
        name="group_step",
        out_shape=(
            V((rows, own_width), BF16),
            V((2 * rows, units), BF16),
            V((2 * rows, width), BF16),
        ),
        in_specs=[hbm] * 9,
        out_specs=(vm, vm, vm),
        scratch_shapes=[scratch[n] for n in names],
        compiler_params=pltpu.CompilerParams(collective_id=0, has_side_effects=True, vmem_limit_bytes=60 * 2**20),
    )(*args)

    step = width // 6 if width % (6 * LANES) == 0 else LANES
    n_step = width // step

    def product(cols, left, right, block, grad, tiles, sem):
        copies = []
        for t in range(n_step):
            at = slice(t * step, (t + 1) * step)
            tiles[t] = lax.dot_general(
                left[...], right[:, at], (((0,), (0,)), ((), ())), preferred_element_type=F32
            ).astype(BF16)
            copies.append(pltpu.make_async_copy(tiles.at[t], grad.at[:, at], sem.at[t]))
            copies[-1].start()
        block[...] = cols[...]
        for cp in copies:
            cp.wait()

    return pl.pallas_call(
        product,
        name="dictionary_product",
        out_shape=(
            jax.ShapeDtypeStruct((rows, own_width), BF16),
            jax.ShapeDtypeStruct((units, width), BF16),
        ),
        in_specs=[vm, vm, vm],
        out_specs=(vm, pl.BlockSpec(memory_space=pl.ANY)),
        scratch_shapes=[V((n_step, units, step), BF16), D((n_step,))],
        compiler_params=pltpu.CompilerParams(vmem_limit_bytes=16 * 2**20),
    )(cols, left, right)


def fits(L, H, rows, own_width, width, units, units_mlp):
    rest = own_width - LANES
    if H != 2 or rows % (ROWS * H) or rows % PACK or width % LANES or units % LANES or units != units_mlp:
        return False
    if rest <= 0 or rest >= LANES or LANES % rest or own_width * L * H != width or width % (PARTS * LANES):
        return False
    return L == 8 and rows // ROWS // H == L + 1


CODE_STEP = 2.0 ** (-6)
NORM_EPSILON = 1e-06
GELU_ROOT = 0.7978845608028654
GELU_CUBIC = 0.044715
ACROSS = (((1,), (1,)), ((), ()))
DOWNWARD = (((0,), (0,)), ((), ()))


def gelu_parts(values):
    argument = GELU_ROOT * (values + GELU_CUBIC * values * values * values)
    tanh_value = jnp.tanh(argument)
    result = 0.5 * values * (1.0 + tanh_value)
    derivative = 0.5 * (1.0 + tanh_value) + 0.5 * values * (
        1.0 - tanh_value * tanh_value
    ) * GELU_ROOT * (1.0 + 3.0 * GELU_CUBIC * values * values)
    return (result, derivative)


def per_device(
    input_codes,
    cotangent_codes,
    dictionary,
    encoder_bias,
    decoder_bias,
    norm_gain,
    gate_weight,
    up_weight,
    down_weight,
):
    L, H = lax.axis_size("latent"), lax.axis_size("hidden")
    rows, width = input_codes.shape[0], dictionary.shape[1]
    if fits(L, H, rows, input_codes.shape[1], width, dictionary.shape[0], gate_weight.shape[0]):
        return run_group(
            L, H, input_codes, cotangent_codes, dictionary, encoder_bias[None, :], decoder_bias,
            norm_gain, gate_weight, up_weight, down_weight,
        )
    own_width = input_codes.shape[1]
    model_width = own_width * lax.axis_size(("latent", "hidden"))
    cotangent_local = (cotangent_codes.astype(jnp.float32) * CODE_STEP).astype(jnp.bfloat16)
    hidden_grad = None
    inputs_local = (input_codes.astype(jnp.float32) * CODE_STEP).astype(jnp.bfloat16)
    inputs = lax.all_gather(inputs_local, ("latent", "hidden"), axis=1, tiled=True)
    preact = (
        lax.dot_general(inputs, dictionary, ACROSS, preferred_element_type=jnp.float32)
        + encoder_bias
    )
    latents = jnp.maximum(preact, 0.0).astype(jnp.bfloat16)
    partial_value = jnp.dot(latents, dictionary, preferred_element_type=jnp.float32)
    rebuilt = lax.psum(partial_value, ("latent", "hidden")) + decoder_bias
    inverse = lax.rsqrt(
        jnp.sum(rebuilt * rebuilt, axis=1, keepdims=True) / model_width + NORM_EPSILON
    )
    normed = (rebuilt * inverse * norm_gain).astype(jnp.bfloat16)
    target = inputs.astype(jnp.float32)
    gate_proj = lax.dot_general(normed, gate_weight, ACROSS, preferred_element_type=jnp.float32)
    up_proj = lax.dot_general(normed, up_weight, ACROSS, preferred_element_type=jnp.float32)
    gelu_value, gelu_slope = gelu_parts(gate_proj)
    hidden = (gelu_value * up_proj).astype(jnp.bfloat16)
    output_terms = jnp.dot(hidden, down_weight, preferred_element_type=jnp.float32)
    block_output = lax.psum_scatter(
        output_terms, ("latent", "hidden"), scatter_dimension=1, tiled=True
    ).astype(jnp.bfloat16)
    hidden_grad = lax.dot_general(
        lax.all_gather(cotangent_local, ("latent", "hidden"), axis=1, tiled=True),
        down_weight,
        ACROSS,
        preferred_element_type=jnp.float32,
    )
    gate_grad = (hidden_grad * up_proj * gelu_slope).astype(jnp.bfloat16)
    up_grad = (hidden_grad * gelu_value).astype(jnp.bfloat16)
    partial_grad = jnp.dot(gate_grad, gate_weight, preferred_element_type=jnp.float32) + jnp.dot(
        up_grad, up_weight, preferred_element_type=jnp.float32
    )
    scaled = lax.psum(partial_grad, ("latent", "hidden")) * norm_gain
    inner_row = jnp.sum(scaled * rebuilt, axis=1, keepdims=True)
    inverse_cube = inverse * inverse * inverse
    rebuilt_grad = (
        inverse * scaled - inverse_cube * rebuilt * (inner_row / model_width) + (rebuilt - target)
    ).astype(jnp.bfloat16)
    latent_grad = lax.dot_general(
        rebuilt_grad, dictionary, ACROSS, preferred_element_type=jnp.float32
    )
    preact_grad = jnp.where(preact > 0.0, latent_grad, 0.0).astype(jnp.bfloat16)
    dictionary_grad = lax.dot_general(
        latents, rebuilt_grad, DOWNWARD, preferred_element_type=jnp.float32
    ) + lax.dot_general(preact_grad, inputs, DOWNWARD, preferred_element_type=jnp.float32)
    return (block_output, dictionary_grad.astype(jnp.bfloat16))


def solution(mesh):
    in_specs = (
        P("groups", ("latent", "hidden")),
        P("groups", ("latent", "hidden")),
        P(("latent", "hidden"), None),
        P(("latent", "hidden")),
        P(),
        P(),
        P(("latent", "hidden"), None),
        P(("latent", "hidden"), None),
        P(("latent", "hidden"), None),
    )
    out_specs = (P("groups", ("latent", "hidden")), P(("latent", "hidden"), "groups"))
    return jax.shard_map(
        per_device, mesh=mesh, in_specs=in_specs, out_specs=out_specs, check_vma=False
    )
```

```python
import types

import jax
import jax.numpy as jnp
from jax import lax
from jax.experimental import pallas as pl
from jax.experimental.pallas import tpu as pltpu
from jax.sharding import PartitionSpec as P

ROWS = 8
PACK = 16
PARTS = 1
LANES = 128
TILE = 256
MESH = pl.DeviceIdType.MESH
F32 = jnp.float32
BF16 = jnp.bfloat16


def group_kernel(L, H, refs_in, refs_out, s):
    (codes_x, codes_u, dic_hbm, ebias_in, dbias_in, gain_in, gate_hbm, up_hbm, down_hbm) = refs_in
    (out_cols, left, right) = refs_out
    me = lax.axis_index("latent")
    h = lax.axis_index("hidden")
    other = 1 - h
    rows, own_width = codes_x.shape
    width = dic_hbm.shape[1]
    units = dic_hbm.shape[0]
    C = rows // ROWS
    K = C // H
    extra = K - L
    n_dev = L * H
    mine = me * H + h
    high = s.gx.shape[1]
    rest = own_width - LANES
    per = LANES // rest

    def ext(hid):
        return (2 + 3 * hid) % L

    def at(lat, hid):
        return {"latent": lat, "hidden": hid}

    def rcopy(src, dst, ss, rs, lat, hid):
        return pltpu.make_async_remote_copy(
            src_ref=src, dst_ref=dst, send_sem=ss, recv_sem=rs,
            device_id=at(lat, hid), device_id_type=MESH,
        )

    def each(n, body):
        def step(i, carry):
            body(i)
            return carry

        lax.fori_loop(0, n, step, 0)

    def slots(body):
        body(0, me)
        if extra:
            @pl.when(me == ext(h))
            def _():
                body(1, L)

    X = 2
    Z = L // X
    z, x = me // X, lax.rem(me, X)
    across_me = z * X + 1 - x
    near_z, same_z, flip_z = z + 1 - 2 * lax.rem(z, 2), z + 2 - 4 * (z // 2), 3 - z
    peers = (near_z, same_z, flip_z)
    far = (same_z, flip_z, near_z)

    def col(zz):
        return zz * X + x

    def beside(zz):
        return zz * X + 1 - x

    barrier = pltpu.get_barrier_semaphore()
    greeted = [(me, other), (across_me, h)] + [(col(zz), h) for zz in far]
    for lat, hid in greeted:
        pl.semaphore_signal(barrier, inc=1, device_id=at(lat, hid), device_id_type=MESH)

    loads = []
    for i, (src, dst) in enumerate((
        (codes_x, s.codes_x), (codes_u, s.codes_u), (dic_hbm, s.dic), (ebias_in, s.ebias),
        (dbias_in, s.dbias), (gain_in, s.gain), (down_hbm, s.down), (gate_hbm, s.gate), (up_hbm, s.up),
    )):
        cp = pltpu.make_async_copy(src, dst, s.load_sem.at[i])
        cp.start()
        loads.append(cp)

    def stage(codes, arr):
        value = codes[...].astype(F32) * (2.0 ** (-6))
        shift = lax.rem(mine * own_width, LANES)
        arr[mine, pl.ds(0, rows)] = pltpu.roll(value[:, :LANES], shift, 1).astype(BF16)
        over = jnp.concatenate([value[:, LANES:], jnp.zeros((rows, LANES - rest), F32)], axis=1)
        for b in range(s.gx.shape[1] // PACK - rows // PACK):
            packed = None
            for g in range(b * per, min((b + 1) * per, rows // PACK)):
                part = over[g * PACK : (g + 1) * PACK]
                part = pltpu.roll(part, (g % per) * rest, 1) if g % per else part
                packed = part if packed is None else packed + part
            arr[mine, pl.ds(rows + b * PACK, PACK)] = packed.astype(BF16)

    ext_z = ext(h) // X
    ext_here = lax.rem(ext(h), X) == x
    ext_mine = me == ext(h)
    ext_passes = jnp.logical_and(ext_here, jnp.logical_not(ext_mine))

    def when_extra(cond, body):
        if extra:
            @pl.when(cond)
            def _():
                body(L, Z)

    def wait_here(buf, sem):
        rcopy(buf, buf, sem, sem, me, other).wait_recv()

    def wait_sent(buf, sem):
        rcopy(buf, buf, sem, sem, me, other).wait_send()

    def cols_send(arr, a, i, lat):
        rcopy(arr.at[i], arr.at[i], s.col_ss.at[a], s.col_rs.at[a, i // H], lat, h).start()

    def cols_give(arr, a, i):
        rcopy(arr.at[i], arr.at[i], s.col_fs.at[a], s.col_fr.at[a], me, other).start()

    def cols_got(arr, a, lat, relay=False):
        i = lat * H + h
        wait_here(arr.at[i], s.col_rs.at[a, lat])
        if relay:
            cols_send(arr, a, i, across_me)
        cols_give(arr, a, i)

    def cols_start(arr, a):
        for zz in far:
            cols_send(arr, a, mine, col(zz))
        cols_send(arr, a, mine, across_me)
        cols_give(arr, a, mine)

    def cols_column(arr, a):
        for zz in peers:
            cols_got(arr, a, col(zz), True)

    def cols_across(arr, a):
        cols_got(arr, a, across_me)
        for zz in peers:
            cols_got(arr, a, beside(zz))

    def cols_take(arr, a):
        wait_here(arr.at[pl.ds(0, L)], s.col_fr.at[a])

    def cols_drain(arr, a):
        wait_sent(arr.at[pl.ds(0, L - 1)], s.col_ss.at[a])
        wait_sent(arr.at[pl.ds(0, L)], s.col_fs.at[a])

    def cols_rows(arr, put):
        lane = lax.broadcasted_iota(jnp.int32, (rows, LANES), 1)

        def main(i):
            return arr[i, pl.ds(0, rows)].astype(F32)

        def over(i):
            block = arr[i, pl.ds(rows, s.gx.shape[1] - rows)].astype(F32)
            parts = []
            for g in range(rows // PACK):
                b = g // per
                move = (i * own_width - (g % per) * rest) % LANES
                part = block[b * PACK : (b + 1) * PACK]
                parts.append(pltpu.roll(part, move, 1) if move else part)
            return jnp.concatenate(parts, axis=0)

        for t in range(width // LANES):
            value = None
            for i in range(n_dev):
                first, offset = divmod(i * own_width, LANES)
                if first == t:
                    new = main(i)
                    value = new if value is None else jnp.where(lane >= offset, new, value)
                elif first == t - 1:
                    value = over(i)
                    if offset:
                        value = jnp.where(lane >= offset, value, main(i))
            put(t, value)

    part_width = width // PARTS

    def part(full, c, p):
        return full.at[c, :, pl.ds(p * part_width, part_width)]

    def hand_over(full, a, k, p):
        piece = part(full, h * K + k, p)
        rcopy(piece, piece, s.ag_fs.at[a], s.ag_fr.at[a, p], me, other).start()

    def step_across(full, a, k, i, p):
        piece = part(full, h * K + k, p)
        rcopy(piece, piece, s.ag_xs.at[a], s.ag_xr.at[a, i, p], across_me, h).start()

    def spread_start(full, a, ready=None):
        def one(slot, k):
            if ready is not None:
                ready(slot, k)
            c = h * K + k
            i = Z if slot else z
            for p in range(PARTS):
                piece = part(full, c, p)
                for zz in far:
                    rcopy(piece, piece, s.ag_ss.at[a, slot], s.ag_rr.at[a, i, p], col(zz), h).start()
                step_across(full, a, k, i, p)
                hand_over(full, a, k, p)

        slots(one)

    def relay_column(full, a, k, i, p):
        wait_here(part(full, h * K + k, p), s.ag_rr.at[a, i, p])
        step_across(full, a, k, i, p)
        hand_over(full, a, k, p)

    def relay_across(full, a, k, i, p):
        wait_here(part(full, h * K + k, p), s.ag_xr.at[a, i, p])
        hand_over(full, a, k, p)

    def spread_column(full, a):
        for p in range(PARTS):
            for zz in peers:
                relay_column(full, a, col(zz), zz, p)
            when_extra(ext_passes, lambda k, i: relay_column(full, a, k, i, p))

    def spread_across(full, a, p):
        relay_across(full, a, across_me, z, p)
        for zz in peers:
            relay_across(full, a, beside(zz), zz, p)
        when_extra(jnp.logical_not(ext_here), lambda k, i: relay_across(full, a, k, i, p))

    def spread_take(full, a, p):
        wait_here(full.at[pl.ds(other * K, K), :, pl.ds(p * part_width, part_width)], s.ag_fr.at[a, p])

    def either(cond, body, no, yes):
        @pl.when(cond)
        def _():
            body(yes)

        @pl.when(jnp.logical_not(cond))
        def _():
            body(no)

    def spread_drain(full, a):
        slots(lambda slot, k: wait_sent(full.at[pl.ds(0, Z - 1)], s.ag_ss.at[a, slot]))
        either(ext_here, lambda n: wait_sent(full.at[pl.ds(0, n)], s.ag_xs.at[a]), Z, Z + 1)
        wait_sent(full.at[pl.ds(0, K)], s.ag_fs.at[a])

    def rows_of(full, dst, p):
        at_cols = slice(p * part_width, (p + 1) * part_width)
        dst[:, at_cols] = full[:, :, at_cols].astype(F32).reshape(rows, part_width).astype(BF16)

    def sum_tile(a, t, value):
        cols = pl.ds(t * wide, wide)
        s.own[a, :, :, cols] = value.reshape(C, ROWS, wide)
        rcopy(
            s.own.at[a, pl.ds(other * K, K), :, cols], s.sib.at[a, :, :, cols],
            s.rs_cs.at[a], s.rs_cr.at[a], me, other,
        ).start()

    wide = 3 * TILE if width % (3 * TILE) == 0 else LANES
    n_wide = width // wide

    def sum_start(a):
        wait_here(s.sib.at[a], s.rs_cr.at[a])

    def sum_chip(a, k):
        return s.own[a, h * K + k] + s.sib[a, k]

    def sum_middle(a):
        def leave(k, i):
            s.comb[a, k] = sum_chip(a, k).astype(BF16)
            rcopy(s.comb.at[a, k], s.xbuf.at[a, k], s.rs_xs.at[a], s.rs_xr.at[a, i], across_me, h).start()

        for zz in far:
            leave(beside(zz), zz)
        when_extra(jnp.logical_not(ext_here), leave)
        leave(across_me, z)

    def sum_cross(a):
        def total(k, i):
            value = sum_chip(a, k)
            wait_here(s.xbuf.at[a, k], s.rs_xr.at[a, i])
            return value + s.xbuf[a, k].astype(F32)

        def leave(slot, k, i, owner):
            s.comb[a, k] = total(k, i).astype(BF16)
            rcopy(s.comb.at[a, k], s.rbuf.at[a, slot, z], s.rs_ss.at[a], s.rs_rr.at[a, slot], owner, h).start()

        for zz in far:
            leave(0, col(zz), zz, col(zz))
        when_extra(ext_passes, lambda k, i: leave(1, k, i, ext(h)))
        s.acc[a, 0] = total(me, z)

        def keep(k, i):
            s.acc[a, 1] = total(k, i)

        when_extra(ext_mine, keep)

    def sum_value(a, slot):
        value = s.acc[a, slot]
        wait_here(s.rbuf.at[a, slot, pl.ds(0, Z - 1)], s.rs_rr.at[a, slot])
        for zz in peers:
            value = value + s.rbuf[a, slot, zz].astype(F32)
        return value

    def sum_drain(a):
        wait_sent(s.sib.at[a], s.rs_cs.at[a])
        either(jnp.logical_not(ext_here), lambda n: wait_sent(s.xbuf.at[a, pl.ds(0, n)], s.rs_xs.at[a]), Z, Z + 1)
        either(ext_passes, lambda n: wait_sent(s.xbuf.at[a, pl.ds(0, n)], s.rs_ss.at[a]), Z - 1, Z)

    def out_tile(t, value):
        s.wide_out[:, t * wide : (t + 1) * wide] = value

    def out_pieces():
        lane = lax.broadcasted_iota(jnp.int32, (rows, LANES), 1)
        group = lax.broadcasted_iota(jnp.int32, (PACK, LANES), 1) // rest
        for i in range(n_dev):
            first, offset = divmod(i * own_width, LANES)
            here = s.wide_out[:, first * LANES : (first + 1) * LANES]
            there = s.wide_out[:, (first + 1) * LANES : (first + 2) * LANES]
            piece = s.own_out.at[i % H, i // H]
            piece[pl.ds(0, rows)] = jnp.where(lane >= offset, here, there) if offset else here
            for b in range(high // PACK - rows // PACK):
                packed = jnp.zeros((PACK, LANES), F32)
                for g in range(b * per, min((b + 1) * per, rows // PACK)):
                    part = there[g * PACK : (g + 1) * PACK]
                    move = ((g % per) * rest - offset) % LANES
                    part = pltpu.roll(part, move, 1) if move else part
                    packed = jnp.where(group == g % per, part, packed)
                piece[pl.ds(rows + b * PACK, PACK)] = packed
        rcopy(s.own_out.at[other], s.sib_out, s.out_cs.at[0], s.out_cr.at[0], me, other).start()

    def out_chip(lat):
        return s.own_out[h, lat] + s.sib_out[lat]

    def out_middle():
        wait_here(s.sib_out, s.out_cr.at[0])
        for lat, i in [(beside(zz), zz) for zz in far] + [(across_me, z)]:
            s.comb_out[lat] = out_chip(lat).astype(BF16)
            rcopy(s.comb_out.at[lat], s.xbuf_out.at[lat], s.out_xs.at[0], s.out_xr.at[i], across_me, h).start()

    def out_total(lat, i):
        wait_here(s.xbuf_out.at[lat], s.out_xr.at[i])
        return out_chip(lat) + s.xbuf_out[lat].astype(F32)

    def out_cross():
        for zz in far:
            lat = col(zz)
            s.comb_out[lat] = out_total(lat, zz).astype(BF16)
            rcopy(s.comb_out.at[lat], s.rbuf_out.at[z], s.out_ss.at[0], s.out_rr.at[0], lat, h).start()
        s.acc_out[...] = out_total(me, z)

    def out_final():
        wait_here(s.rbuf_out.at[pl.ds(0, Z - 1)], s.out_rr.at[0])
        value = s.acc_out[...]
        for zz in peers:
            value = value + s.rbuf_out[zz].astype(F32)
        back_by = lax.rem(LANES - lax.rem(mine * own_width, LANES), LANES)
        out_cols[:, :LANES] = pltpu.roll(value[:rows], back_by, 1).astype(BF16)
        parts = []
        for g in range(rows // PACK):
            part = value[rows + (g // per) * PACK : rows + (g // per + 1) * PACK]
            move = (-(g % per) * rest) % LANES
            parts.append(pltpu.roll(part, move, 1) if move else part)
        out_cols[:, LANES:] = jnp.concatenate(parts, axis=0)[:, :rest].astype(BF16)

    def out_drain():
        wait_sent(s.sib_out, s.out_cs.at[0])
        wait_sent(s.xbuf_out.at[pl.ds(0, Z)], s.out_xs.at[0])
        wait_sent(s.xbuf_out.at[pl.ds(0, Z - 1)], s.out_ss.at[0])

    across = (((1,), (1,)), ((), ()))

    def mm_t(x, w):
        return lax.dot_general(x, w, across, preferred_element_type=F32)

    def mm(x, w):
        return lax.dot_general(x, w, (((1,), (0,)), ((), ())), preferred_element_type=F32)

    deep = TILE if units % TILE == 0 else units
    n_deep = units // deep

    def flip(src, dst):
        for t in range(units // LANES):
            at_rows = slice(t * LANES, (t + 1) * LANES)
            dst[:, at_rows] = src[at_rows, :].T

    loads[0].wait()
    stage(s.codes_x, s.gx)
    pl.semaphore_wait(barrier, len(greeted))
    cols_start(s.gx, 0)
    loads[1].wait()
    stage(s.codes_u, s.gu)
    loads[2].wait()
    flip(s.dic, s.dic_t)
    cols_column(s.gx, 0)
    cols_across(s.gx, 0)
    cols_start(s.gu, 1)
    cols_take(s.gx, 0)
    x_rows = right.at[pl.ds(rows, rows)]
    r_rows = right.at[pl.ds(0, rows)]

    def put_x(t, value):
        right[pl.ds(rows, rows), t * LANES : (t + 1) * LANES] = value.astype(BF16)
        s.full_x[:, :, t * LANES : (t + 1) * LANES] = value.reshape(C, ROWS, LANES).astype(BF16)

    cols_rows(s.gx, put_x)
    loads[3].wait()
    for t in range(n_deep):
        cols = pl.ds(t * deep, deep)
        pre = mm(x_rows[...], s.dic_t[:, cols]) + s.ebias[:, cols]
        s.pre[:, cols] = pre
        left[pl.ds(0, rows), cols] = jnp.maximum(pre, 0.0).astype(BF16)
    for t in range(n_wide):
        sum_tile(0, t, mm(left[pl.ds(0, rows), :], s.dic[:, t * wide : (t + 1) * wide]))
    sum_start(0)
    sum_middle(0)
    loads[7].wait()
    flip(s.gate, s.gate_t)
    loads[8].wait()
    flip(s.up, s.up_t)
    sum_cross(0)
    cols_column(s.gu, 1)

    def put_u(t, value):
        s.u_rows[:, t * LANES : (t + 1) * LANES] = value.astype(BF16)

    loads[4].wait()
    loads[5].wait()

    def norm(slot, k):
        rebuilt = sum_value(0, slot) + s.dbias[...]
        inverse = lax.rsqrt(jnp.sum(rebuilt * rebuilt, axis=1, keepdims=True) / width + 1e-06)
        s.rebuilt[slot] = rebuilt
        s.inverse[slot] = jnp.broadcast_to(inverse, (ROWS, LANES))
        s.full_n[h * K + k] = (rebuilt * inverse * s.gain[...]).astype(BF16)

    spread_start(s.full_n, 0, norm)
    cols_across(s.gu, 1)
    cols_take(s.gu, 1)
    cols_rows(s.gu, put_u)
    loads[6].wait()
    for t in range(n_deep):
        cols = pl.ds(t * deep, deep)
        s.hgrad[:, cols] = mm_t(s.u_rows[...], s.down[cols, :])
    spread_column(s.full_n, 0)
    for p in range(PARTS):
        spread_across(s.full_n, 0, p)
        spread_take(s.full_n, 0, p)
        rows_of(s.full_n, s.n_rows, p)
        if p < PARTS - 1:
            at_cols = slice(p * part_width, (p + 1) * part_width)
            for t in range(n_deep):
                cols = pl.ds(t * deep, deep)
                g = mm(s.n_rows[:, at_cols], s.gate_t[at_cols, cols])
                u = mm(s.n_rows[:, at_cols], s.up_t[at_cols, cols])
                s.g_sum[:, cols] = g + s.g_sum[:, cols] if p else g
                s.u_sum[:, cols] = u + s.u_sum[:, cols] if p else u
    last = slice((PARTS - 1) * part_width, width)
    for t in range(n_deep):
        cols = pl.ds(t * deep, deep)
        g = mm(s.n_rows[:, last], s.gate_t[last, cols])
        u = mm(s.n_rows[:, last], s.up_t[last, cols])
        if PARTS > 1:
            g = g + s.g_sum[:, cols]
            u = u + s.u_sum[:, cols]
        th = jnp.tanh(0.7978845608028654 * (g + 0.044715 * g * g * g))
        value = 0.5 * g * (1.0 + th)
        slope = 0.5 * (1.0 + th) + 0.5 * g * (1.0 - th * th) * 0.7978845608028654 * (
            1.0 + 3.0 * 0.044715 * g * g
        )
        hg = s.hgrad[:, cols]
        s.hid[:, cols] = (value * u).astype(BF16)
        s.ggrad[:, cols] = (hg * u * slope).astype(BF16)
        s.ugrad[:, cols] = (hg * value).astype(BF16)
    for t in range(n_wide):
        cols = slice(t * wide, (t + 1) * wide)
        sum_tile(1, t, mm(s.ggrad[...], s.gate[:, cols]) + mm(s.ugrad[...], s.up[:, cols]))
    sum_start(1)
    sum_middle(1)
    for t in range(n_wide):
        out_tile(t, mm(s.hid[...], s.down[:, t * wide : (t + 1) * wide]))
    sum_cross(1)
    out_pieces()
    out_middle()

    def back(slot, k):
        scaled = sum_value(1, slot) * s.gain[...]
        rebuilt = s.rebuilt[slot]
        inverse = s.inverse[slot][:, :1]
        inner = jnp.sum(scaled * rebuilt, axis=1, keepdims=True)
        target = s.full_x[h * K + k].astype(F32)
        s.full_r[h * K + k] = (
            inverse * scaled - inverse * inverse * inverse * rebuilt * (inner / width) + (rebuilt - target)
        ).astype(BF16)

    spread_start(s.full_r, 1, back)
    for a, arr in enumerate((s.gx, s.gu)):
        cols_drain(arr, a)
    spread_drain(s.full_n, 0)
    sum_drain(0)
    spread_column(s.full_r, 1)
    out_cross()
    for p in range(PARTS):
        spread_across(s.full_r, 1, p)
        spread_take(s.full_r, 1, p)
        rows_of(s.full_r, r_rows, p)
        if p < PARTS - 1:
            at_cols = slice(p * part_width, (p + 1) * part_width)
            for t in range(n_deep):
                cols = pl.ds(t * deep, deep)
                g = mm(r_rows[:, at_cols], s.dic_t[at_cols, cols])
                s.g_sum[:, cols] = g + s.g_sum[:, cols] if p else g
    for t in range(n_deep):
        cols = pl.ds(t * deep, deep)
        grad = mm(r_rows[:, last], s.dic_t[last, cols])
        if PARTS > 1:
            grad = grad + s.g_sum[:, cols]
        left[pl.ds(rows, rows), cols] = jnp.where(s.pre[:, cols] > 0.0, grad, 0.0).astype(BF16)

    out_final()
    spread_drain(s.full_r, 1)
    sum_drain(1)
    out_drain()


def run_group(L, H, *args):
    codes, dic = args[0], args[2]
    rows, own_width = codes.shape
    units, width = dic.shape
    C = rows // ROWS
    K = C // H
    Z = L // 2
    n_dev = L * H
    per = LANES // (own_width - LANES)
    high = rows + PACK * -(-(rows // PACK) // per)
    V, D, R = pltpu.VMEM, pltpu.SemaphoreType.DMA, ROWS
    scratch = dict(
        codes_x=V((rows, own_width), jnp.int32), codes_u=V((rows, own_width), jnp.int32),
        ebias=V((1, units), F32), dbias=V((width,), F32), gain=V((width,), F32),
        dic=V((units, width), BF16), gate=V((units, width), BF16),
        up=V((units, width), BF16), down=V((units, width), BF16),
        dic_t=V((width, units), BF16), gate_t=V((width, units), BF16), up_t=V((width, units), BF16),
        g_sum=V((rows, units), F32), u_sum=V((rows, units), F32),
        gx=V((n_dev, high, LANES), BF16), gu=V((n_dev, high, LANES), BF16),
        full_x=V((C, R, width), BF16), full_n=V((C, R, width), BF16), full_r=V((C, R, width), BF16),
        u_rows=V((rows, width), BF16), n_rows=V((rows, width), BF16),
        pre=V((rows, units), F32), hgrad=V((rows, units), F32), hid=V((rows, units), BF16),
        ggrad=V((rows, units), BF16), ugrad=V((rows, units), BF16),
        own=V((2, C, R, width), F32), xbuf=V((2, K, R, width), BF16),
        sib=V((2, K, R, width), F32), comb=V((2, K, R, width), BF16),
        rbuf=V((2, 2, Z, R, width), BF16), acc=V((2, 2, R, width), F32),
        rebuilt=V((2, R, width), F32), inverse=V((2, R, LANES), F32),
        wide_out=V((rows, width), F32), own_out=V((H, L, high, LANES), F32), sib_out=V((L, high, LANES), F32),
        comb_out=V((L, high, LANES), BF16), xbuf_out=V((L, high, LANES), BF16),
        rbuf_out=V((Z, high, LANES), BF16), acc_out=V((high, LANES), F32),
        load_sem=D((9,)),
        col_ss=D((2,)), col_rs=D((2, L)), col_fs=D((2,)), col_fr=D((2,)),
        ag_ss=D((2, 2)), ag_xs=D((2,)), ag_xr=D((2, Z + 1, PARTS)), ag_rr=D((2, Z + 1, PARTS)), ag_fs=D((2,)), ag_fr=D((2, PARTS)),
        rs_cs=D((2,)), rs_cr=D((2,)), rs_ss=D((2,)), rs_rr=D((2, 2)), rs_xs=D((2,)), rs_xr=D((2, Z + 1)),
        out_cs=D((1,)), out_cr=D((1,)), out_xs=D((1,)), out_xr=D((Z,)), out_ss=D((1,)), out_rr=D((1,)),
    )
    names = list(scratch)

    def body(*refs):
        group_kernel(L, H, refs[:9], refs[9:12], types.SimpleNamespace(**dict(zip(names, refs[12:]))))

    hbm = pl.BlockSpec(memory_space=pltpu.HBM)
    vm = pl.BlockSpec(memory_space=pltpu.VMEM)
    cols, left, right = pl.pallas_call(
        body,
        name="group_step",
        out_shape=(
            V((rows, own_width), BF16),
            V((2 * rows, units), BF16),
            V((2 * rows, width), BF16),
        ),
        in_specs=[hbm] * 9,
        out_specs=(vm, vm, vm),
        scratch_shapes=[scratch[n] for n in names],
        compiler_params=pltpu.CompilerParams(collective_id=0, has_side_effects=True, vmem_limit_bytes=60 * 2**20),
    )(*args)

    step = width // 6 if width % (6 * LANES) == 0 else LANES
    n_step = width // step

    def product(cols, left, right, block, grad, tiles, sem):
        copies = []
        for t in range(n_step):
            at = slice(t * step, (t + 1) * step)
            tiles[t] = lax.dot_general(
                left[...], right[:, at], (((0,), (0,)), ((), ())), preferred_element_type=F32
            ).astype(BF16)
            copies.append(pltpu.make_async_copy(tiles.at[t], grad.at[:, at], sem.at[t]))
            copies[-1].start()
        block[...] = cols[...]
        for cp in copies:
            cp.wait()

    return pl.pallas_call(
        product,
        name="dictionary_product",
        out_shape=(
            jax.ShapeDtypeStruct((rows, own_width), BF16),
            jax.ShapeDtypeStruct((units, width), BF16),
        ),
        in_specs=[vm, vm, vm],
        out_specs=(vm, pl.BlockSpec(memory_space=pl.ANY)),
        scratch_shapes=[V((n_step, units, step), BF16), D((n_step,))],
        compiler_params=pltpu.CompilerParams(vmem_limit_bytes=16 * 2**20),
    )(cols, left, right)


def fits(L, H, rows, own_width, width, units, units_mlp):
    rest = own_width - LANES
    if H != 2 or rows % (ROWS * H) or rows % PACK or width % LANES or units % LANES or units != units_mlp:
        return False
    if rest <= 0 or rest >= LANES or LANES % rest or own_width * L * H != width or width % (PARTS * LANES):
        return False
    return L == 8 and rows // ROWS // H == L + 1


CODE_STEP = 2.0 ** (-6)
NORM_EPSILON = 1e-06
GELU_ROOT = 0.7978845608028654
GELU_CUBIC = 0.044715
ACROSS = (((1,), (1,)), ((), ()))
DOWNWARD = (((0,), (0,)), ((), ()))


def gelu_parts(values):
    argument = GELU_ROOT * (values + GELU_CUBIC * values * values * values)
    tanh_value = jnp.tanh(argument)
    result = 0.5 * values * (1.0 + tanh_value)
    derivative = 0.5 * (1.0 + tanh_value) + 0.5 * values * (
        1.0 - tanh_value * tanh_value
    ) * GELU_ROOT * (1.0 + 3.0 * GELU_CUBIC * values * values)
    return (result, derivative)


def per_device(
    input_codes,
    cotangent_codes,
    dictionary,
    encoder_bias,
    decoder_bias,
    norm_gain,
    gate_weight,
    up_weight,
    down_weight,
):
    L, H = lax.axis_size("latent"), lax.axis_size("hidden")
    rows, width = input_codes.shape[0], dictionary.shape[1]
    if fits(L, H, rows, input_codes.shape[1], width, dictionary.shape[0], gate_weight.shape[0]):
        return run_group(
            L, H, input_codes, cotangent_codes, dictionary, encoder_bias[None, :], decoder_bias,
            norm_gain, gate_weight, up_weight, down_weight,
        )
    own_width = input_codes.shape[1]
    model_width = own_width * lax.axis_size(("latent", "hidden"))
    cotangent_local = (cotangent_codes.astype(jnp.float32) * CODE_STEP).astype(jnp.bfloat16)
    hidden_grad = None
    inputs_local = (input_codes.astype(jnp.float32) * CODE_STEP).astype(jnp.bfloat16)
    inputs = lax.all_gather(inputs_local, ("latent", "hidden"), axis=1, tiled=True)
    preact = (
        lax.dot_general(inputs, dictionary, ACROSS, preferred_element_type=jnp.float32)
        + encoder_bias
    )
    latents = jnp.maximum(preact, 0.0).astype(jnp.bfloat16)
    partial_value = jnp.dot(latents, dictionary, preferred_element_type=jnp.float32)
    rebuilt = lax.psum(partial_value, ("latent", "hidden")) + decoder_bias
    inverse = lax.rsqrt(
        jnp.sum(rebuilt * rebuilt, axis=1, keepdims=True) / model_width + NORM_EPSILON
    )
    normed = (rebuilt * inverse * norm_gain).astype(jnp.bfloat16)
    target = inputs.astype(jnp.float32)
    gate_proj = lax.dot_general(normed, gate_weight, ACROSS, preferred_element_type=jnp.float32)
    up_proj = lax.dot_general(normed, up_weight, ACROSS, preferred_element_type=jnp.float32)
    gelu_value, gelu_slope = gelu_parts(gate_proj)
    hidden = (gelu_value * up_proj).astype(jnp.bfloat16)
    output_terms = jnp.dot(hidden, down_weight, preferred_element_type=jnp.float32)
    block_output = lax.psum_scatter(
        output_terms, ("latent", "hidden"), scatter_dimension=1, tiled=True
    ).astype(jnp.bfloat16)
    hidden_grad = lax.dot_general(
        lax.all_gather(cotangent_local, ("latent", "hidden"), axis=1, tiled=True),
        down_weight,
        ACROSS,
        preferred_element_type=jnp.float32,
    )
    gate_grad = (hidden_grad * up_proj * gelu_slope).astype(jnp.bfloat16)
    up_grad = (hidden_grad * gelu_value).astype(jnp.bfloat16)
    partial_grad = jnp.dot(gate_grad, gate_weight, preferred_element_type=jnp.float32) + jnp.dot(
        up_grad, up_weight, preferred_element_type=jnp.float32
    )
    scaled = lax.psum(partial_grad, ("latent", "hidden")) * norm_gain
    inner_row = jnp.sum(scaled * rebuilt, axis=1, keepdims=True)
    inverse_cube = inverse * inverse * inverse
    rebuilt_grad = (
        inverse * scaled - inverse_cube * rebuilt * (inner_row / model_width) + (rebuilt - target)
    ).astype(jnp.bfloat16)
    latent_grad = lax.dot_general(
        rebuilt_grad, dictionary, ACROSS, preferred_element_type=jnp.float32
    )
    preact_grad = jnp.where(preact > 0.0, latent_grad, 0.0).astype(jnp.bfloat16)
    dictionary_grad = lax.dot_general(
        latents, rebuilt_grad, DOWNWARD, preferred_element_type=jnp.float32
    ) + lax.dot_general(preact_grad, inputs, DOWNWARD, preferred_element_type=jnp.float32)
    return (block_output, dictionary_grad.astype(jnp.bfloat16))


def solution(mesh):
    in_specs = (
        P("groups", ("latent", "hidden")),
        P("groups", ("latent", "hidden")),
        P(("latent", "hidden"), None),
        P(("latent", "hidden")),
        P(),
        P(),
        P(("latent", "hidden"), None),
        P(("latent", "hidden"), None),
        P(("latent", "hidden"), None),
    )
    out_specs = (P("groups", ("latent", "hidden")), P(("latent", "hidden"), "groups"))
    return jax.shard_map(
        per_device, mesh=mesh, in_specs=in_specs, out_specs=out_specs, check_vma=False
    )
```

```python
import types

import jax
import jax.numpy as jnp
from jax import lax
from jax.experimental import pallas as pl
from jax.experimental.pallas import tpu as pltpu
from jax.sharding import PartitionSpec as P

ROWS = 8
PACK = 16
PARTS = 1
LANES = 128
TILE = 256
MESH = pl.DeviceIdType.MESH
F32 = jnp.float32
BF16 = jnp.bfloat16


def group_kernel(L, H, refs_in, refs_out, s):
    (codes_x, codes_u, dic_hbm, ebias_in, dbias_in, gain_in, gate_hbm, up_hbm, down_hbm) = refs_in
    (out_cols, left, right) = refs_out
    me = lax.axis_index("latent")
    h = lax.axis_index("hidden")
    other = 1 - h
    rows, own_width = codes_x.shape
    width = dic_hbm.shape[1]
    units = dic_hbm.shape[0]
    C = rows // ROWS
    K = C // H
    extra = K - L
    n_dev = L * H
    mine = me * H + h
    high = s.gx.shape[1]
    rest = own_width - LANES
    per = LANES // rest

    def ext(hid):
        return (2 + 3 * hid) % L

    def at(lat, hid):
        return {"latent": lat, "hidden": hid}

    def rcopy(src, dst, ss, rs, lat, hid):
        return pltpu.make_async_remote_copy(
            src_ref=src, dst_ref=dst, send_sem=ss, recv_sem=rs,
            device_id=at(lat, hid), device_id_type=MESH,
        )

    def each(n, body):
        def step(i, carry):
            body(i)
            return carry

        lax.fori_loop(0, n, step, 0)

    def slots(body):
        body(0, me)
        if extra:
            @pl.when(me == ext(h))
            def _():
                body(1, L)

    X = 2
    Z = L // X
    z, x = me // X, lax.rem(me, X)
    across_me = z * X + 1 - x
    near_z, same_z, flip_z = z + 1 - 2 * lax.rem(z, 2), z + 2 - 4 * (z // 2), 3 - z
    peers = (near_z, same_z, flip_z)
    far = (same_z, flip_z, near_z)

    def col(zz):
        return zz * X + x

    def beside(zz):
        return zz * X + 1 - x

    barrier = pltpu.get_barrier_semaphore()
    greeted = [(me, other), (across_me, h)] + [(col(zz), h) for zz in far]
    for lat, hid in greeted:
        pl.semaphore_signal(barrier, inc=1, device_id=at(lat, hid), device_id_type=MESH)

    loads = []
    for i, (src, dst) in enumerate((
        (codes_x, s.codes_x), (codes_u, s.codes_u), (dic_hbm, s.dic), (ebias_in, s.ebias),
        (dbias_in, s.dbias), (gain_in, s.gain), (down_hbm, s.down), (gate_hbm, s.gate), (up_hbm, s.up),
    )):
        cp = pltpu.make_async_copy(src, dst, s.load_sem.at[i])
        cp.start()
        loads.append(cp)

    def stage(codes, arr):
        value = codes[...].astype(F32) * (2.0 ** (-6))
        shift = lax.rem(mine * own_width, LANES)
        arr[mine, pl.ds(0, rows)] = pltpu.roll(value[:, :LANES], shift, 1).astype(BF16)
        over = jnp.concatenate([value[:, LANES:], jnp.zeros((rows, LANES - rest), F32)], axis=1)
        for b in range(s.gx.shape[1] // PACK - rows // PACK):
            packed = None
            for g in range(b * per, min((b + 1) * per, rows // PACK)):
                part = over[g * PACK : (g + 1) * PACK]
                part = pltpu.roll(part, (g % per) * rest, 1) if g % per else part
                packed = part if packed is None else packed + part
            arr[mine, pl.ds(rows + b * PACK, PACK)] = packed.astype(BF16)

    ext_z = ext(h) // X
    ext_here = lax.rem(ext(h), X) == x
    ext_mine = me == ext(h)
    ext_passes = jnp.logical_and(ext_here, jnp.logical_not(ext_mine))

    def when_extra(cond, body):
        if extra:
            @pl.when(cond)
            def _():
                body(L, Z)

    def wait_here(buf, sem):
        rcopy(buf, buf, sem, sem, me, other).wait_recv()

    def wait_sent(buf, sem):
        rcopy(buf, buf, sem, sem, me, other).wait_send()

    def cols_send(arr, a, i, lat):
        rcopy(arr.at[i], arr.at[i], s.col_ss.at[a], s.col_rs.at[a, i // H], lat, h).start()

    def cols_give(arr, a, i):
        rcopy(arr.at[i], arr.at[i], s.col_fs.at[a], s.col_fr.at[a], me, other).start()

    def cols_got(arr, a, lat, relay=False):
        i = lat * H + h
        wait_here(arr.at[i], s.col_rs.at[a, lat])
        if relay:
            cols_send(arr, a, i, across_me)
        cols_give(arr, a, i)

    def cols_start(arr, a):
        for zz in far:
            cols_send(arr, a, mine, col(zz))
        cols_send(arr, a, mine, across_me)
        cols_give(arr, a, mine)

    def cols_column(arr, a):
        for zz in peers:
            cols_got(arr, a, col(zz), True)

    def cols_across(arr, a):
        cols_got(arr, a, across_me)
        for zz in peers:
            cols_got(arr, a, beside(zz))

    def cols_take(arr, a):
        wait_here(arr.at[pl.ds(0, L)], s.col_fr.at[a])

    def cols_drain(arr, a):
        wait_sent(arr.at[pl.ds(0, L - 1)], s.col_ss.at[a])
        wait_sent(arr.at[pl.ds(0, L)], s.col_fs.at[a])

    def cols_rows(arr, put):
        lane = lax.broadcasted_iota(jnp.int32, (rows, LANES), 1)

        def main(i):
            return arr[i, pl.ds(0, rows)].astype(F32)

        def over(i):
            block = arr[i, pl.ds(rows, s.gx.shape[1] - rows)].astype(F32)
            parts = []
            for g in range(rows // PACK):
                b = g // per
                move = (i * own_width - (g % per) * rest) % LANES
                part = block[b * PACK : (b + 1) * PACK]
                parts.append(pltpu.roll(part, move, 1) if move else part)
            return jnp.concatenate(parts, axis=0)

        for t in range(width // LANES):
            value = None
            for i in range(n_dev):
                first, offset = divmod(i * own_width, LANES)
                if first == t:
                    new = main(i)
                    value = new if value is None else jnp.where(lane >= offset, new, value)
                elif first == t - 1:
                    value = over(i)
                    if offset:
                        value = jnp.where(lane >= offset, value, main(i))
            put(t, value)

    part_width = width // PARTS

    def part(full, c, p):
        return full.at[c, :, pl.ds(p * part_width, part_width)]

    def hand_over(full, a, k, p):
        piece = part(full, h * K + k, p)
        rcopy(piece, piece, s.ag_fs.at[a], s.ag_fr.at[a, p], me, other).start()

    def step_across(full, a, k, i, p):
        piece = part(full, h * K + k, p)
        rcopy(piece, piece, s.ag_xs.at[a], s.ag_xr.at[a, i, p], across_me, h).start()

    def spread_start(full, a, ready=None):
        def one(slot, k):
            if ready is not None:
                ready(slot, k)
            c = h * K + k
            i = Z if slot else z
            for p in range(PARTS):
                piece = part(full, c, p)
                for zz in far:
                    rcopy(piece, piece, s.ag_ss.at[a, slot], s.ag_rr.at[a, i, p], col(zz), h).start()
                    if slot:
                        rcopy(piece, piece, s.ag_ss.at[a, slot], s.ag_xr.at[a, i, p], beside(zz), h).start()
                step_across(full, a, k, i, p)
                hand_over(full, a, k, p)

        slots(one)

    def relay_column(full, a, k, i, p):
        wait_here(part(full, h * K + k, p), s.ag_rr.at[a, i, p])
        step_across(full, a, k, i, p)
        hand_over(full, a, k, p)

    def relay_across(full, a, k, i, p):
        wait_here(part(full, h * K + k, p), s.ag_xr.at[a, i, p])
        hand_over(full, a, k, p)

    def spread_column(full, a):
        for p in range(PARTS):
            for zz in peers:
                relay_column(full, a, col(zz), zz, p)

            def passing(k, i):
                wait_here(part(full, h * K + k, p), s.ag_rr.at[a, i, p])
                hand_over(full, a, k, p)

            when_extra(ext_passes, passing)

    def spread_across(full, a, p):
        relay_across(full, a, across_me, z, p)
        for zz in peers:
            relay_across(full, a, beside(zz), zz, p)
        when_extra(jnp.logical_not(ext_here), lambda k, i: relay_across(full, a, k, i, p))

    def spread_take(full, a, p):
        wait_here(full.at[pl.ds(other * K, K), :, pl.ds(p * part_width, part_width)], s.ag_fr.at[a, p])

    def either(cond, body, no, yes):
        @pl.when(cond)
        def _():
            body(yes)

        @pl.when(jnp.logical_not(cond))
        def _():
            body(no)

    def spread_drain(full, a):
        slots(lambda slot, k: wait_sent(full.at[pl.ds(0, (slot + 1) * (Z - 1))], s.ag_ss.at[a, slot]))
        either(ext_mine, lambda n: wait_sent(full.at[pl.ds(0, n)], s.ag_xs.at[a]), Z, Z + 1)
        wait_sent(full.at[pl.ds(0, K)], s.ag_fs.at[a])

    def rows_of(full, dst, p):
        at_cols = slice(p * part_width, (p + 1) * part_width)
        dst[:, at_cols] = full[:, :, at_cols].astype(F32).reshape(rows, part_width).astype(BF16)

    def sum_tile(a, t, value):
        cols = pl.ds(t * wide, wide)
        s.own[a, :, :, cols] = value.reshape(C, ROWS, wide)
        rcopy(
            s.own.at[a, pl.ds(other * K, K), :, cols], s.sib.at[a, :, :, cols],
            s.rs_cs.at[a], s.rs_cr.at[a], me, other,
        ).start()

    wide = 3 * TILE if width % (3 * TILE) == 0 else LANES
    n_wide = width // wide

    def sum_start(a):
        wait_here(s.sib.at[a], s.rs_cr.at[a])

    def sum_chip(a, k):
        return s.own[a, h * K + k] + s.sib[a, k]

    def sum_middle(a):
        def leave(k, i):
            s.comb[a, k] = sum_chip(a, k).astype(BF16)
            rcopy(s.comb.at[a, k], s.xbuf.at[a, k], s.rs_xs.at[a], s.rs_xr.at[a, i], across_me, h).start()

        for zz in far:
            leave(beside(zz), zz)
        when_extra(jnp.logical_not(ext_here), leave)
        leave(across_me, z)

    def sum_cross(a):
        def total(k, i):
            value = sum_chip(a, k)
            wait_here(s.xbuf.at[a, k], s.rs_xr.at[a, i])
            return value + s.xbuf[a, k].astype(F32)

        def leave(slot, k, i, owner):
            s.comb[a, k] = total(k, i).astype(BF16)
            rcopy(s.comb.at[a, k], s.rbuf.at[a, slot, z], s.rs_ss.at[a], s.rs_rr.at[a, slot], owner, h).start()

        for zz in far:
            leave(0, col(zz), zz, col(zz))
        when_extra(ext_passes, lambda k, i: leave(1, k, i, ext(h)))
        s.acc[a, 0] = total(me, z)

        def keep(k, i):
            s.acc[a, 1] = total(k, i)

        when_extra(ext_mine, keep)

    def sum_value(a, slot):
        value = s.acc[a, slot]
        wait_here(s.rbuf.at[a, slot, pl.ds(0, Z - 1)], s.rs_rr.at[a, slot])
        for zz in peers:
            value = value + s.rbuf[a, slot, zz].astype(F32)
        return value

    def sum_drain(a):
        wait_sent(s.sib.at[a], s.rs_cs.at[a])
        either(jnp.logical_not(ext_here), lambda n: wait_sent(s.xbuf.at[a, pl.ds(0, n)], s.rs_xs.at[a]), Z, Z + 1)
        either(ext_passes, lambda n: wait_sent(s.xbuf.at[a, pl.ds(0, n)], s.rs_ss.at[a]), Z - 1, Z)

    def out_tile(t, value):
        s.wide_out[:, t * wide : (t + 1) * wide] = value

    def out_pieces():
        lane = lax.broadcasted_iota(jnp.int32, (rows, LANES), 1)
        group = lax.broadcasted_iota(jnp.int32, (PACK, LANES), 1) // rest
        for i in range(n_dev):
            first, offset = divmod(i * own_width, LANES)
            here = s.wide_out[:, first * LANES : (first + 1) * LANES]
            there = s.wide_out[:, (first + 1) * LANES : (first + 2) * LANES]
            piece = s.own_out.at[i % H, i // H]
            piece[pl.ds(0, rows)] = jnp.where(lane >= offset, here, there) if offset else here
            for b in range(high // PACK - rows // PACK):
                packed = jnp.zeros((PACK, LANES), F32)
                for g in range(b * per, min((b + 1) * per, rows // PACK)):
                    part = there[g * PACK : (g + 1) * PACK]
                    move = ((g % per) * rest - offset) % LANES
                    part = pltpu.roll(part, move, 1) if move else part
                    packed = jnp.where(group == g % per, part, packed)
                piece[pl.ds(rows + b * PACK, PACK)] = packed
        rcopy(s.own_out.at[other], s.sib_out, s.out_cs.at[0], s.out_cr.at[0], me, other).start()

    def out_chip(lat):
        return s.own_out[h, lat] + s.sib_out[lat]

    def out_middle():
        wait_here(s.sib_out, s.out_cr.at[0])
        for lat, i in [(beside(zz), zz) for zz in far] + [(across_me, z)]:
            s.comb_out[lat] = out_chip(lat).astype(BF16)
            rcopy(s.comb_out.at[lat], s.xbuf_out.at[lat], s.out_xs.at[0], s.out_xr.at[i], across_me, h).start()

    def out_total(lat, i):
        wait_here(s.xbuf_out.at[lat], s.out_xr.at[i])
        return out_chip(lat) + s.xbuf_out[lat].astype(F32)

    def out_cross():
        for zz in far:
            lat = col(zz)
            s.comb_out[lat] = out_total(lat, zz).astype(BF16)
            rcopy(s.comb_out.at[lat], s.rbuf_out.at[z], s.out_ss.at[0], s.out_rr.at[0], lat, h).start()
        s.acc_out[...] = out_total(me, z)

    def out_final():
        wait_here(s.rbuf_out.at[pl.ds(0, Z - 1)], s.out_rr.at[0])
        value = s.acc_out[...]
        for zz in peers:
            value = value + s.rbuf_out[zz].astype(F32)
        back_by = lax.rem(LANES - lax.rem(mine * own_width, LANES), LANES)
        out_cols[:, :LANES] = pltpu.roll(value[:rows], back_by, 1).astype(BF16)
        parts = []
        for g in range(rows // PACK):
            part = value[rows + (g // per) * PACK : rows + (g // per + 1) * PACK]
            move = (-(g % per) * rest) % LANES
            parts.append(pltpu.roll(part, move, 1) if move else part)
        out_cols[:, LANES:] = jnp.concatenate(parts, axis=0)[:, :rest].astype(BF16)

    def out_drain():
        wait_sent(s.sib_out, s.out_cs.at[0])
        wait_sent(s.xbuf_out.at[pl.ds(0, Z)], s.out_xs.at[0])
        wait_sent(s.xbuf_out.at[pl.ds(0, Z - 1)], s.out_ss.at[0])

    across = (((1,), (1,)), ((), ()))

    def mm_t(x, w):
        return lax.dot_general(x, w, across, preferred_element_type=F32)

    def mm(x, w):
        return lax.dot_general(x, w, (((1,), (0,)), ((), ())), preferred_element_type=F32)

    deep = TILE if units % TILE == 0 else units
    n_deep = units // deep

    def flip(src, dst):
        for t in range(units // LANES):
            at_rows = slice(t * LANES, (t + 1) * LANES)
            dst[:, at_rows] = src[at_rows, :].T

    loads[0].wait()
    stage(s.codes_x, s.gx)
    pl.semaphore_wait(barrier, len(greeted))
    cols_start(s.gx, 0)
    loads[1].wait()
    stage(s.codes_u, s.gu)
    loads[2].wait()
    flip(s.dic, s.dic_t)
    cols_column(s.gx, 0)
    cols_across(s.gx, 0)
    cols_start(s.gu, 1)
    cols_take(s.gx, 0)
    x_rows = right.at[pl.ds(rows, rows)]
    r_rows = right.at[pl.ds(0, rows)]

    def put_x(t, value):
        right[pl.ds(rows, rows), t * LANES : (t + 1) * LANES] = value.astype(BF16)

    cols_rows(s.gx, put_x)
    loads[3].wait()
    for t in range(n_deep):
        cols = pl.ds(t * deep, deep)
        pre = mm(x_rows[...], s.dic_t[:, cols]) + s.ebias[:, cols]
        s.pre[:, cols] = pre
        left[pl.ds(0, rows), cols] = jnp.maximum(pre, 0.0).astype(BF16)
    for t in range(n_wide):
        sum_tile(0, t, mm(left[pl.ds(0, rows), :], s.dic[:, t * wide : (t + 1) * wide]))
    sum_start(0)
    sum_middle(0)
    s.full_x[...] = x_rows[...].astype(F32).reshape(C, ROWS, width).astype(BF16)
    loads[7].wait()
    flip(s.gate, s.gate_t)
    loads[8].wait()
    flip(s.up, s.up_t)
    sum_cross(0)
    cols_column(s.gu, 1)

    def put_u(t, value):
        s.u_rows[:, t * LANES : (t + 1) * LANES] = value.astype(BF16)

    loads[4].wait()
    loads[5].wait()

    def norm(slot, k):
        rebuilt = sum_value(0, slot) + s.dbias[...]
        inverse = lax.rsqrt(jnp.sum(rebuilt * rebuilt, axis=1, keepdims=True) / width + 1e-06)
        s.rebuilt[slot] = rebuilt
        s.inverse[slot] = jnp.broadcast_to(inverse, (ROWS, LANES))
        s.full_n[h * K + k] = (rebuilt * inverse * s.gain[...]).astype(BF16)

    spread_start(s.full_n, 0, norm)
    cols_across(s.gu, 1)
    spread_column(s.full_n, 0)
    cols_take(s.gu, 1)
    cols_rows(s.gu, put_u)
    loads[6].wait()
    for t in range(n_deep):
        cols = pl.ds(t * deep, deep)
        s.hgrad[:, cols] = mm_t(s.u_rows[...], s.down[cols, :])
    for p in range(PARTS):
        spread_across(s.full_n, 0, p)
        spread_take(s.full_n, 0, p)
        rows_of(s.full_n, s.n_rows, p)
        if p < PARTS - 1:
            at_cols = slice(p * part_width, (p + 1) * part_width)
            for t in range(n_deep):
                cols = pl.ds(t * deep, deep)
                g = mm(s.n_rows[:, at_cols], s.gate_t[at_cols, cols])
                u = mm(s.n_rows[:, at_cols], s.up_t[at_cols, cols])
                s.g_sum[:, cols] = g + s.g_sum[:, cols] if p else g
                s.u_sum[:, cols] = u + s.u_sum[:, cols] if p else u
    last = slice((PARTS - 1) * part_width, width)
    for t in range(n_deep):
        cols = pl.ds(t * deep, deep)
        g = mm(s.n_rows[:, last], s.gate_t[last, cols])
        u = mm(s.n_rows[:, last], s.up_t[last, cols])
        if PARTS > 1:
            g = g + s.g_sum[:, cols]
            u = u + s.u_sum[:, cols]
        th = jnp.tanh(0.7978845608028654 * (g + 0.044715 * g * g * g))
        value = 0.5 * g * (1.0 + th)
        slope = 0.5 * (1.0 + th) + 0.5 * g * (1.0 - th * th) * 0.7978845608028654 * (
            1.0 + 3.0 * 0.044715 * g * g
        )
        hg = s.hgrad[:, cols]
        s.hid[:, cols] = (value * u).astype(BF16)
        s.ggrad[:, cols] = (hg * u * slope).astype(BF16)
        s.ugrad[:, cols] = (hg * value).astype(BF16)
    for t in range(n_wide):
        cols = slice(t * wide, (t + 1) * wide)
        sum_tile(1, t, mm(s.ggrad[...], s.gate[:, cols]) + mm(s.ugrad[...], s.up[:, cols]))
    sum_start(1)
    sum_middle(1)
    for t in range(n_wide):
        out_tile(t, mm(s.hid[...], s.down[:, t * wide : (t + 1) * wide]))
    sum_cross(1)
    out_pieces()
    out_middle()

    def back(slot, k):
        scaled = sum_value(1, slot) * s.gain[...]
        rebuilt = s.rebuilt[slot]
        inverse = s.inverse[slot][:, :1]
        inner = jnp.sum(scaled * rebuilt, axis=1, keepdims=True)
        target = s.full_x[h * K + k].astype(F32)
        s.full_r[h * K + k] = (
            inverse * scaled - inverse * inverse * inverse * rebuilt * (inner / width) + (rebuilt - target)
        ).astype(BF16)

    spread_start(s.full_r, 1, back)
    for a, arr in enumerate((s.gx, s.gu)):
        cols_drain(arr, a)
    spread_drain(s.full_n, 0)
    sum_drain(0)
    spread_column(s.full_r, 1)
    out_cross()
    for p in range(PARTS):
        spread_across(s.full_r, 1, p)
        spread_take(s.full_r, 1, p)
        rows_of(s.full_r, r_rows, p)
        if p < PARTS - 1:
            at_cols = slice(p * part_width, (p + 1) * part_width)
            for t in range(n_deep):
                cols = pl.ds(t * deep, deep)
                g = mm(r_rows[:, at_cols], s.dic_t[at_cols, cols])
                s.g_sum[:, cols] = g + s.g_sum[:, cols] if p else g
    for t in range(n_deep):
        cols = pl.ds(t * deep, deep)
        grad = mm(r_rows[:, last], s.dic_t[last, cols])
        if PARTS > 1:
            grad = grad + s.g_sum[:, cols]
        left[pl.ds(rows, rows), cols] = jnp.where(s.pre[:, cols] > 0.0, grad, 0.0).astype(BF16)

    out_final()
    spread_drain(s.full_r, 1)
    sum_drain(1)
    out_drain()


def run_group(L, H, *args):
    codes, dic = args[0], args[2]
    rows, own_width = codes.shape
    units, width = dic.shape
    C = rows // ROWS
    K = C // H
    Z = L // 2
    n_dev = L * H
    per = LANES // (own_width - LANES)
    high = rows + PACK * -(-(rows // PACK) // per)
    V, D, R = pltpu.VMEM, pltpu.SemaphoreType.DMA, ROWS
    scratch = dict(
        codes_x=V((rows, own_width), jnp.int32), codes_u=V((rows, own_width), jnp.int32),
        ebias=V((1, units), F32), dbias=V((width,), F32), gain=V((width,), F32),
        dic=V((units, width), BF16), gate=V((units, width), BF16),
        up=V((units, width), BF16), down=V((units, width), BF16),
        dic_t=V((width, units), BF16), gate_t=V((width, units), BF16), up_t=V((width, units), BF16),
        g_sum=V((rows, units), F32), u_sum=V((rows, units), F32),
        gx=V((n_dev, high, LANES), BF16), gu=V((n_dev, high, LANES), BF16),
        full_x=V((C, R, width), BF16), full_n=V((C, R, width), BF16), full_r=V((C, R, width), BF16),
        u_rows=V((rows, width), BF16), n_rows=V((rows, width), BF16),
        pre=V((rows, units), F32), hgrad=V((rows, units), F32), hid=V((rows, units), BF16),
        ggrad=V((rows, units), BF16), ugrad=V((rows, units), BF16),
        own=V((2, C, R, width), F32), xbuf=V((2, K, R, width), BF16),
        sib=V((2, K, R, width), F32), comb=V((2, K, R, width), BF16),
        rbuf=V((2, 2, Z, R, width), BF16), acc=V((2, 2, R, width), F32),
        rebuilt=V((2, R, width), F32), inverse=V((2, R, LANES), F32),
        wide_out=V((rows, width), F32), own_out=V((H, L, high, LANES), F32), sib_out=V((L, high, LANES), F32),
        comb_out=V((L, high, LANES), BF16), xbuf_out=V((L, high, LANES), BF16),
        rbuf_out=V((Z, high, LANES), BF16), acc_out=V((high, LANES), F32),
        load_sem=D((9,)),
        col_ss=D((2,)), col_rs=D((2, L)), col_fs=D((2,)), col_fr=D((2,)),
        ag_ss=D((2, 2)), ag_xs=D((2,)), ag_xr=D((2, Z + 1, PARTS)), ag_rr=D((2, Z + 1, PARTS)), ag_fs=D((2,)), ag_fr=D((2, PARTS)),
        rs_cs=D((2,)), rs_cr=D((2,)), rs_ss=D((2,)), rs_rr=D((2, 2)), rs_xs=D((2,)), rs_xr=D((2, Z + 1)),
        out_cs=D((1,)), out_cr=D((1,)), out_xs=D((1,)), out_xr=D((Z,)), out_ss=D((1,)), out_rr=D((1,)),
    )
    names = list(scratch)

    def body(*refs):
        group_kernel(L, H, refs[:9], refs[9:12], types.SimpleNamespace(**dict(zip(names, refs[12:]))))

    hbm = pl.BlockSpec(memory_space=pltpu.HBM)
    vm = pl.BlockSpec(memory_space=pltpu.VMEM)
    cols, left, right = pl.pallas_call(
        body,
        name="group_step",
        out_shape=(
            V((rows, own_width), BF16),
            V((2 * rows, units), BF16),
            V((2 * rows, width), BF16),
        ),
        in_specs=[hbm] * 9,
        out_specs=(vm, vm, vm),
        scratch_shapes=[scratch[n] for n in names],
        compiler_params=pltpu.CompilerParams(collective_id=0, has_side_effects=True, vmem_limit_bytes=60 * 2**20),
    )(*args)

    step = width // 6 if width % (6 * LANES) == 0 else LANES
    n_step = width // step

    def product(cols, left, right, block, grad, tiles, sem):
        copies = [pltpu.make_async_copy(cols, block, sem.at[n_step])]
        copies[0].start()
        for t in range(n_step):
            at = slice(t * step, (t + 1) * step)
            tiles[t] = lax.dot_general(
                left[...], right[:, at], (((0,), (0,)), ((), ())), preferred_element_type=F32
            ).astype(BF16)
            copies.append(pltpu.make_async_copy(tiles.at[t], grad.at[:, at], sem.at[t]))
            copies[-1].start()
        for cp in copies:
            cp.wait()

    return pl.pallas_call(
        product,
        name="dictionary_product",
        out_shape=(
            jax.ShapeDtypeStruct((rows, own_width), BF16),
            jax.ShapeDtypeStruct((units, width), BF16),
        ),
        in_specs=[vm, vm, vm],
        out_specs=(pl.BlockSpec(memory_space=pl.ANY), pl.BlockSpec(memory_space=pl.ANY)),
        scratch_shapes=[V((n_step, units, step), BF16), D((n_step + 1,))],
        compiler_params=pltpu.CompilerParams(vmem_limit_bytes=16 * 2**20),
    )(cols, left, right)


def fits(L, H, rows, own_width, width, units, units_mlp):
    rest = own_width - LANES
    if H != 2 or rows % (ROWS * H) or rows % PACK or width % LANES or units % LANES or units != units_mlp:
        return False
    if rest <= 0 or rest >= LANES or LANES % rest or own_width * L * H != width or width % (PARTS * LANES):
        return False
    return L == 8 and rows // ROWS // H == L + 1


CODE_STEP = 2.0 ** (-6)
NORM_EPSILON = 1e-06
GELU_ROOT = 0.7978845608028654
GELU_CUBIC = 0.044715
ACROSS = (((1,), (1,)), ((), ()))
DOWNWARD = (((0,), (0,)), ((), ()))


def gelu_parts(values):
    argument = GELU_ROOT * (values + GELU_CUBIC * values * values * values)
    tanh_value = jnp.tanh(argument)
    result = 0.5 * values * (1.0 + tanh_value)
    derivative = 0.5 * (1.0 + tanh_value) + 0.5 * values * (
        1.0 - tanh_value * tanh_value
    ) * GELU_ROOT * (1.0 + 3.0 * GELU_CUBIC * values * values)
    return (result, derivative)


def per_device(
    input_codes,
    cotangent_codes,
    dictionary,
    encoder_bias,
    decoder_bias,
    norm_gain,
    gate_weight,
    up_weight,
    down_weight,
):
    L, H = lax.axis_size("latent"), lax.axis_size("hidden")
    rows, width = input_codes.shape[0], dictionary.shape[1]
    if fits(L, H, rows, input_codes.shape[1], width, dictionary.shape[0], gate_weight.shape[0]):
        return run_group(
            L, H, input_codes, cotangent_codes, dictionary, encoder_bias[None, :], decoder_bias,
            norm_gain, gate_weight, up_weight, down_weight,
        )
    own_width = input_codes.shape[1]
    model_width = own_width * lax.axis_size(("latent", "hidden"))
    cotangent_local = (cotangent_codes.astype(jnp.float32) * CODE_STEP).astype(jnp.bfloat16)
    hidden_grad = None
    inputs_local = (input_codes.astype(jnp.float32) * CODE_STEP).astype(jnp.bfloat16)
    inputs = lax.all_gather(inputs_local, ("latent", "hidden"), axis=1, tiled=True)
    preact = (
        lax.dot_general(inputs, dictionary, ACROSS, preferred_element_type=jnp.float32)
        + encoder_bias
    )
    latents = jnp.maximum(preact, 0.0).astype(jnp.bfloat16)
    partial_value = jnp.dot(latents, dictionary, preferred_element_type=jnp.float32)
    rebuilt = lax.psum(partial_value, ("latent", "hidden")) + decoder_bias
    inverse = lax.rsqrt(
        jnp.sum(rebuilt * rebuilt, axis=1, keepdims=True) / model_width + NORM_EPSILON
    )
    normed = (rebuilt * inverse * norm_gain).astype(jnp.bfloat16)
    target = inputs.astype(jnp.float32)
    gate_proj = lax.dot_general(normed, gate_weight, ACROSS, preferred_element_type=jnp.float32)
    up_proj = lax.dot_general(normed, up_weight, ACROSS, preferred_element_type=jnp.float32)
    gelu_value, gelu_slope = gelu_parts(gate_proj)
    hidden = (gelu_value * up_proj).astype(jnp.bfloat16)
    output_terms = jnp.dot(hidden, down_weight, preferred_element_type=jnp.float32)
    block_output = lax.psum_scatter(
        output_terms, ("latent", "hidden"), scatter_dimension=1, tiled=True
    ).astype(jnp.bfloat16)
    hidden_grad = lax.dot_general(
        lax.all_gather(cotangent_local, ("latent", "hidden"), axis=1, tiled=True),
        down_weight,
        ACROSS,
        preferred_element_type=jnp.float32,
    )
    gate_grad = (hidden_grad * up_proj * gelu_slope).astype(jnp.bfloat16)
    up_grad = (hidden_grad * gelu_value).astype(jnp.bfloat16)
    partial_grad = jnp.dot(gate_grad, gate_weight, preferred_element_type=jnp.float32) + jnp.dot(
        up_grad, up_weight, preferred_element_type=jnp.float32
    )
    scaled = lax.psum(partial_grad, ("latent", "hidden")) * norm_gain
    inner_row = jnp.sum(scaled * rebuilt, axis=1, keepdims=True)
    inverse_cube = inverse * inverse * inverse
    rebuilt_grad = (
        inverse * scaled - inverse_cube * rebuilt * (inner_row / model_width) + (rebuilt - target)
    ).astype(jnp.bfloat16)
    latent_grad = lax.dot_general(
        rebuilt_grad, dictionary, ACROSS, preferred_element_type=jnp.float32
    )
    preact_grad = jnp.where(preact > 0.0, latent_grad, 0.0).astype(jnp.bfloat16)
    dictionary_grad = lax.dot_general(
        latents, rebuilt_grad, DOWNWARD, preferred_element_type=jnp.float32
    ) + lax.dot_general(preact_grad, inputs, DOWNWARD, preferred_element_type=jnp.float32)
    return (block_output, dictionary_grad.astype(jnp.bfloat16))


def solution(mesh):
    in_specs = (
        P("groups", ("latent", "hidden")),
        P("groups", ("latent", "hidden")),
        P(("latent", "hidden"), None),
        P(("latent", "hidden")),
        P(),
        P(),
        P(("latent", "hidden"), None),
        P(("latent", "hidden"), None),
        P(("latent", "hidden"), None),
    )
    out_specs = (P("groups", ("latent", "hidden")), P(("latent", "hidden"), "groups"))
    return jax.shard_map(
        per_device, mesh=mesh, in_specs=in_specs, out_specs=out_specs, check_vma=False
    )
```

```python
import types

import jax
import jax.numpy as jnp
from jax import lax
from jax.experimental import pallas as pl
from jax.experimental.pallas import tpu as pltpu
from jax.sharding import PartitionSpec as P

ROWS = 8
PACK = 16
PARTS = 1
LANES = 128
TILE = 256
MESH = pl.DeviceIdType.MESH
F32 = jnp.float32
BF16 = jnp.bfloat16


def group_kernel(L, H, refs_in, refs_out, s):
    (codes_x, codes_u, dic_hbm, ebias_in, dbias_in, gain_in, gate_hbm, up_hbm, down_hbm) = refs_in
    (out_cols, left, right) = refs_out
    me = lax.axis_index("latent")
    h = lax.axis_index("hidden")
    other = 1 - h
    rows, own_width = codes_x.shape
    width = dic_hbm.shape[1]
    units = dic_hbm.shape[0]
    C = rows // ROWS
    K = C // H
    extra = K - L
    n_dev = L * H
    mine = me * H + h
    high = s.gx.shape[1]
    rest = own_width - LANES
    per = LANES // rest

    def ext(hid):
        return (2 + 3 * hid) % L

    def at(lat, hid):
        return {"latent": lat, "hidden": hid}

    def rcopy(src, dst, ss, rs, lat, hid):
        return pltpu.make_async_remote_copy(
            src_ref=src, dst_ref=dst, send_sem=ss, recv_sem=rs,
            device_id=at(lat, hid), device_id_type=MESH,
        )

    def each(n, body):
        def step(i, carry):
            body(i)
            return carry

        lax.fori_loop(0, n, step, 0)

    def slots(body):
        body(0, me)
        if extra:
            @pl.when(me == ext(h))
            def _():
                body(1, L)

    X = 2
    Z = L // X
    z, x = me // X, lax.rem(me, X)
    across_me = z * X + 1 - x
    near_z, same_z, flip_z = z + 1 - 2 * lax.rem(z, 2), z + 2 - 4 * (z // 2), 3 - z
    peers = (near_z, same_z, flip_z)
    far = (same_z, flip_z, near_z)

    def col(zz):
        return zz * X + x

    def beside(zz):
        return zz * X + 1 - x

    barrier = pltpu.get_barrier_semaphore()
    greeted = [(me, other), (across_me, h)] + [(col(zz), h) for zz in far]
    for lat, hid in greeted:
        pl.semaphore_signal(barrier, inc=1, device_id=at(lat, hid), device_id_type=MESH)

    loads = []
    for i, (src, dst) in enumerate((
        (codes_x, s.codes_x), (codes_u, s.codes_u), (dic_hbm, s.dic), (ebias_in, s.ebias),
        (dbias_in, s.dbias), (gain_in, s.gain), (down_hbm, s.down), (gate_hbm, s.gate), (up_hbm, s.up),
    )):
        cp = pltpu.make_async_copy(src, dst, s.load_sem.at[i])
        cp.start()
        loads.append(cp)

    def stage(codes, arr):
        value = codes[...].astype(F32) * (2.0 ** (-6))
        shift = lax.rem(mine * own_width, LANES)
        arr[mine, pl.ds(0, rows)] = pltpu.roll(value[:, :LANES], shift, 1).astype(BF16)
        over = jnp.concatenate([value[:, LANES:], jnp.zeros((rows, LANES - rest), F32)], axis=1)
        for b in range(s.gx.shape[1] // PACK - rows // PACK):
            packed = None
            for g in range(b * per, min((b + 1) * per, rows // PACK)):
                part = over[g * PACK : (g + 1) * PACK]
                part = pltpu.roll(part, (g % per) * rest, 1) if g % per else part
                packed = part if packed is None else packed + part
            arr[mine, pl.ds(rows + b * PACK, PACK)] = packed.astype(BF16)

    ext_z = ext(h) // X
    ext_here = lax.rem(ext(h), X) == x
    ext_mine = me == ext(h)
    ext_passes = jnp.logical_and(ext_here, jnp.logical_not(ext_mine))

    def when_extra(cond, body):
        if extra:
            @pl.when(cond)
            def _():
                body(L, Z)

    def wait_here(buf, sem):
        rcopy(buf, buf, sem, sem, me, other).wait_recv()

    def wait_sent(buf, sem):
        rcopy(buf, buf, sem, sem, me, other).wait_send()

    def cols_send(arr, a, i, lat):
        rcopy(arr.at[i], arr.at[i], s.col_ss.at[a], s.col_rs.at[a, i // H], lat, h).start()

    def cols_give(arr, a, i):
        rcopy(arr.at[i], arr.at[i], s.col_fs.at[a], s.col_fr.at[a], me, other).start()

    def cols_got(arr, a, lat, relay=False):
        i = lat * H + h
        wait_here(arr.at[i], s.col_rs.at[a, lat])
        if relay:
            cols_send(arr, a, i, across_me)
        cols_give(arr, a, i)

    def cols_start(arr, a):
        for zz in far:
            cols_send(arr, a, mine, col(zz))
        cols_send(arr, a, mine, across_me)
        cols_give(arr, a, mine)

    def cols_column(arr, a):
        for zz in peers:
            cols_got(arr, a, col(zz), True)

    def cols_across(arr, a):
        cols_got(arr, a, across_me)
        for zz in peers:
            cols_got(arr, a, beside(zz))

    def cols_take(arr, a):
        wait_here(arr.at[pl.ds(0, L)], s.col_fr.at[a])

    def cols_drain(arr, a):
        wait_sent(arr.at[pl.ds(0, L - 1)], s.col_ss.at[a])
        wait_sent(arr.at[pl.ds(0, L)], s.col_fs.at[a])

    def cols_rows(arr, put):
        lane = lax.broadcasted_iota(jnp.int32, (rows, LANES), 1)

        def main(i):
            return arr[i, pl.ds(0, rows)].astype(F32)

        def over(i):
            block = arr[i, pl.ds(rows, s.gx.shape[1] - rows)].astype(F32)
            parts = []
            for g in range(rows // PACK):
                b = g // per
                move = (i * own_width - (g % per) * rest) % LANES
                part = block[b * PACK : (b + 1) * PACK]
                parts.append(pltpu.roll(part, move, 1) if move else part)
            return jnp.concatenate(parts, axis=0)

        for t in range(width // LANES):
            value = None
            for i in range(n_dev):
                first, offset = divmod(i * own_width, LANES)
                if first == t:
                    new = main(i)
                    value = new if value is None else jnp.where(lane >= offset, new, value)
                elif first == t - 1:
                    value = over(i)
                    if offset:
                        value = jnp.where(lane >= offset, value, main(i))
            put(t, value)

    part_width = width // PARTS

    def part(full, c, p):
        return full.at[c, :, pl.ds(p * part_width, part_width)]

    def hand_over(full, a, k, p):
        piece = part(full, h * K + k, p)
        rcopy(piece, piece, s.ag_fs.at[a], s.ag_fr.at[a, p], me, other).start()

    def step_across(full, a, k, i, p):
        piece = part(full, h * K + k, p)
        rcopy(piece, piece, s.ag_xs.at[a], s.ag_xr.at[a, i, p], across_me, h).start()

    def spread_start(full, a, ready=None):
        def one(slot, k):
            if ready is not None:
                ready(slot, k)
            c = h * K + k
            i = Z if slot else z
            for p in range(PARTS):
                piece = part(full, c, p)
                for zz in far:
                    rcopy(piece, piece, s.ag_ss.at[a, slot], s.ag_rr.at[a, i, p], col(zz), h).start()
                    if slot:
                        rcopy(piece, piece, s.ag_ss.at[a, slot], s.ag_xr.at[a, i, p], beside(zz), h).start()
                step_across(full, a, k, i, p)
                hand_over(full, a, k, p)

        slots(one)

    def relay_column(full, a, k, i, p):
        wait_here(part(full, h * K + k, p), s.ag_rr.at[a, i, p])
        step_across(full, a, k, i, p)
        hand_over(full, a, k, p)

    def relay_across(full, a, k, i, p):
        wait_here(part(full, h * K + k, p), s.ag_xr.at[a, i, p])
        hand_over(full, a, k, p)

    def spread_column(full, a):
        for p in range(PARTS):
            for zz in peers:
                relay_column(full, a, col(zz), zz, p)

            def passing(k, i):
                wait_here(part(full, h * K + k, p), s.ag_rr.at[a, i, p])
                hand_over(full, a, k, p)

            when_extra(ext_passes, passing)

    def spread_across(full, a, p):
        relay_across(full, a, across_me, z, p)
        for zz in peers:
            relay_across(full, a, beside(zz), zz, p)
        when_extra(jnp.logical_not(ext_here), lambda k, i: relay_across(full, a, k, i, p))

    def spread_take(full, a, p):
        wait_here(full.at[pl.ds(other * K, K), :, pl.ds(p * part_width, part_width)], s.ag_fr.at[a, p])

    def either(cond, body, no, yes):
        @pl.when(cond)
        def _():
            body(yes)

        @pl.when(jnp.logical_not(cond))
        def _():
            body(no)

    def spread_drain(full, a):
        slots(lambda slot, k: wait_sent(full.at[pl.ds(0, (slot + 1) * (Z - 1))], s.ag_ss.at[a, slot]))
        either(ext_mine, lambda n: wait_sent(full.at[pl.ds(0, n)], s.ag_xs.at[a]), Z, Z + 1)
        wait_sent(full.at[pl.ds(0, K)], s.ag_fs.at[a])

    def rows_of(full, dst, p):
        at_cols = slice(p * part_width, (p + 1) * part_width)
        dst[:, at_cols] = full[:, :, at_cols].astype(F32).reshape(rows, part_width).astype(BF16)

    def sum_tile(a, t, value):
        cols = pl.ds(t * wide, wide)
        s.own[a, :, :, cols] = value.reshape(C, ROWS, wide)
        rcopy(
            s.own.at[a, pl.ds(other * K, K), :, cols], s.sib.at[a, :, :, cols],
            s.rs_cs.at[a], s.rs_cr.at[a], me, other,
        ).start()

    wide = 3 * TILE if width % (3 * TILE) == 0 else LANES
    n_wide = width // wide

    def sum_start(a):
        wait_here(s.sib.at[a], s.rs_cr.at[a])

    def sum_chip(a, k):
        return s.own[a, h * K + k] + s.sib[a, k]

    def sum_middle(a):
        def leave(k, i):
            s.comb[a, k] = sum_chip(a, k).astype(BF16)
            rcopy(s.comb.at[a, k], s.xbuf.at[a, k], s.rs_xs.at[a], s.rs_xr.at[a, i], across_me, h).start()

        for zz in far:
            leave(beside(zz), zz)
        when_extra(jnp.logical_not(ext_here), leave)
        leave(across_me, z)

    def sum_cross(a):
        def total(k, i):
            value = sum_chip(a, k)
            wait_here(s.xbuf.at[a, k], s.rs_xr.at[a, i])
            return value + s.xbuf[a, k].astype(F32)

        def leave(slot, k, i, owner):
            s.comb[a, k] = total(k, i).astype(BF16)
            rcopy(s.comb.at[a, k], s.rbuf.at[a, slot, z], s.rs_ss.at[a], s.rs_rr.at[a, slot], owner, h).start()

        for zz in far:
            leave(0, col(zz), zz, col(zz))
        when_extra(ext_passes, lambda k, i: leave(1, k, i, ext(h)))
        s.acc[a, 0] = total(me, z)

        def keep(k, i):
            s.acc[a, 1] = total(k, i)

        when_extra(ext_mine, keep)

    def sum_value(a, slot):
        value = s.acc[a, slot]
        wait_here(s.rbuf.at[a, slot, pl.ds(0, Z - 1)], s.rs_rr.at[a, slot])
        for zz in peers:
            value = value + s.rbuf[a, slot, zz].astype(F32)
        return value

    def sum_drain(a):
        wait_sent(s.sib.at[a], s.rs_cs.at[a])
        either(jnp.logical_not(ext_here), lambda n: wait_sent(s.xbuf.at[a, pl.ds(0, n)], s.rs_xs.at[a]), Z, Z + 1)
        either(ext_passes, lambda n: wait_sent(s.xbuf.at[a, pl.ds(0, n)], s.rs_ss.at[a]), Z - 1, Z)

    def out_tile(t, value):
        s.wide_out[:, t * wide : (t + 1) * wide] = value

    def out_pieces():
        lane = lax.broadcasted_iota(jnp.int32, (rows, LANES), 1)
        group = lax.broadcasted_iota(jnp.int32, (PACK, LANES), 1) // rest
        for i in range(n_dev):
            first, offset = divmod(i * own_width, LANES)
            here = s.wide_out[:, first * LANES : (first + 1) * LANES]
            there = s.wide_out[:, (first + 1) * LANES : (first + 2) * LANES]
            piece = s.own_out.at[i % H, i // H]
            piece[pl.ds(0, rows)] = jnp.where(lane >= offset, here, there) if offset else here
            for b in range(high // PACK - rows // PACK):
                packed = jnp.zeros((PACK, LANES), F32)
                for g in range(b * per, min((b + 1) * per, rows // PACK)):
                    part = there[g * PACK : (g + 1) * PACK]
                    move = ((g % per) * rest - offset) % LANES
                    part = pltpu.roll(part, move, 1) if move else part
                    packed = jnp.where(group == g % per, part, packed)
                piece[pl.ds(rows + b * PACK, PACK)] = packed
        rcopy(s.own_out.at[other], s.sib_out, s.out_cs.at[0], s.out_cr.at[0], me, other).start()

    def out_chip(lat):
        return s.own_out[h, lat] + s.sib_out[lat]

    def out_middle():
        wait_here(s.sib_out, s.out_cr.at[0])
        for lat, i in [(beside(zz), zz) for zz in far] + [(across_me, z)]:
            s.comb_out[lat] = out_chip(lat).astype(BF16)
            rcopy(s.comb_out.at[lat], s.xbuf_out.at[lat], s.out_xs.at[0], s.out_xr.at[i], across_me, h).start()

    def out_total(lat, i):
        wait_here(s.xbuf_out.at[lat], s.out_xr.at[i])
        return out_chip(lat) + s.xbuf_out[lat].astype(F32)

    def out_cross():
        for zz in far:
            lat = col(zz)
            s.comb_out[lat] = out_total(lat, zz).astype(BF16)
            rcopy(s.comb_out.at[lat], s.rbuf_out.at[z], s.out_ss.at[0], s.out_rr.at[0], lat, h).start()
        s.acc_out[...] = out_total(me, z)

    def out_final():
        wait_here(s.rbuf_out.at[pl.ds(0, Z - 1)], s.out_rr.at[0])
        value = s.acc_out[...]
        for zz in peers:
            value = value + s.rbuf_out[zz].astype(F32)
        back_by = lax.rem(LANES - lax.rem(mine * own_width, LANES), LANES)
        out_cols[:, :LANES] = pltpu.roll(value[:rows], back_by, 1).astype(BF16)
        parts = []
        for g in range(rows // PACK):
            part = value[rows + (g // per) * PACK : rows + (g // per + 1) * PACK]
            move = (-(g % per) * rest) % LANES
            parts.append(pltpu.roll(part, move, 1) if move else part)
        out_cols[:, LANES:] = jnp.concatenate(parts, axis=0)[:, :rest].astype(BF16)

    def out_drain():
        wait_sent(s.sib_out, s.out_cs.at[0])
        wait_sent(s.xbuf_out.at[pl.ds(0, Z)], s.out_xs.at[0])
        wait_sent(s.xbuf_out.at[pl.ds(0, Z - 1)], s.out_ss.at[0])

    across = (((1,), (1,)), ((), ()))

    def mm_t(x, w):
        return lax.dot_general(x, w, across, preferred_element_type=F32)

    def mm(x, w):
        return lax.dot_general(x, w, (((1,), (0,)), ((), ())), preferred_element_type=F32)

    deep = units
    n_deep = units // deep

    def flip(src, dst):
        for t in range(units // LANES):
            at_rows = slice(t * LANES, (t + 1) * LANES)
            dst[:, at_rows] = src[at_rows, :].T

    loads[0].wait()
    stage(s.codes_x, s.gx)
    pl.semaphore_wait(barrier, len(greeted))
    cols_start(s.gx, 0)
    loads[1].wait()
    stage(s.codes_u, s.gu)
    loads[2].wait()
    flip(s.dic, s.dic_t)
    cols_column(s.gx, 0)
    cols_across(s.gx, 0)
    cols_start(s.gu, 1)
    cols_take(s.gx, 0)
    x_rows = right.at[pl.ds(rows, rows)]
    r_rows = right.at[pl.ds(0, rows)]

    def put_x(t, value):
        right[pl.ds(rows, rows), t * LANES : (t + 1) * LANES] = value.astype(BF16)

    cols_rows(s.gx, put_x)
    loads[3].wait()
    for t in range(n_deep):
        cols = pl.ds(t * deep, deep)
        pre = mm(x_rows[...], s.dic_t[:, cols]) + s.ebias[:, cols]
        s.pre[:, cols] = pre
        left[pl.ds(0, rows), cols] = jnp.maximum(pre, 0.0).astype(BF16)
    for t in range(n_wide):
        sum_tile(0, t, mm(left[pl.ds(0, rows), :], s.dic[:, t * wide : (t + 1) * wide]))
    sum_start(0)
    sum_middle(0)
    s.full_x[...] = x_rows[...].astype(F32).reshape(C, ROWS, width).astype(BF16)
    loads[7].wait()
    flip(s.gate, s.gate_t)
    loads[8].wait()
    flip(s.up, s.up_t)
    sum_cross(0)
    cols_column(s.gu, 1)

    def put_u(t, value):
        s.u_rows[:, t * LANES : (t + 1) * LANES] = value.astype(BF16)

    loads[4].wait()
    loads[5].wait()

    def norm(slot, k):
        rebuilt = sum_value(0, slot) + s.dbias[...]
        inverse = lax.rsqrt(jnp.sum(rebuilt * rebuilt, axis=1, keepdims=True) / width + 1e-06)
        s.rebuilt[slot] = rebuilt
        s.inverse[slot] = jnp.broadcast_to(inverse, (ROWS, LANES))
        s.full_n[h * K + k] = (rebuilt * inverse * s.gain[...]).astype(BF16)

    spread_start(s.full_n, 0, norm)
    cols_across(s.gu, 1)
    spread_column(s.full_n, 0)
    cols_take(s.gu, 1)
    cols_rows(s.gu, put_u)
    loads[6].wait()
    for t in range(n_deep):
        cols = pl.ds(t * deep, deep)
        s.hgrad[:, cols] = mm_t(s.u_rows[...], s.down[cols, :])
    for p in range(PARTS):
        spread_across(s.full_n, 0, p)
        spread_take(s.full_n, 0, p)
        rows_of(s.full_n, s.n_rows, p)
        if p < PARTS - 1:
            at_cols = slice(p * part_width, (p + 1) * part_width)
            for t in range(n_deep):
                cols = pl.ds(t * deep, deep)
                g = mm(s.n_rows[:, at_cols], s.gate_t[at_cols, cols])
                u = mm(s.n_rows[:, at_cols], s.up_t[at_cols, cols])
                s.g_sum[:, cols] = g + s.g_sum[:, cols] if p else g
                s.u_sum[:, cols] = u + s.u_sum[:, cols] if p else u
    last = slice((PARTS - 1) * part_width, width)
    for t in range(n_deep):
        cols = pl.ds(t * deep, deep)
        g = mm(s.n_rows[:, last], s.gate_t[last, cols])
        u = mm(s.n_rows[:, last], s.up_t[last, cols])
        if PARTS > 1:
            g = g + s.g_sum[:, cols]
            u = u + s.u_sum[:, cols]
        th = jnp.tanh(0.7978845608028654 * (g + 0.044715 * g * g * g))
        value = 0.5 * g * (1.0 + th)
        slope = 0.5 * (1.0 + th) + 0.5 * g * (1.0 - th * th) * 0.7978845608028654 * (
            1.0 + 3.0 * 0.044715 * g * g
        )
        hg = s.hgrad[:, cols]
        s.hid[:, cols] = (value * u).astype(BF16)
        s.ggrad[:, cols] = (hg * u * slope).astype(BF16)
        s.ugrad[:, cols] = (hg * value).astype(BF16)
    for t in range(n_wide):
        cols = slice(t * wide, (t + 1) * wide)
        sum_tile(1, t, mm(s.ggrad[...], s.gate[:, cols]) + mm(s.ugrad[...], s.up[:, cols]))
    sum_start(1)
    sum_middle(1)
    for t in range(n_wide):
        out_tile(t, mm(s.hid[...], s.down[:, t * wide : (t + 1) * wide]))
    sum_cross(1)
    out_pieces()
    out_middle()

    def back(slot, k):
        scaled = sum_value(1, slot) * s.gain[...]
        rebuilt = s.rebuilt[slot]
        inverse = s.inverse[slot][:, :1]
        inner = jnp.sum(scaled * rebuilt, axis=1, keepdims=True)
        target = s.full_x[h * K + k].astype(F32)
        s.full_r[h * K + k] = (
            inverse * scaled - inverse * inverse * inverse * rebuilt * (inner / width) + (rebuilt - target)
        ).astype(BF16)

    spread_start(s.full_r, 1, back)
    for a, arr in enumerate((s.gx, s.gu)):
        cols_drain(arr, a)
    spread_drain(s.full_n, 0)
    sum_drain(0)
    spread_column(s.full_r, 1)
    out_cross()
    sum_drain(1)
    for p in range(PARTS):
        spread_across(s.full_r, 1, p)
        spread_take(s.full_r, 1, p)
        rows_of(s.full_r, r_rows, p)
        if p < PARTS - 1:
            at_cols = slice(p * part_width, (p + 1) * part_width)
            for t in range(n_deep):
                cols = pl.ds(t * deep, deep)
                g = mm(r_rows[:, at_cols], s.dic_t[at_cols, cols])
                s.g_sum[:, cols] = g + s.g_sum[:, cols] if p else g
    for t in range(n_deep):
        cols = pl.ds(t * deep, deep)
        grad = mm(r_rows[:, last], s.dic_t[last, cols])
        if PARTS > 1:
            grad = grad + s.g_sum[:, cols]
        left[pl.ds(rows, rows), cols] = jnp.where(s.pre[:, cols] > 0.0, grad, 0.0).astype(BF16)

    out_final()
    spread_drain(s.full_r, 1)
    out_drain()


def run_group(L, H, *args):
    codes, dic = args[0], args[2]
    rows, own_width = codes.shape
    units, width = dic.shape
    C = rows // ROWS
    K = C // H
    Z = L // 2
    n_dev = L * H
    per = LANES // (own_width - LANES)
    high = rows + PACK * -(-(rows // PACK) // per)
    V, D, R = pltpu.VMEM, pltpu.SemaphoreType.DMA, ROWS
    scratch = dict(
        codes_x=V((rows, own_width), jnp.int32), codes_u=V((rows, own_width), jnp.int32),
        ebias=V((1, units), F32), dbias=V((width,), F32), gain=V((width,), F32),
        dic=V((units, width), BF16), gate=V((units, width), BF16),
        up=V((units, width), BF16), down=V((units, width), BF16),
        dic_t=V((width, units), BF16), gate_t=V((width, units), BF16), up_t=V((width, units), BF16),
        g_sum=V((rows, units), F32), u_sum=V((rows, units), F32),
        gx=V((n_dev, high, LANES), BF16), gu=V((n_dev, high, LANES), BF16),
        full_x=V((C, R, width), BF16), full_n=V((C, R, width), BF16), full_r=V((C, R, width), BF16),
        u_rows=V((rows, width), BF16), n_rows=V((rows, width), BF16),
        pre=V((rows, units), F32), hgrad=V((rows, units), F32), hid=V((rows, units), BF16),
        ggrad=V((rows, units), BF16), ugrad=V((rows, units), BF16),
        own=V((2, C, R, width), F32), xbuf=V((2, K, R, width), BF16),
        sib=V((2, K, R, width), F32), comb=V((2, K, R, width), BF16),
        rbuf=V((2, 2, Z, R, width), BF16), acc=V((2, 2, R, width), F32),
        rebuilt=V((2, R, width), F32), inverse=V((2, R, LANES), F32),
        wide_out=V((rows, width), F32), own_out=V((H, L, high, LANES), F32), sib_out=V((L, high, LANES), F32),
        comb_out=V((L, high, LANES), BF16), xbuf_out=V((L, high, LANES), BF16),
        rbuf_out=V((Z, high, LANES), BF16), acc_out=V((high, LANES), F32),
        load_sem=D((9,)),
        col_ss=D((2,)), col_rs=D((2, L)), col_fs=D((2,)), col_fr=D((2,)),
        ag_ss=D((2, 2)), ag_xs=D((2,)), ag_xr=D((2, Z + 1, PARTS)), ag_rr=D((2, Z + 1, PARTS)), ag_fs=D((2,)), ag_fr=D((2, PARTS)),
        rs_cs=D((2,)), rs_cr=D((2,)), rs_ss=D((2,)), rs_rr=D((2, 2)), rs_xs=D((2,)), rs_xr=D((2, Z + 1)),
        out_cs=D((1,)), out_cr=D((1,)), out_xs=D((1,)), out_xr=D((Z,)), out_ss=D((1,)), out_rr=D((1,)),
    )
    names = list(scratch)

    def body(*refs):
        group_kernel(L, H, refs[:9], refs[9:12], types.SimpleNamespace(**dict(zip(names, refs[12:]))))

    hbm = pl.BlockSpec(memory_space=pltpu.HBM)
    vm = pl.BlockSpec(memory_space=pltpu.VMEM)
    cols, left, right = pl.pallas_call(
        body,
        name="group_step",
        out_shape=(
            V((rows, own_width), BF16),
            V((2 * rows, units), BF16),
            V((2 * rows, width), BF16),
        ),
        in_specs=[hbm] * 9,
        out_specs=(vm, vm, vm),
        scratch_shapes=[scratch[n] for n in names],
        compiler_params=pltpu.CompilerParams(collective_id=0, has_side_effects=True, vmem_limit_bytes=60 * 2**20),
    )(*args)

    step = width // 6 if width % (6 * LANES) == 0 else LANES
    n_step = width // step

    def product(cols, left, right, block, grad, tiles, sem):
        copies = [pltpu.make_async_copy(cols, block, sem.at[n_step])]
        copies[0].start()
        for t in range(n_step):
            at = slice(t * step, (t + 1) * step)
            tiles[t] = lax.dot_general(
                left[...], right[:, at], (((0,), (0,)), ((), ())), preferred_element_type=F32
            ).astype(BF16)
            copies.append(pltpu.make_async_copy(tiles.at[t], grad.at[:, at], sem.at[t]))
            copies[-1].start()
        for cp in copies:
            cp.wait()

    return pl.pallas_call(
        product,
        name="dictionary_product",
        out_shape=(
            jax.ShapeDtypeStruct((rows, own_width), BF16),
            jax.ShapeDtypeStruct((units, width), BF16),
        ),
        in_specs=[vm, vm, vm],
        out_specs=(pl.BlockSpec(memory_space=pl.ANY), pl.BlockSpec(memory_space=pl.ANY)),
        scratch_shapes=[V((n_step, units, step), BF16), D((n_step + 1,))],
        compiler_params=pltpu.CompilerParams(vmem_limit_bytes=16 * 2**20),
    )(cols, left, right)


def fits(L, H, rows, own_width, width, units, units_mlp):
    rest = own_width - LANES
    if H != 2 or rows % (ROWS * H) or rows % PACK or width % LANES or units % LANES or units != units_mlp:
        return False
    if rest <= 0 or rest >= LANES or LANES % rest or own_width * L * H != width or width % (PARTS * LANES):
        return False
    return L == 8 and rows // ROWS // H == L + 1


CODE_STEP = 2.0 ** (-6)
NORM_EPSILON = 1e-06
GELU_ROOT = 0.7978845608028654
GELU_CUBIC = 0.044715
ACROSS = (((1,), (1,)), ((), ()))
DOWNWARD = (((0,), (0,)), ((), ()))


def gelu_parts(values):
    argument = GELU_ROOT * (values + GELU_CUBIC * values * values * values)
    tanh_value = jnp.tanh(argument)
    result = 0.5 * values * (1.0 + tanh_value)
    derivative = 0.5 * (1.0 + tanh_value) + 0.5 * values * (
        1.0 - tanh_value * tanh_value
    ) * GELU_ROOT * (1.0 + 3.0 * GELU_CUBIC * values * values)
    return (result, derivative)


def per_device(
    input_codes,
    cotangent_codes,
    dictionary,
    encoder_bias,
    decoder_bias,
    norm_gain,
    gate_weight,
    up_weight,
    down_weight,
):
    L, H = lax.axis_size("latent"), lax.axis_size("hidden")
    rows, width = input_codes.shape[0], dictionary.shape[1]
    if fits(L, H, rows, input_codes.shape[1], width, dictionary.shape[0], gate_weight.shape[0]):
        return run_group(
            L, H, input_codes, cotangent_codes, dictionary, encoder_bias[None, :], decoder_bias,
            norm_gain, gate_weight, up_weight, down_weight,
        )
    own_width = input_codes.shape[1]
    model_width = own_width * lax.axis_size(("latent", "hidden"))
    cotangent_local = (cotangent_codes.astype(jnp.float32) * CODE_STEP).astype(jnp.bfloat16)
    hidden_grad = None
    inputs_local = (input_codes.astype(jnp.float32) * CODE_STEP).astype(jnp.bfloat16)
    inputs = lax.all_gather(inputs_local, ("latent", "hidden"), axis=1, tiled=True)
    preact = (
        lax.dot_general(inputs, dictionary, ACROSS, preferred_element_type=jnp.float32)
        + encoder_bias
    )
    latents = jnp.maximum(preact, 0.0).astype(jnp.bfloat16)
    partial_value = jnp.dot(latents, dictionary, preferred_element_type=jnp.float32)
    rebuilt = lax.psum(partial_value, ("latent", "hidden")) + decoder_bias
    inverse = lax.rsqrt(
        jnp.sum(rebuilt * rebuilt, axis=1, keepdims=True) / model_width + NORM_EPSILON
    )
    normed = (rebuilt * inverse * norm_gain).astype(jnp.bfloat16)
    target = inputs.astype(jnp.float32)
    gate_proj = lax.dot_general(normed, gate_weight, ACROSS, preferred_element_type=jnp.float32)
    up_proj = lax.dot_general(normed, up_weight, ACROSS, preferred_element_type=jnp.float32)
    gelu_value, gelu_slope = gelu_parts(gate_proj)
    hidden = (gelu_value * up_proj).astype(jnp.bfloat16)
    output_terms = jnp.dot(hidden, down_weight, preferred_element_type=jnp.float32)
    block_output = lax.psum_scatter(
        output_terms, ("latent", "hidden"), scatter_dimension=1, tiled=True
    ).astype(jnp.bfloat16)
    hidden_grad = lax.dot_general(
        lax.all_gather(cotangent_local, ("latent", "hidden"), axis=1, tiled=True),
        down_weight,
        ACROSS,
        preferred_element_type=jnp.float32,
    )
    gate_grad = (hidden_grad * up_proj * gelu_slope).astype(jnp.bfloat16)
    up_grad = (hidden_grad * gelu_value).astype(jnp.bfloat16)
    partial_grad = jnp.dot(gate_grad, gate_weight, preferred_element_type=jnp.float32) + jnp.dot(
        up_grad, up_weight, preferred_element_type=jnp.float32
    )
    scaled = lax.psum(partial_grad, ("latent", "hidden")) * norm_gain
    inner_row = jnp.sum(scaled * rebuilt, axis=1, keepdims=True)
    inverse_cube = inverse * inverse * inverse
    rebuilt_grad = (
        inverse * scaled - inverse_cube * rebuilt * (inner_row / model_width) + (rebuilt - target)
    ).astype(jnp.bfloat16)
    latent_grad = lax.dot_general(
        rebuilt_grad, dictionary, ACROSS, preferred_element_type=jnp.float32
    )
    preact_grad = jnp.where(preact > 0.0, latent_grad, 0.0).astype(jnp.bfloat16)
    dictionary_grad = lax.dot_general(
        latents, rebuilt_grad, DOWNWARD, preferred_element_type=jnp.float32
    ) + lax.dot_general(preact_grad, inputs, DOWNWARD, preferred_element_type=jnp.float32)
    return (block_output, dictionary_grad.astype(jnp.bfloat16))


def solution(mesh):
    in_specs = (
        P("groups", ("latent", "hidden")),
        P("groups", ("latent", "hidden")),
        P(("latent", "hidden"), None),
        P(("latent", "hidden")),
        P(),
        P(),
        P(("latent", "hidden"), None),
        P(("latent", "hidden"), None),
        P(("latent", "hidden"), None),
    )
    out_specs = (P("groups", ("latent", "hidden")), P(("latent", "hidden"), "groups"))
    return jax.shard_map(
        per_device, mesh=mesh, in_specs=in_specs, out_specs=out_specs, check_vma=False
    )
```
